32 devices in a mesh: ops: 8 (over z, x), sec: 4 (over y, core).
Axes of the slice: x: 2, y: 2, z: 4, core: 2. Of those that a mesh axis runs over, the one named last changes fastest.
Arguments:
- sector_states: int32 [4], P('sec'), may hold values from 85 to 256, as said below
- psi_guess: bfloat16 [4, 256, 256], P('sec'), may hold values from -6 to 6
- precond_diag: bfloat16 [4, 256, 256], P('sec'), may hold values from -12 to 12
- left_ops: float32 [16, 4, 256, 256], P('ops', 'sec'), may hold values from -0.375 to 0.375
- right_ops: float32 [16, 4, 256, 256], P('ops', 'sec'), may hold values from -0.375 to 0.375
- couple: int32 [16, 4], P('ops', 'sec'), may hold values from -1 to 3, as said below
- new_sector: int32 [4], P('sec'), may hold values from 0 to 3, as said below
Outputs:
- wavefunction: float32 [4, 256, 256], P('sec')
- rotated_ops: float32 [16, 4, 256, 256], P('ops', 'sec')
The draws below stay inside these ranges and needn't reach their ends.
Inputs may be any that keep to these rules, and one draw needn't show every extreme that they name: `sector_states`: at least one sector has 256 states. couple[p, s] is s - 1, s or s + 1, or -1 where that lies outside the sectors. `new_sector`: each aligned pair of sectors 2k, 2k + 1 either keeps its labels or swaps them; the pair with 2k = 2 always swaps.
All inputs are finite; a program needn't handle non-finite values.
Results may differ from the reference program's by a relative error of at most 0.0003.
Values sent between devices are 32-bit elements; how exact they have to be, the bound alone decides.
No kernel may reach another device: no remote copies, remote signals or barrier semaphores. Data moves between devices by JAX's collectives and lax.ppermute only.
A program may use at most 64 MiB of HBM per device.

```python
import jax
import jax.numpy as jnp
from jax import lax

MAXS = 256
UPDATES = 2
PAIRS = 16
NSEC = 4


def draw_sector_states(key, part):
    states = jax.random.randint(key, (NSEC,), MAXS // 3, MAXS + 1)
    where = jax.random.randint(jax.random.fold_in(key, 7), (), 0, NSEC)
    return states.at[where].set(MAXS).astype(jnp.int32)


def draw_couple(key, part):
    offset = jax.random.randint(key, (PAIRS, NSEC), -1, 2)
    sector = jnp.arange(NSEC, dtype=jnp.int32)[None, :]
    source = sector + offset
    outside = (source < 0) | (source >= NSEC)
    return jnp.where(outside, -1, source).astype(jnp.int32)


def draw_new_sector(key, part):
    flips = jax.random.randint(key, (NSEC // 2,), 0, 2)
    flips = flips.at[NSEC // 4].set(1)
    base = 2 * jnp.arange(NSEC // 2, dtype=jnp.int32)
    labels = jnp.stack([base + flips, base + 1 - flips], axis=1)
    return labels.reshape(NSEC).astype(jnp.int32)


def levels(stream_key, extent, cuts, low, largest):
    def one(position, parts):
        steps = jax.random.uniform(jax.random.fold_in(jax.random.fold_in(stream_key, 6), position), (parts,), jnp.float32, low / len(cuts), largest / len(cuts))
        return jnp.repeat(jnp.exp(steps), extent[position] // parts).reshape((-1,) + (1,) * (len(extent) - position - 1))

    loudness = one(*cuts[0])
    for cut in cuts[1:]:
        loudness = loudness * one(*cut)
    return loudness


def centred(own_key, dims, width, limit, pieces=(), kind=jnp.bfloat16):
    drawn = jax.random.normal(own_key, dims, jnp.float32) * width
    if len(pieces) > 0:
        drawn = levels(own_key, dims, pieces, -0.22, 0.18) * drawn
    return jnp.clip(drawn, min=-limit, max=limit).astype(kind)


def setup_inputs(seed: int = 0) -> dict:
    seeds = jax.random.split(jax.random.key(seed), 8)
    return {
        "sector_states": draw_sector_states(jax.random.fold_in(seeds[7], 71), 0),
        "psi_guess": centred(seeds[1], (NSEC, MAXS, MAXS), 1.0, 6.0, ((0, 4),)),
        "precond_diag": centred(seeds[2], (NSEC, MAXS, MAXS), 2.0, 12.0, ((0, 4),)),
        "left_ops": centred(seeds[3], (PAIRS, NSEC, MAXS, MAXS), MAXS ** -0.5, 0.375, ((0, 8), (1, 4)), jnp.float32),
        "right_ops": centred(seeds[4], (PAIRS, NSEC, MAXS, MAXS), MAXS ** -0.5, 0.375, ((0, 8), (1, 4)), jnp.float32),
        "couple": draw_couple(jax.random.fold_in(seeds[7], 71), 0),
        "new_sector": draw_new_sector(jax.random.fold_in(seeds[7], 71), 0),
    }


HIGH = lax.Precision.HIGHEST

def apply_ham(vec, left_ops, right_ops, couple, live):

    def step(total, item):
        left, right, source = item
        valid = (source >= 0).astype(jnp.float32)
        picked = vec[jnp.clip(source, 0, NSEC - 1)] * valid[:, None, None]
        mixed = jnp.einsum('sij,sjk->sik', left, picked, precision=HIGH)
        return (total + jnp.einsum('sik,slk->sil', mixed, right, precision=HIGH), None)
    total, _ = lax.scan(step, jnp.zeros(vec.shape, jnp.float32), (left_ops, right_ops, couple))
    return total * live

def reference(sector_states, psi_guess, precond_diag, left_ops, right_ops, couple, new_sector):
    index = jnp.arange(MAXS, dtype=jnp.int32)
    sizes = sector_states[:, None, None]
    live = ((index[None, :, None] < sizes) & (index[None, None, :] < sizes)).astype(jnp.float32)
    diag = precond_diag.astype(jnp.float32)
    vecx = psi_guess.astype(jnp.float32) * live
    vecx = vecx * lax.rsqrt(jnp.sum(vecx * vecx) + 1e-06)
    hvec = apply_ham(vecx, left_ops, right_ops, couple, live)
    theta = jnp.sum(vecx * hvec)
    for update in range(UPDATES):
        corr = live * (hvec - theta * vecx) / (jnp.abs(diag - theta) + 1.0)
        corr = corr - jnp.sum(vecx * corr) * vecx
        corr = corr * lax.rsqrt(jnp.sum(corr * corr) + 1e-06)
        hcorr = apply_ham(corr, left_ops, right_ops, couple, live)
        first = theta
        middle = 0.5 * (jnp.sum(vecx * hcorr) + jnp.sum(corr * hvec))
        last = jnp.sum(corr * hcorr)
        angle = 0.5 * jnp.arctan2(-2.0 * middle, last - first)
        vecx = jnp.cos(angle) * vecx + jnp.sin(angle) * corr
        hvec = jnp.cos(angle) * hvec + jnp.sin(angle) * hcorr
        theta = 0.5 * (first + last) - 0.5 * jnp.sqrt((last - first) ** 2 + 4.0 * middle * middle)
    wavefunction = vecx * jnp.sqrt(jnp.float32(NSEC * MAXS * MAXS))
    valid = (couple >= 0).astype(jnp.float32)
    picked = wavefunction[jnp.clip(couple, 0, NSEC - 1)] * valid[:, :, None, None]
    inner = jnp.einsum('psjk,pskl->psjl', left_ops, picked, precision=HIGH)
    turned = jnp.einsum('sji,psjl->psil', wavefunction, inner, precision=HIGH) / jnp.sqrt(jnp.float32(MAXS))
    rotated_ops = turned[:, new_sector]
    return (wavefunction, rotated_ops)
```

```python
import functools

import jax
import jax.numpy as jnp
from jax import lax
from jax.experimental import pallas as pl
from jax.experimental.pallas import tpu as pltpu
from jax.sharding import PartitionSpec as P

LANES = 128
F32 = jnp.float32
BF16 = jnp.bfloat16
VMEM = pl.BlockSpec(memory_space=pltpu.VMEM)
SMEM = pl.BlockSpec(memory_space=pltpu.SMEM)


def call(body, outs, in_specs, scratch, flops, *args):
    size = sum(a.size * a.dtype.itemsize for a in args)
    size += sum(o.size * o.dtype.itemsize for o in outs)
    return pl.pallas_call(
        body,
        out_shape=tuple(outs),
        in_specs=in_specs,
        out_specs=tuple(VMEM for _ in outs),
        scratch_shapes=scratch,
        compiler_params=pltpu.CompilerParams(vmem_limit_bytes=24 * 1024 * 1024),
        cost_estimate=pl.CostEstimate(flops=flops, bytes_accessed=size, transcendentals=0),
    )(*args)


def pack(ref, lead, block, value):
    rc = value.shape[0] // block[0]
    for o in range(block[0]):
        for j in range(value.shape[1] // LANES):
            ref[lead + (o, slice(j * rc, (j + 1) * rc))] = value[
                o * rc : (o + 1) * rc, j * LANES : (j + 1) * LANES
            ]


def unpack(ref, k, value):
    chunks, cw, _ = value.shape
    side = ref.shape[1]
    rc = side // chunks
    for o in range(chunks):
        for j in range(side // LANES):
            ref[k, o * rc : (o + 1) * rc, j * LANES : (j + 1) * LANES] = value[
                o, j * rc : (j + 1) * rc
            ]


def halves(value):
    high = value.astype(BF16)
    low = (value - high.astype(F32)).astype(BF16)
    return high, low


def dot(a, b):
    return jnp.dot(a, b, preferred_element_type=F32)


def mask(size, side):
    rows = lax.broadcasted_iota(jnp.int32, (side, side), 0)
    cols = lax.broadcasted_iota(jnp.int32, (side, side), 1)
    return (rows < size) & (cols < size)


def pick(couple_ref, p, here, ref):
    source = couple_ref[p, 0]
    slot = jnp.where(source == here, 0, jnp.where(source == here + 1 - 2 * (here % 2), 1, 2))
    return jnp.where(source >= 0, ref[slot], 0.0)


def apply(couple_ref, here, ref, lcat_ref, rcat_ref):
    total = None
    for p in range(lcat_ref.shape[0]):
        high, low = halves(pick(couple_ref, p, here, ref))
        mixed = dot(lcat_ref[p], jnp.concatenate([high, low, high], axis=0))
        high, low = halves(mixed)
        term = dot(jnp.concatenate([high, low, high], axis=1), rcat_ref[p])
        total = term if total is None else total + term
    return total


def rows(value):
    return jnp.sum(value.reshape(-1, LANES), axis=0, keepdims=True)


def tile(parts):
    parts = parts + [jnp.zeros((8 - len(parts), LANES), F32)]
    return jnp.concatenate(parts, axis=0)


def half_angle(middle, first, last):
    gap = last - first
    tilt = -2.0 * middle
    length = jnp.sqrt(gap * gap + tilt * tilt)
    safe = jnp.where(length > 0.0, length, 1.0)
    big = jnp.where(length > 0.0, jnp.sqrt(0.5 + 0.5 * jnp.abs(gap) / safe), 1.0)
    small = 0.5 * tilt / (safe * big)
    sign = jnp.where(tilt > 0.0, 1.0, -1.0)
    cosine = jnp.where(gap >= 0.0, big, jnp.abs(small))
    sine = jnp.where(gap >= 0.0, small, sign * big)
    return cosine, sine, 0.5 * (first + last) - 0.5 * length


def update(xx, first, xr, rr, rh, xhr, rhr):
    n = lax.rsqrt(rr - 2.0 * xr * xr + xr * xr * xx + 1e-06)
    middle = 0.5 * n * ((xhr - xr * first) + (rh - xr * first))
    last = n * n * (rhr - xr * rh - xr * xhr + xr * xr * first)
    cosine, sine, theta = half_angle(middle, first, last)
    on_r = sine * n
    on_x = cosine - on_r * xr
    xx = on_x * on_x * xx + 2.0 * on_x * on_r * xr + on_r * on_r * rr
    return on_x, on_r, theta, xx


def start_body(size_ref, psi_ref, diag_ref, x_ref, d_ref):
    block = x_ref.shape
    side = psi_ref.shape[1]
    live = mask(size_ref[0], side)
    pack(x_ref, (), block, jnp.where(live, psi_ref[0].astype(F32), 0.0))
    pack(d_ref, (), block, diag_ref[0].astype(F32))


def split_body(left_ref, right_ref, lcat_ref, rcat_ref):
    for p in range(left_ref.shape[0]):
        high, low = halves(left_ref[p, 0])
        lcat_ref[p] = jnp.concatenate([high, high, low], axis=1)
        high, low = halves(right_ref[p, 0].T)
        rcat_ref[p] = jnp.concatenate([high, high, low], axis=0)


def first_body(size_ref, couple_ref, x0, x1, x2, lcat_ref, rcat_ref, y_ref, v_ref):
    here = lax.axis_index("sec")
    side = v_ref.shape[1]
    for k, x in enumerate((x0, x1, x2)):
        unpack(v_ref, k, x[...])
    y = apply(couple_ref, here, v_ref, lcat_ref, rcat_ref)
    pack(y_ref, (), y_ref.shape, jnp.where(mask(size_ref[0], side), y, 0.0))


def fan(out_ref, cw, block, scalars):
    for o in range(out_ref.shape[0]):
        out_ref[o, :cw] = block
        out_ref[o, cw:] = scalars


def first_sum_body(part_ref, x_ref, out_ref):
    o = lax.axis_index("ops")
    cw = part_ref.shape[1]
    block = jnp.sum(part_ref[...], axis=0)
    x = x_ref[o]
    fan(out_ref, cw, block, tile([rows(x * x), rows(x * block)]))


def second_sum_body(part_ref, x_ref, r_ref, g_ref, out_ref):
    o = lax.axis_index("ops")
    cw = part_ref.shape[1]
    block = jnp.sum(part_ref[...], axis=0)
    x, r, h = x_ref[o], r_ref[0, o], g_ref[o][:cw]
    scalars = tile([rows(x * r), rows(r * r), rows(r * h), rows(x * block), rows(r * block)])
    fan(out_ref, cw, block, scalars)


def numbers(g_refs, others, cw, count):
    total = others[...]
    for g in g_refs:
        total = total + jnp.sum(g[:, cw:], axis=0)
    total = jnp.sum(total, axis=1, keepdims=True)
    return [total[i : i + 1] for i in range(count)]


def keep(out_ref, values):
    out_ref[...] = tile([jnp.broadcast_to(v, (1, LANES)) for v in values])


def second_body(
    size_ref, couple_ref, g0, g1, g2, others, x0, x1, x2, d0, d1, d2, lcat_ref, rcat_ref,
    y_ref, r_ref, c_ref, v_ref,
):
    here = lax.axis_index("sec")
    side = v_ref.shape[1]
    cw = x0.shape[1]
    squares, energy = numbers((g0, g1), others, cw, 2)
    factor = lax.rsqrt(squares + 1e-06)
    theta = energy * factor * factor
    keep(c_ref, [factor, theta, squares * factor * factor])
    for k, (g, x, d) in enumerate(((g0, x0, d0), (g1, x1, d1), (g2, x2, d2))):
        r = factor * (g[:, :cw] - theta * x[...]) / (jnp.abs(d[...] - theta) + 1.0)
        r_ref[k] = r
        unpack(v_ref, k, r)
    y = apply(couple_ref, here, v_ref, lcat_ref, rcat_ref)
    pack(y_ref, (), y_ref.shape, jnp.where(mask(size_ref[0], side), y, 0.0))


def third_body(
    size_ref, couple_ref, s0, s1, s2, others, g0, g1, g2, x0, x1, x2, d0, d1, d2, r_in, c_in,
    lcat_ref, rcat_ref, x_ref, r_ref, c_ref, part_ref, v_ref, y_ref,
):
    here = lax.axis_index("sec")
    o = lax.axis_index("ops")
    side = v_ref.shape[1]
    cw = x0.shape[1]
    xr, rr, rh, xhr, rhr = numbers((s0, s1), others, cw, 5)
    factor, first, xx = c_in[0:1, 0:1], c_in[1:2, 0:1], c_in[2:3, 0:1]
    on_x, on_r, theta, xx = update(
        xx, first, factor * xr, rr, factor * rh, factor * xhr, rhr
    )
    on_x = on_x * factor
    keep(c_ref, [theta, xx])
    for k, (s, g, x, d) in enumerate(((s0, g0, x0, d0), (s1, g1, x1, d1), (s2, g2, x2, d2))):
        x = on_x * x[...] + on_r * r_in[k]
        h = on_x * g[:, :cw] + on_r * s[:, :cw]
        r = (h - theta * x) / (jnp.abs(d[...] - theta) + 1.0)
        x_ref[k] = x
        r_ref[k] = r
        unpack(v_ref, k, r)
    y = apply(couple_ref, here, v_ref, lcat_ref, rcat_ref)
    pack(y_ref, (), y_ref.shape, jnp.where(mask(size_ref[0], side), y, 0.0))
    y = y_ref[...]
    x, r = x_ref[0, o], r_ref[0, o]
    h = on_x * g0[o][:cw] + on_r * s0[o][:cw]
    part_ref[...] = tile(
        [rows(x * r), rows(r * r), rows(r * h), rows(x_ref[0] * y), rows(r_ref[0] * y)]
    )


def last_body(
    scale, couple_ref, parts_ref, c_in, x_ref, r_ref, lcat_ref, wave_ref, turn_ref, v_ref
):
    here = lax.axis_index("sec")
    side = v_ref.shape[1]
    total = jnp.sum(jnp.sum(parts_ref[...], axis=0), axis=1, keepdims=True)
    xr, rr, rh, xhr, rhr = [total[i : i + 1] for i in range(5)]
    first, xx = c_in[0:1, 0:1], c_in[1:2, 0:1]
    on_x, on_r, _, _ = update(xx, first, xr, rr, rh, xhr, rhr)
    for k in range(3):
        unpack(v_ref, k, (on_x * scale) * x_ref[k] + (on_r * scale) * r_ref[k])
    wave = v_ref[0]
    wave_ref[0] = wave
    high, low = halves(wave.T * (1.0 / side**0.5))
    turning = jnp.concatenate([high, low, high], axis=1)
    for p in range(lcat_ref.shape[0]):
        high, low = halves(pick(couple_ref, p, here, v_ref))
        inner = dot(lcat_ref[p], jnp.concatenate([high, low, high], axis=0))
        high, low = halves(inner)
        turn_ref[p] = dot(turning, jnp.concatenate([high, high, low], axis=0))


def partner(value):
    count = lax.axis_size("sec")
    return lax.ppermute(value, "sec", [(i, i ^ 1) for i in range(count)])


def other(value):
    count = lax.axis_size("sec")
    route = []
    for i in range(1, count - 1, 2):
        route += [(i, i + 1), (i + 1, i)]
    return lax.ppermute(value, "sec", route)


def rest(value):
    count = lax.axis_size("sec")
    total = jnp.zeros_like(value)
    for d in range(2, count):
        total = total + lax.ppermute(value, "sec", [(i, i ^ d) for i in range(count)])
    return total


def exchange(value):
    return lax.all_to_all(value, "ops", 0, 0)


def local(sector_states, psi_guess, precond_diag, left_ops, right_ops, couple, new_sector):
    side = psi_guess.shape[1]
    pairs = left_ops.shape[0]
    here = lax.axis_index("sec")
    chunks = lax.axis_size("ops")
    sectors = lax.axis_size("sec")
    rc = side // chunks
    cw = rc * side // LANES
    block = jax.ShapeDtypeStruct((chunks, cw, LANES), F32)
    wide = jax.ShapeDtypeStruct((chunks, cw + 8, LANES), F32)
    three = jax.ShapeDtypeStruct((3, chunks, cw, LANES), F32)
    small = jax.ShapeDtypeStruct((8, LANES), F32)
    scratch = pltpu.VMEM((3, side, side), F32)
    work = 12 * pairs * side**3
    light = 20 * side**2

    x0, d0 = call(
        start_body, (block, block), [SMEM, VMEM, VMEM], [], light,
        sector_states, psi_guess, precond_diag,
    )
    x2, x1 = other(x0), partner(x0)
    d2, d1 = other(d0), partner(d0)
    lcat, rcat = call(
        split_body,
        (
            jax.ShapeDtypeStruct((pairs, side, 3 * side), BF16),
            jax.ShapeDtypeStruct((pairs, 3 * side, side), BF16),
        ),
        [VMEM, VMEM], [], light * pairs, left_ops, right_ops,
    )
    (y,) = call(
        first_body, (block,), [SMEM] * 2 + [VMEM] * 5, [scratch], work,
        sector_states, couple, x0, x1, x2, lcat, rcat,
    )
    (g0,) = call(
        first_sum_body, (wide,), [VMEM] * 2, [], light, exchange(y), x0
    )
    g0 = exchange(g0)
    others = rest(jnp.sum(g0[:, cw:], axis=0))
    g2, g1 = other(g0), partner(g0)
    y, r, c = call(
        second_body, (block, three, small), [SMEM] * 2 + [VMEM] * 12, [scratch], work,
        sector_states, couple, g0, g1, g2, others, x0, x1, x2, d0, d1, d2, lcat, rcat,
    )
    (s0,) = call(
        second_sum_body, (wide,), [VMEM] * 4, [], light, exchange(y), x0, r, g0
    )
    s0 = exchange(s0)
    others = rest(jnp.sum(s0[:, cw:], axis=0))
    s2, s1 = other(s0), partner(s0)
    x, r, c, part = call(
        third_body, (three, three, small, small), [SMEM] * 2 + [VMEM] * 17,
        [scratch, pltpu.VMEM(block.shape, F32)], work,
        sector_states, couple, s0, s1, s2, others, g0, g1, g2, x0, x1, x2, d0, d1, d2, r, c,
        lcat, rcat,
    )
    count = chunks * sectors
    parts = lax.all_to_all(
        jnp.broadcast_to(part[None], (count, 8, LANES)), ("ops", "sec"), 0, 0
    )
    wavefunction, turned = call(
        functools.partial(last_body, float((sectors * side * side) ** 0.5)),
        (
            jax.ShapeDtypeStruct((1, side, side), F32),
            jax.ShapeDtypeStruct((pairs, side, side), F32),
        ),
        [SMEM] + [VMEM] * 5, [scratch], work,
        couple, parts, c, x, r, lcat,
    )
    rotated_ops = jnp.where(new_sector[0] == here, turned, partner(turned))[:, None]
    return (wavefunction, rotated_ops)


def solution(mesh):
    in_specs = (
        P("sec"),
        P("sec", None, None),
        P("sec", None, None),
        P("ops", "sec", None, None),
        P("ops", "sec", None, None),
        P("ops", "sec"),
        P("sec"),
    )
    out_specs = (P("sec", None, None), P("ops", "sec", None, None))
    return jax.shard_map(local, mesh=mesh, in_specs=in_specs, out_specs=out_specs, check_vma=False)
```

```python
import functools

import jax
import jax.numpy as jnp
from jax import lax
from jax.experimental import pallas as pl
from jax.experimental.pallas import tpu as pltpu
from jax.sharding import PartitionSpec as P

LANES = 128
F32 = jnp.float32
BF16 = jnp.bfloat16
VMEM = pl.BlockSpec(memory_space=pltpu.VMEM)
SMEM = pl.BlockSpec(memory_space=pltpu.SMEM)


def call(body, outs, in_specs, scratch, flops, *args):
    size = sum(a.size * a.dtype.itemsize for a in args)
    size += sum(o.size * o.dtype.itemsize for o in outs)
    return pl.pallas_call(
        body,
        out_shape=tuple(outs),
        in_specs=in_specs,
        out_specs=tuple(VMEM for _ in outs),
        scratch_shapes=scratch,
        compiler_params=pltpu.CompilerParams(vmem_limit_bytes=24 * 1024 * 1024),
        cost_estimate=pl.CostEstimate(flops=flops, bytes_accessed=size, transcendentals=0),
    )(*args)


def pack(ref, lead, block, value):
    rc = value.shape[0] // block[0]
    for o in range(block[0]):
        for j in range(value.shape[1] // LANES):
            ref[lead + (o, slice(j * rc, (j + 1) * rc))] = value[
                o * rc : (o + 1) * rc, j * LANES : (j + 1) * LANES
            ]


def unpack(ref, k, value):
    chunks, cw, _ = value.shape
    side = ref.shape[1]
    rc = side // chunks
    for o in range(chunks):
        for j in range(side // LANES):
            ref[k, o * rc : (o + 1) * rc, j * LANES : (j + 1) * LANES] = value[
                o, j * rc : (j + 1) * rc
            ]


def halves(value):
    high = value.astype(BF16)
    low = (value - high.astype(F32)).astype(BF16)
    return high, low


def dot(a, b):
    return jnp.dot(a, b, preferred_element_type=F32)


def mask(size, side):
    rows = lax.broadcasted_iota(jnp.int32, (side, side), 0)
    cols = lax.broadcasted_iota(jnp.int32, (side, side), 1)
    return (rows < size) & (cols < size)


def pick(couple_ref, p, here, ref):
    source = couple_ref[p, 0]
    slot = jnp.where(source == here, 0, jnp.where(source == here + 1 - 2 * (here % 2), 1, 2))
    return jnp.where(source >= 0, ref[slot], 0.0)


def apply(couple_ref, here, ref, lcat_ref, rcat_ref):
    total = None
    for p in range(lcat_ref.shape[0]):
        high, low = halves(pick(couple_ref, p, here, ref))
        mixed = dot(lcat_ref[p], jnp.concatenate([high, low, high], axis=0))
        high, low = halves(mixed)
        term = dot(jnp.concatenate([high, low, high], axis=1), rcat_ref[p])
        total = term if total is None else total + term
    return total


def rows(value):
    return jnp.sum(value.reshape(-1, LANES), axis=0, keepdims=True)


def tile(parts):
    parts = parts + [jnp.zeros((8 - len(parts), LANES), F32)]
    return jnp.concatenate(parts, axis=0)


def half_angle(middle, first, last):
    gap = last - first
    tilt = -2.0 * middle
    length = jnp.sqrt(gap * gap + tilt * tilt)
    safe = jnp.where(length > 0.0, length, 1.0)
    big = jnp.where(length > 0.0, jnp.sqrt(0.5 + 0.5 * jnp.abs(gap) / safe), 1.0)
    small = 0.5 * tilt / (safe * big)
    sign = jnp.where(tilt > 0.0, 1.0, -1.0)
    cosine = jnp.where(gap >= 0.0, big, jnp.abs(small))
    sine = jnp.where(gap >= 0.0, small, sign * big)
    return cosine, sine, 0.5 * (first + last) - 0.5 * length


def update(xx, first, xr, rr, rh, xhr, rhr):
    n = lax.rsqrt(rr - 2.0 * xr * xr + xr * xr * xx + 1e-06)
    middle = 0.5 * n * ((xhr - xr * first) + (rh - xr * first))
    last = n * n * (rhr - xr * rh - xr * xhr + xr * xr * first)
    cosine, sine, theta = half_angle(middle, first, last)
    on_r = sine * n
    on_x = cosine - on_r * xr
    xx = on_x * on_x * xx + 2.0 * on_x * on_r * xr + on_r * on_r * rr
    return on_x, on_r, theta, xx


def start_body(size_ref, psi_ref, x_ref):
    live = mask(size_ref[0], psi_ref.shape[1])
    pack(x_ref, (), x_ref.shape, jnp.where(live, psi_ref[0].astype(F32), 0.0))


def split_body(left_ref, right_ref, diag_ref, lcat_ref, rcat_ref, d_ref):
    for p in range(left_ref.shape[0]):
        high, low = halves(left_ref[p, 0])
        lcat_ref[p] = jnp.concatenate([high, high, low], axis=1)
        high, low = halves(right_ref[p, 0].T)
        rcat_ref[p] = jnp.concatenate([high, high, low], axis=0)
    pack(d_ref, (), d_ref.shape, diag_ref[0].astype(F32))


def product(size_ref, couple_ref, blocks, lcat_ref, rcat_ref, y_ref, v_ref):
    here = lax.axis_index("sec")
    for k, block in enumerate(blocks):
        unpack(v_ref, k, block[...])
    y = apply(couple_ref, here, v_ref, lcat_ref, rcat_ref)
    y = jnp.where(mask(size_ref[0], v_ref.shape[1]), y, 0.0)
    pack(y_ref, (), y_ref.shape, y)


def first_body(size_ref, couple_ref, x0, x1, x2, lcat_ref, rcat_ref, y_ref, part_ref, v_ref):
    product(size_ref, couple_ref, (x0, x1, x2), lcat_ref, rcat_ref, y_ref, v_ref)
    x = x0[lax.axis_index("ops")]
    part_ref[...] = tile([rows(x * x), rows(x0[...] * y_ref[...])])


def second_body(
    size_ref, couple_ref, r0, r1, r2, x0, g0, lcat_ref, rcat_ref, y_ref, part_ref, v_ref
):
    product(size_ref, couple_ref, (r0, r1, r2), lcat_ref, rcat_ref, y_ref, v_ref)
    o = lax.axis_index("ops")
    x, r, h = x0[o], r0[o], g0[o][: x0.shape[1]]
    y = y_ref[...]
    part_ref[...] = tile(
        [rows(x * r), rows(r * r), rows(r * h), rows(x0[...] * y), rows(r0[...] * y)]
    )


def sum_body(terms_ref, mine, others, out_ref):
    cw = terms_ref.shape[1]
    block = jnp.sum(terms_ref[...], axis=0)
    scalars = mine[...] + others[...]
    for o in range(out_ref.shape[0]):
        out_ref[o, :cw] = block
        out_ref[o, cw:] = scalars


def numbers(tiles, count):
    total = jnp.sum(jnp.sum(tiles, axis=0), axis=1, keepdims=True)
    return [total[i : i + 1] for i in range(count)]


def store(out_ref, values):
    out_ref[...] = tile([jnp.broadcast_to(v, (1, LANES)) for v in values])


def first_residual_body(g_ref, x_ref, d_ref, r_ref, c_ref):
    cw = x_ref.shape[1]
    squares, energy = numbers(g_ref[:, cw:], 2)
    factor = lax.rsqrt(squares + 1e-06)
    theta = energy * factor * factor
    r = factor * (g_ref[:, :cw] - theta * x_ref[...]) / (jnp.abs(d_ref[...] - theta) + 1.0)
    r_ref[...] = r
    store(c_ref, [factor, theta, squares * factor * factor])


def second_residual_body(s_ref, g_ref, x_ref, d_ref, r_in, c_in, x_out, h_out, r_ref, c_ref):
    cw = x_ref.shape[1]
    xr, rr, rh, xhr, rhr = numbers(s_ref[:, cw:], 5)
    factor, first, xx = c_in[0:1, 0:1], c_in[1:2, 0:1], c_in[2:3, 0:1]
    on_x, on_r, theta, xx = update(
        xx, first, factor * xr, rr, factor * rh, factor * xhr, rhr
    )
    on_x = on_x * factor
    x = on_x * x_ref[...] + on_r * r_in[...]
    h = on_x * g_ref[:, :cw] + on_r * s_ref[:, :cw]
    x_out[...] = x
    h_out[...] = h
    r_ref[...] = (h - theta * x) / (jnp.abs(d_ref[...] - theta) + 1.0)
    store(c_ref, [theta, xx, on_x, on_r])


def last_body(
    scale, couple_ref, parts_ref, c_in, x0, x1, x2, r0, r1, r2, s0, s1, s2, lcat_ref,
    wave_ref, turn_ref, v_ref,
):
    here = lax.axis_index("sec")
    side = v_ref.shape[1]
    xr, rr, rh, xhr, rhr = numbers(parts_ref[...], 5)
    first, xx, x_part, r_part = [c_in[i : i + 1, 0:1] for i in range(4)]
    on_x, on_s, _, _ = update(xx, first, xr, rr, rh, xhr, rhr)
    on_r = on_x * r_part * scale
    on_x = on_x * x_part * scale
    on_s = on_s * scale
    for k, (x, r, s) in enumerate(((x0, r0, s0), (x1, r1, s1), (x2, r2, s2))):
        unpack(v_ref, k, on_x * x[...] + on_r * r[...] + on_s * s[...])
    wave = v_ref[0]
    wave_ref[0] = wave
    high, low = halves(wave.T * (1.0 / side**0.5))
    turning = jnp.concatenate([high, low, high], axis=1)
    for p in range(lcat_ref.shape[0]):
        high, low = halves(pick(couple_ref, p, here, v_ref))
        inner = dot(lcat_ref[p], jnp.concatenate([high, low, high], axis=0))
        high, low = halves(inner)
        turn_ref[p] = dot(turning, jnp.concatenate([high, high, low], axis=0))


def partner(value):
    count = lax.axis_size("sec")
    return lax.ppermute(value, "sec", [(i, i ^ 1) for i in range(count)])


def other(value):
    count = lax.axis_size("sec")
    route = []
    for i in range(1, count - 1, 2):
        route += [(i, i + 1), (i + 1, i)]
    return lax.ppermute(value, "sec", route)


def over_sectors(value):
    count = lax.axis_size("sec")
    total = jnp.zeros_like(value)
    for d in range(1, count):
        total = total + lax.ppermute(value, "sec", [(i, i ^ d) for i in range(count)])
    return total


def exchange(value):
    return lax.all_to_all(value, "ops", 0, 0)


def local(sector_states, psi_guess, precond_diag, left_ops, right_ops, couple, new_sector):
    side = psi_guess.shape[1]
    pairs = left_ops.shape[0]
    here = lax.axis_index("sec")
    chunks = lax.axis_size("ops")
    sectors = lax.axis_size("sec")
    cw = side // chunks * side // LANES
    block = jax.ShapeDtypeStruct((chunks, cw, LANES), F32)
    wide = jax.ShapeDtypeStruct((chunks, cw + 8, LANES), F32)
    small = jax.ShapeDtypeStruct((8, LANES), F32)
    scratch = pltpu.VMEM((3, side, side), F32)
    work = 12 * pairs * side**3
    light = 20 * side**2

    def gathered(y, part):
        others = over_sectors(part)
        (full,) = call(
            sum_body, (wide,), [VMEM] * 3, [], light, exchange(y), part, others
        )
        return exchange(full)

    (x0,) = call(start_body, (block,), [SMEM, VMEM], [], light, sector_states, psi_guess)
    x2, x1 = other(x0), partner(x0)
    lcat, rcat, d = call(
        split_body,
        (
            jax.ShapeDtypeStruct((pairs, side, 3 * side), BF16),
            jax.ShapeDtypeStruct((pairs, 3 * side, side), BF16),
            block,
        ),
        [VMEM] * 3, [], light * pairs, left_ops, right_ops, precond_diag,
    )
    y, part = call(
        first_body, (block, small), [SMEM] * 2 + [VMEM] * 5, [scratch], work,
        sector_states, couple, x0, x1, x2, lcat, rcat,
    )
    g = gathered(y, part)
    r0, c = call(first_residual_body, (block, small), [VMEM] * 3, [], light, g, x0, d)
    r2, r1 = other(r0), partner(r0)
    y, part = call(
        second_body, (block, small), [SMEM] * 2 + [VMEM] * 7, [scratch], work,
        sector_states, couple, r0, r1, r2, x0, g, lcat, rcat,
    )
    s = gathered(y, part)
    x, h, s0, c = call(
        second_residual_body, (block, block, block, small), [VMEM] * 6, [], light,
        s, g, x0, d, r0, c,
    )
    s2, s1 = other(s0), partner(s0)
    y, part = call(
        second_body, (block, small), [SMEM] * 2 + [VMEM] * 7, [scratch], work,
        sector_states, couple, s0, s1, s2, x, h, lcat, rcat,
    )
    count = chunks * sectors
    parts = lax.all_to_all(
        jnp.broadcast_to(part[None], (count, 8, LANES)), ("ops", "sec"), 0, 0
    )
    wavefunction, turned = call(
        functools.partial(last_body, float((sectors * side * side) ** 0.5)),
        (
            jax.ShapeDtypeStruct((1, side, side), F32),
            jax.ShapeDtypeStruct((pairs, side, side), F32),
        ),
        [SMEM] + [VMEM] * 12, [scratch], work,
        couple, parts, c, x0, x1, x2, r0, r1, r2, s0, s1, s2, lcat,
    )
    rotated_ops = jnp.where(new_sector[0] == here, turned, partner(turned))[:, None]
    return (wavefunction, rotated_ops)


def solution(mesh):
    in_specs = (
        P("sec"),
        P("sec", None, None),
        P("sec", None, None),
        P("ops", "sec", None, None),
        P("ops", "sec", None, None),
        P("ops", "sec"),
        P("sec"),
    )
    out_specs = (P("sec", None, None), P("ops", "sec", None, None))
    return jax.shard_map(local, mesh=mesh, in_specs=in_specs, out_specs=out_specs, check_vma=False)
```

```python
import functools

import jax
import jax.numpy as jnp
from jax import lax
from jax.experimental import pallas as pl
from jax.experimental.pallas import tpu as pltpu
from jax.sharding import PartitionSpec as P


LANES = 128
F32 = jnp.float32
BF16 = jnp.bfloat16
VMEM = pl.BlockSpec(memory_space=pltpu.VMEM)
SMEM = pl.BlockSpec(memory_space=pltpu.SMEM)


def call(body, outs, in_specs, scratch, flops, *args):
    size = sum(a.size * a.dtype.itemsize for a in args)
    size += sum(o.size * o.dtype.itemsize for o in outs)
    return pl.pallas_call(
        body,
        out_shape=tuple(outs),
        in_specs=in_specs,
        out_specs=tuple(VMEM for _ in outs),
        scratch_shapes=scratch,
        compiler_params=pltpu.CompilerParams(vmem_limit_bytes=8 * 1024 * 1024),
        cost_estimate=pl.CostEstimate(flops=flops, bytes_accessed=size, transcendentals=0),
    )(*args)


def pack(ref, lead, block, value):
    rc = value.shape[0] // block[0]
    for o in range(block[0]):
        for j in range(value.shape[1] // LANES):
            ref[lead + (o, slice(j * rc, (j + 1) * rc))] = value[
                o * rc : (o + 1) * rc, j * LANES : (j + 1) * LANES
            ]


def unpack(ref, k, value):
    chunks, _, _ = value.shape
    side = ref.shape[1]
    rc = side // chunks
    for o in range(chunks):
        for j in range(side // LANES):
            ref[k, o * rc : (o + 1) * rc, j * LANES : (j + 1) * LANES] = value[
                o, j * rc : (j + 1) * rc
            ]


def halves(value):
    high = value.astype(BF16)
    low = (value - high.astype(F32)).astype(BF16)
    return high, low


def dot(a, b):
    return jnp.dot(a, b, preferred_element_type=F32)


def mask(size, side):
    rows = lax.broadcasted_iota(jnp.int32, (side, side), 0)
    cols = lax.broadcasted_iota(jnp.int32, (side, side), 1)
    return (rows < size) & (cols < size)


def pick(couple_ref, p, here, ref):
    source = couple_ref[p, 0]
    slot = jnp.where(source == here, 0, jnp.where(source == here + 1 - 2 * (here % 2), 1, 2))
    return jnp.where(source >= 0, ref[slot], 0.0)


def apply(couple_ref, here, ref, lcat_ref, rcat_ref, m_ref):
    total = None
    for p in range(lcat_ref.shape[0]):
        high, low = halves(pick(couple_ref, p, here, ref))
        mixed = dot(lcat_ref[p], jnp.concatenate([high, low, high], axis=0))
        m_ref[p] = mixed
        high, low = halves(mixed)
        term = dot(jnp.concatenate([high, low, high], axis=1), rcat_ref[p])
        total = term if total is None else total + term
    return total


def rows(value):
    return jnp.sum(value.reshape(-1, LANES), axis=0, keepdims=True)


def tile(parts):
    parts = parts + [jnp.zeros((8 - len(parts), LANES), F32)]
    return jnp.concatenate(parts, axis=0)


def half_angle(middle, first, last):
    gap = last - first
    tilt = -2.0 * middle
    length = jnp.sqrt(gap * gap + tilt * tilt)
    safe = jnp.where(length > 0.0, length, 1.0)
    big = jnp.where(length > 0.0, jnp.sqrt(0.5 + 0.5 * jnp.abs(gap) / safe), 1.0)
    small = 0.5 * tilt / (safe * big)
    sign = jnp.where(tilt > 0.0, 1.0, -1.0)
    cosine = jnp.where(gap >= 0.0, big, jnp.abs(small))
    sine = jnp.where(gap >= 0.0, small, sign * big)
    return cosine, sine, 0.5 * (first + last) - 0.5 * length


def update(xx, first, xr, rr, rh, xhr, rhr):
    n = lax.rsqrt(rr - 2.0 * xr * xr + xr * xr * xx + 1e-06)
    middle = 0.5 * n * ((xhr - xr * first) + (rh - xr * first))
    last = n * n * (rhr - xr * rh - xr * xhr + xr * xr * first)
    cosine, sine, theta = half_angle(middle, first, last)
    on_r = sine * n
    on_x = cosine - on_r * xr
    xx = on_x * on_x * xx + 2.0 * on_x * on_r * xr + on_r * on_r * rr
    return on_x, on_r, theta, xx


def start_body(size_ref, psi_ref, x_ref):
    live = mask(size_ref[0], psi_ref.shape[1])
    pack(x_ref, (), x_ref.shape, jnp.where(live, psi_ref[0].astype(F32), 0.0))


def split_body(left_ref, right_ref, diag_ref, lcat_ref, rcat_ref, d_ref):
    for p in range(left_ref.shape[0]):
        high, low = halves(left_ref[p, 0])
        lcat_ref[p] = jnp.concatenate([high, high, low], axis=1)
        high, low = halves(right_ref[p, 0].T)
        rcat_ref[p] = jnp.concatenate([high, high, low], axis=0)
    pack(d_ref, (), d_ref.shape, diag_ref[0].astype(F32))


def product(size_ref, couple_ref, blocks, lcat_ref, rcat_ref, y_ref, m_ref, v_ref):
    here = lax.axis_index("sec")
    for k, block in enumerate(blocks):
        unpack(v_ref, k, block[...])
    y = apply(couple_ref, here, v_ref, lcat_ref, rcat_ref, m_ref)
    y = jnp.where(mask(size_ref[0], v_ref.shape[1]), y, 0.0)
    pack(y_ref, (), y_ref.shape, y)


def first_body(
    size_ref, couple_ref, x0, x1, x2, lcat_ref, rcat_ref, y_ref, m_ref, part_ref, v_ref
):
    product(size_ref, couple_ref, (x0, x1, x2), lcat_ref, rcat_ref, y_ref, m_ref, v_ref)
    x = x0[lax.axis_index("ops")]
    part_ref[...] = tile([rows(x * x), rows(x0[...] * y_ref[...])])


def second_body(
    size_ref, couple_ref, r0, r1, r2, x0, g0, lcat_ref, rcat_ref, y_ref, m_ref, part_ref, v_ref
):
    product(size_ref, couple_ref, (r0, r1, r2), lcat_ref, rcat_ref, y_ref, m_ref, v_ref)
    o = lax.axis_index("ops")
    x, r, h = x0[o], r0[o], g0[o][: x0.shape[1]]
    y = y_ref[...]
    part_ref[...] = tile(
        [rows(x * r), rows(r * r), rows(r * h), rows(x0[...] * y), rows(r0[...] * y)]
    )


def sum_body(terms_ref, mine, others, out_ref):
    cw = terms_ref.shape[1]
    block = jnp.sum(terms_ref[...], axis=0)
    scalars = mine[...] + others[...]
    for o in range(out_ref.shape[0]):
        out_ref[o, :cw] = block
        out_ref[o, cw:] = scalars


def numbers(tiles, count):
    total = jnp.sum(jnp.sum(tiles, axis=0), axis=1, keepdims=True)
    return [total[i : i + 1] for i in range(count)]


def store(out_ref, values):
    out_ref[...] = tile([jnp.broadcast_to(v, (1, LANES)) for v in values])


def first_residual_body(g_ref, x_ref, d_ref, r_ref, c_ref):
    cw = x_ref.shape[1]
    squares, energy = numbers(g_ref[:, cw:], 2)
    factor = lax.rsqrt(squares + 1e-06)
    theta = energy * factor * factor
    r = factor * (g_ref[:, :cw] - theta * x_ref[...]) / (jnp.abs(d_ref[...] - theta) + 1.0)
    r_ref[...] = r
    store(c_ref, [factor, theta, squares * factor * factor])


def second_residual_body(s_ref, g_ref, x_ref, d_ref, r_in, c_in, x_out, h_out, r_ref, c_ref):
    cw = x_ref.shape[1]
    xr, rr, rh, xhr, rhr = numbers(s_ref[:, cw:], 5)
    factor, first, xx = c_in[0:1, 0:1], c_in[1:2, 0:1], c_in[2:3, 0:1]
    on_x, on_r, theta, xx = update(
        xx, first, factor * xr, rr, factor * rh, factor * xhr, rhr
    )
    on_x = on_x * factor
    x = on_x * x_ref[...] + on_r * r_in[...]
    h = on_x * g_ref[:, :cw] + on_r * s_ref[:, :cw]
    x_out[...] = x
    h_out[...] = h
    r_ref[...] = (h - theta * x) / (jnp.abs(d_ref[...] - theta) + 1.0)
    store(c_ref, [theta, xx, on_x, on_r])


def last_body(
    scale, label_ref, parts_ref, c_in, x0, x1, r0, r1, s0, s1, mx, mr, ms, nx, nr, ns,
    wave_ref, turn_ref, v_ref,
):
    side = v_ref.shape[1]
    stay = label_ref[0] == lax.axis_index("sec")
    xr, rr, rh, xhr, rhr = numbers(parts_ref[...], 5)
    first, xx, x_part, r_part = [c_in[i : i + 1, 0:1] for i in range(4)]
    on_x, on_s, _, _ = update(xx, first, xr, rr, rh, xhr, rhr)
    on_r = on_x * r_part * scale
    on_x = on_x * x_part * scale
    on_s = on_s * scale
    for k, (x, r, s) in enumerate(((x0, r0, s0), (x1, r1, s1))):
        unpack(v_ref, k, on_x * x[...] + on_r * r[...] + on_s * s[...])
    wave_ref[0] = v_ref[0]
    high, low = halves(jnp.where(stay, v_ref[0], v_ref[1]).T * (1.0 / side**0.5))
    turning = jnp.concatenate([high, low, high], axis=1)
    for p in range(turn_ref.shape[0]):
        inner = (
            on_x * jnp.where(stay, mx[p], nx[p])
            + on_r * jnp.where(stay, mr[p], nr[p])
            + on_s * jnp.where(stay, ms[p], ns[p])
        )
        high, low = halves(inner)
        turn_ref[p, 0] = dot(turning, jnp.concatenate([high, high, low], axis=0))


def paired(value):
    count = lax.axis_size("sec")
    return lax.ppermute(value, "sec", [(i, i ^ 1) for i in range(count)])


def other(value):
    count = lax.axis_size("sec")
    route = []
    for i in range(1, count - 1, 2):
        route += [(i, i + 1), (i + 1, i)]
    return lax.ppermute(value, "sec", route)


def over_sectors(value):
    count = lax.axis_size("sec")
    total = jnp.zeros_like(value)
    for d in range(1, count):
        total = total + lax.ppermute(value, "sec", [(i, i ^ d) for i in range(count)])
    return total


def exchange(value):
    return lax.all_to_all(value, "ops", 0, 0)


def local(sector_states, psi_guess, precond_diag, left_ops, right_ops, couple, new_sector):
    side = psi_guess.shape[1]
    pairs = left_ops.shape[0]
    chunks = lax.axis_size("ops")
    sectors = lax.axis_size("sec")
    cw = side // chunks * side // LANES
    block = jax.ShapeDtypeStruct((chunks, cw, LANES), F32)
    wide = jax.ShapeDtypeStruct((chunks, cw + 8, LANES), F32)
    small = jax.ShapeDtypeStruct((8, LANES), F32)
    inner = jax.ShapeDtypeStruct((pairs, side, side), F32)
    scratch = pltpu.VMEM((3, side, side), F32)
    work = 12 * pairs * side**3
    light = 20 * side**2

    def gathered(y, part):
        others = over_sectors(part)
        (full,) = call(sum_body, (wide,), [VMEM] * 3, [], light, exchange(y), part, others)
        return exchange(full)

    (x0,) = call(start_body, (block,), [SMEM, VMEM], [], light, sector_states, psi_guess)
    x2, x1 = other(x0), paired(x0)
    lcat, rcat, d = call(
        split_body,
        (
            jax.ShapeDtypeStruct((pairs, side, 3 * side), BF16),
            jax.ShapeDtypeStruct((pairs, 3 * side, side), BF16),
            block,
        ),
        [VMEM] * 3, [], light * pairs, left_ops, right_ops, precond_diag,
    )
    y, mx, part = call(
        first_body, (block, inner, small), [SMEM] * 2 + [VMEM] * 5, [scratch], work,
        sector_states, couple, x0, x1, x2, lcat, rcat,
    )
    g = gathered(y, part)
    r0, c = call(first_residual_body, (block, small), [VMEM] * 3, [], light, g, x0, d)
    r2, r1 = other(r0), paired(r0)
    y, mr, part = call(
        second_body, (block, inner, small), [SMEM] * 2 + [VMEM] * 7, [scratch], work,
        sector_states, couple, r0, r1, r2, x0, g, lcat, rcat,
    )
    s = gathered(y, part)
    x, h, s0, c = call(
        second_residual_body, (block, block, block, small), [VMEM] * 6, [], light,
        s, g, x0, d, r0, c,
    )
    s2, s1 = other(s0), paired(s0)
    y, ms, part = call(
        second_body, (block, inner, small), [SMEM] * 2 + [VMEM] * 7, [scratch], work,
        sector_states, couple, s0, s1, s2, x, h, lcat, rcat,
    )
    nx, nr, ns = paired(mx), paired(mr), paired(ms)
    count = chunks * sectors
    parts = lax.all_to_all(jnp.broadcast_to(part[None], (count, 8, LANES)), ("ops", "sec"), 0, 0)
    return call(
        functools.partial(last_body, float((sectors * side * side) ** 0.5)),
        (
            jax.ShapeDtypeStruct((1, side, side), F32),
            jax.ShapeDtypeStruct((pairs, 1, side, side), F32),
        ),
        [SMEM] + [VMEM] * 14, [pltpu.VMEM((2, side, side), F32)], work,
        new_sector, parts, c, x0, x1, r0, r1, s0, s1, mx, mr, ms, nx, nr, ns,
    )


def solution(mesh):
    in_specs = (
        P("sec"),
        P("sec", None, None),
        P("sec", None, None),
        P("ops", "sec", None, None),
        P("ops", "sec", None, None),
        P("ops", "sec"),
        P("sec"),
    )
    out_specs = (P("sec", None, None), P("ops", "sec", None, None))
    return jax.shard_map(local, mesh=mesh, in_specs=in_specs, out_specs=out_specs, check_vma=False)
```

```python
import functools

import jax
import jax.numpy as jnp
from jax import lax
from jax.experimental import pallas as pl
from jax.experimental.pallas import tpu as pltpu
from jax.sharding import PartitionSpec as P


LANES = 128
F32 = jnp.float32
BF16 = jnp.bfloat16
VMEM = pl.BlockSpec(memory_space=pltpu.VMEM)
SMEM = pl.BlockSpec(memory_space=pltpu.SMEM)


def call(body, outs, in_specs, scratch, flops, *args):
    size = sum(a.size * a.dtype.itemsize for a in args)
    size += sum(o.size * o.dtype.itemsize for o in outs)
    return pl.pallas_call(
        body,
        out_shape=tuple(outs),
        in_specs=in_specs,
        out_specs=tuple(VMEM for _ in outs),
        scratch_shapes=scratch,
        compiler_params=pltpu.CompilerParams(vmem_limit_bytes=8 * 1024 * 1024),
        cost_estimate=pl.CostEstimate(flops=flops, bytes_accessed=size, transcendentals=0),
    )(*args)


def pack(ref, lead, block, value):
    rc = value.shape[0] // block[0]
    for o in range(block[0]):
        for j in range(value.shape[1] // LANES):
            ref[lead + (o, slice(j * rc, (j + 1) * rc))] = value[
                o * rc : (o + 1) * rc, j * LANES : (j + 1) * LANES
            ]


def unpack(ref, k, value):
    chunks, _, _ = value.shape
    side = ref.shape[1]
    rc = side // chunks
    for o in range(chunks):
        for j in range(side // LANES):
            ref[k, o * rc : (o + 1) * rc, j * LANES : (j + 1) * LANES] = value[
                o, j * rc : (j + 1) * rc
            ]


def halves(value):
    high = value.astype(BF16)
    low = (value - high.astype(F32)).astype(BF16)
    return high, low


def dot(a, b):
    return jnp.dot(a, b, preferred_element_type=F32)


def three(ah, al, bh, bl):
    return dot(
        jnp.concatenate([ah, ah, al], axis=1), jnp.concatenate([bh, bl, bh], axis=0)
    )


def mask(size, side):
    rows = lax.broadcasted_iota(jnp.int32, (side, side), 0)
    cols = lax.broadcasted_iota(jnp.int32, (side, side), 1)
    return (rows < size) & (cols < size)


def pick(couple_ref, p, here, ref):
    source = couple_ref[p]
    slot = jnp.where(source == here, 0, jnp.where(source == here + 1 - 2 * (here % 2), 1, 2))
    return jnp.where(source >= 0, ref[slot], 0.0)


def mix(couple_ref, p, here, ref, lcat_ref):
    high, low = halves(pick(couple_ref, p, here, ref))
    return three(lcat_ref[p, 0], lcat_ref[p, 1], high, low)


def fold(mixed, rcat_ref):
    total = None
    for p, one in enumerate(mixed):
        high, low = halves(one)
        term = three(high, low, rcat_ref[p, 0], rcat_ref[p, 1])
        total = term if total is None else total + term
    return total


def rows(value):
    return jnp.sum(value.reshape(-1, LANES), axis=0, keepdims=True)


def tile(parts):
    parts = parts + [jnp.zeros((8 - len(parts), LANES), F32)]
    return jnp.concatenate(parts, axis=0)


def half_angle(middle, first, last):
    gap = last - first
    tilt = -2.0 * middle
    length = jnp.sqrt(gap * gap + tilt * tilt)
    safe = jnp.where(length > 0.0, length, 1.0)
    big = jnp.where(length > 0.0, jnp.sqrt(0.5 + 0.5 * jnp.abs(gap) / safe), 1.0)
    small = 0.5 * tilt / (safe * big)
    sign = jnp.where(tilt > 0.0, 1.0, -1.0)
    cosine = jnp.where(gap >= 0.0, big, jnp.abs(small))
    sine = jnp.where(gap >= 0.0, small, sign * big)
    return cosine, sine, 0.5 * (first + last) - 0.5 * length


def update(xx, first, xr, rr, rh, xhr, rhr):
    n = lax.rsqrt(rr - 2.0 * xr * xr + xr * xr * xx + 1e-06)
    middle = 0.5 * n * ((xhr - xr * first) + (rh - xr * first))
    last = n * n * (rhr - xr * rh - xr * xhr + xr * xr * first)
    cosine, sine, theta = half_angle(middle, first, last)
    on_r = sine * n
    on_x = cosine - on_r * xr
    xx = on_x * on_x * xx + 2.0 * on_x * on_r * xr + on_r * on_r * rr
    return on_x, on_r, theta, xx


def start_body(size_ref, psi_ref, x_ref):
    live = mask(size_ref[0], psi_ref.shape[1])
    pack(x_ref, (), x_ref.shape, jnp.where(live, psi_ref[0].astype(F32), 0.0))


def split_body(label_ref, left_ref, right_ref, lcat_ref, rcat_ref, flag_ref):
    for p in range(left_ref.shape[0]):
        lcat_ref[p, 0], lcat_ref[p, 1] = halves(left_ref[p, 0])
        rcat_ref[p, 0], rcat_ref[p, 1] = halves(right_ref[p, 0].T)
    stay = jnp.where(label_ref[0] == lax.axis_index("sec"), 1.0, 0.0)
    flag_ref[...] = jnp.full(flag_ref.shape, stay)


def mix_all(couple_ref, blocks, lcat_ref, m_ref, v_ref):
    here = lax.axis_index("sec")
    for k, block in enumerate(blocks):
        unpack(v_ref, k, block[...])
    mixed = [mix(couple_ref, p, here, v_ref, lcat_ref) for p in range(lcat_ref.shape[0])]
    for p, one in enumerate(mixed):
        m_ref[p] = one
    return mixed


def fold_all(size_ref, mixed, rcat_ref, y_ref):
    y = fold(mixed, rcat_ref)
    pack(y_ref, (), y_ref.shape, jnp.where(mask(size_ref[0], y.shape[0]), y, 0.0))
    return y_ref[...]


def first_body(
    size_ref, couple_ref, x0, x1, x2, lcat_ref, rcat_ref, y_ref, m_ref, part_ref, v_ref
):
    mixed = mix_all(couple_ref, (x0, x1, x2), lcat_ref, m_ref, v_ref)
    y = fold_all(size_ref, mixed, rcat_ref, y_ref)
    x = x0[lax.axis_index("ops")]
    part_ref[...] = tile([rows(x * x), rows(x0[...] * y)])


def five(x0, r0, h0, y):
    o = lax.axis_index("ops")
    x, r, h = x0[o], r0[o], h0[o][: x0.shape[1]]
    return tile([rows(x * r), rows(r * r), rows(r * h), rows(x0[...] * y), rows(r0[...] * y)])


def second_body(
    size_ref, couple_ref, r0, r1, r2, x0, g0, lcat_ref, rcat_ref, y_ref, m_ref, part_ref, v_ref
):
    mixed = mix_all(couple_ref, (r0, r1, r2), lcat_ref, m_ref, v_ref)
    part_ref[...] = five(x0, r0, g0, fold_all(size_ref, mixed, rcat_ref, y_ref))


def mix_body(couple_ref, r0, r1, r2, lcat_ref, m_ref, v_ref):
    mix_all(couple_ref, (r0, r1, r2), lcat_ref, m_ref, v_ref)


def fold_body(size_ref, m_ref, r0, x0, h0, rcat_ref, part_ref, y_ref):
    mixed = [m_ref[p] for p in range(m_ref.shape[0])]
    part_ref[...] = five(x0, r0, h0, fold_all(size_ref, mixed, rcat_ref, y_ref))


def blend_body(c_in, a_ref, b_ref, x_ref, out_ref):
    pairs = a_ref.shape[0]
    out_ref[:pairs] = c_in[2:3, 0:1] * a_ref[...] + c_in[3:4, 0:1] * b_ref[...]
    unpack(out_ref, pairs, x_ref[...])


def cross_body(flag_ref, b_ref, n_ref, m_ref, w_ref, s0, s1, u_ref, v_ref):
    stay = flag_ref[0:1, 0:1] > 0.5
    pairs, side, _ = m_ref.shape
    unpack(v_ref, 0, jnp.where(stay[None], s0[...], s1[...]))
    x = jnp.where(stay, b_ref[pairs], n_ref[pairs])
    left = jnp.concatenate([x.T, v_ref[0].T], axis=0)
    lh, ll = halves(left)
    for p in range(pairs):
        old, new = jnp.where(stay, b_ref[p], n_ref[p]), jnp.where(stay, m_ref[p], w_ref[p])
        rh, rl = halves(jnp.concatenate([old, new], axis=1))
        both = three(lh, ll, rh, rl)
        u_ref[0, p] = both[:side, :side]
        u_ref[1, p] = both[:side, side:] + both[side:, :side]
        u_ref[2, p] = both[side:, side:]


def sum_body(terms_ref, mine, *refs):
    others, out_ref = refs[:-1], refs[-1]
    cw = terms_ref.shape[1]
    block = jnp.sum(terms_ref[...], axis=0)
    scalars = mine[...]
    for one in others:
        scalars = scalars + one[...]
    for o in range(out_ref.shape[0]):
        out_ref[o, :cw] = block
        out_ref[o, cw:] = scalars


def numbers(tiles, count):
    total = jnp.sum(jnp.sum(tiles, axis=0), axis=1, keepdims=True)
    return [total[i : i + 1] for i in range(count)]


def store(out_ref, values):
    out_ref[...] = tile([jnp.broadcast_to(v, (1, LANES)) for v in values])


def first_residual_body(g_ref, x_ref, diag_ref, r_ref, c_ref, d_ref):
    pack(d_ref, (), d_ref.shape, diag_ref[0].astype(F32))
    cw = x_ref.shape[1]
    squares, energy = numbers(g_ref[:, cw:], 2)
    factor = lax.rsqrt(squares + 1e-06)
    theta = energy * factor * factor
    r = factor * (g_ref[:, :cw] - theta * x_ref[...]) / (jnp.abs(d_ref[...] - theta) + 1.0)
    r_ref[...] = r
    store(c_ref, [factor, theta, squares * factor * factor])


def second_residual_body(
    s_ref, g_ref, x_ref, diag_ref, r_in, c_in, x_out, h_out, r_ref, c_ref, d_ref
):
    pack(d_ref, (), d_ref.shape, diag_ref[0].astype(F32))
    cw = x_ref.shape[1]
    xr, rr, rh, xhr, rhr = numbers(s_ref[:, cw:], 5)
    factor, first, xx = c_in[0:1, 0:1], c_in[1:2, 0:1], c_in[2:3, 0:1]
    on_x, on_r, theta, xx = update(
        xx, first, factor * xr, rr, factor * rh, factor * xhr, rhr
    )
    on_x = on_x * factor
    x = on_x * x_ref[...] + on_r * r_in[...]
    h = on_x * g_ref[:, :cw] + on_r * s_ref[:, :cw]
    x_out[...] = x
    h_out[...] = h
    r_ref[...] = (h - theta * x) / (jnp.abs(d_ref[...] - theta) + 1.0)
    store(c_ref, [theta, xx, on_x, on_r])


def last_body(scale, parts_ref, c_in, b_ref, s0, u_ref, wave_ref, turn_ref, v_ref):
    side = v_ref.shape[1]
    pairs = u_ref.shape[1]
    xr, rr, rh, xhr, rhr = numbers(parts_ref[...], 5)
    on_x, on_s, _, _ = update(c_in[1:2, 0:1], c_in[0:1, 0:1], xr, rr, rh, xhr, rhr)
    on_x = on_x * scale
    on_s = on_s * scale
    unpack(v_ref, 0, on_s * s0[...])
    wave_ref[0] = on_x * b_ref[pairs] + v_ref[0]
    root = 1.0 / side**0.5
    xx, xs, ss = on_x * on_x * root, on_x * on_s * root, on_s * on_s * root
    for p in range(pairs):
        turn_ref[p, 0] = xx * u_ref[0, p] + xs * u_ref[1, p] + ss * u_ref[2, p]


def paired(value):
    count = lax.axis_size("sec")
    return lax.ppermute(value, "sec", [(i, i ^ 1) for i in range(count)])


def other(value):
    count = lax.axis_size("sec")
    route = []
    for i in range(1, count - 1, 2):
        route += [(i, i + 1), (i + 1, i)]
    return lax.ppermute(value, "sec", route)


def over_sectors(value):
    count = lax.axis_size("sec")
    found = []
    for d in range(1, count):
        found.append(lax.ppermute(value, "sec", [(i, i ^ d) for i in range(count)]))
    return found


def exchange(value):
    return lax.all_to_all(value, "ops", 0, 0)


def local(sector_states, psi_guess, precond_diag, left_ops, right_ops, couple, new_sector):
    side = psi_guess.shape[1]
    pairs = left_ops.shape[0]
    couple = couple.reshape(pairs)
    chunks = lax.axis_size("ops")
    sectors = lax.axis_size("sec")
    cw = side // chunks * side // LANES
    block = jax.ShapeDtypeStruct((chunks, cw, LANES), F32)
    wide = jax.ShapeDtypeStruct((chunks, cw + 8, LANES), F32)
    small = jax.ShapeDtypeStruct((8, LANES), F32)
    inner = jax.ShapeDtypeStruct((pairs, side, side), F32)
    scratch = pltpu.VMEM((3, side, side), F32)
    work = 12 * pairs * side**3
    light = 20 * side**2

    def gathered(y, part):
        others = over_sectors(part)
        (full,) = call(
            sum_body, (wide,), [VMEM] * (2 + len(others)), [], light,
            exchange(y), part, *others,
        )
        return exchange(full)

    (x0,) = call(start_body, (block,), [SMEM, VMEM], [], light, sector_states, psi_guess)
    x2, x1 = other(x0), paired(x0)
    lcat, rcat, flag = call(
        split_body,
        (
            jax.ShapeDtypeStruct((pairs, 2, side, side), BF16),
            jax.ShapeDtypeStruct((pairs, 2, side, side), BF16),
            small,
        ),
        [SMEM] + [VMEM] * 2, [], light * pairs, new_sector, left_ops, right_ops,
    )
    y, mx, part = call(
        first_body, (block, inner, small), [SMEM] * 2 + [VMEM] * 5, [scratch], work,
        sector_states, couple, x0, x1, x2, lcat, rcat,
    )
    g = gathered(y, part)
    r0, c = call(
        first_residual_body, (block, small), [VMEM] * 3, [pltpu.VMEM(block.shape, F32)], light,
        g, x0, precond_diag,
    )
    r2, r1 = other(r0), paired(r0)
    y, mr, part = call(
        second_body, (block, inner, small), [SMEM] * 2 + [VMEM] * 7, [scratch], work,
        sector_states, couple, r0, r1, r2, x0, g, lcat, rcat,
    )
    s = gathered(y, part)
    x, h, s0, c = call(
        second_residual_body, (block, block, block, small), [VMEM] * 6,
        [pltpu.VMEM(block.shape, F32)], light, s, g, x0, precond_diag, r0, c,
    )
    s2, s1 = other(s0), paired(s0)
    (mx,) = call(
        blend_body, (jax.ShapeDtypeStruct((pairs + 1, side, side), F32),), [VMEM] * 4, [],
        light, c, mx, mr, x,
    )
    nx = paired(mx)
    (ms,) = call(
        mix_body, (inner,), [SMEM] + [VMEM] * 4, [scratch], work // 2,
        couple, s0, s1, s2, lcat,
    )
    ns = paired(ms)
    (part,) = call(
        fold_body, (small,), [SMEM] + [VMEM] * 5, [pltpu.VMEM(block.shape, F32)], work // 2,
        sector_states, ms, s0, x, h, rcat,
    )
    count = chunks * sectors
    parts = lax.all_to_all(jnp.broadcast_to(part[None], (count, 8, LANES)), ("ops", "sec"), 0, 0)
    single = pltpu.VMEM((1, side, side), F32)
    (u,) = call(
        cross_body, (jax.ShapeDtypeStruct((3, pairs, side, side), F32),), [VMEM] * 7,
        [single], work, flag, mx, nx, ms, ns, s0, s1,
    )
    return call(
        functools.partial(last_body, float((sectors * side * side) ** 0.5)),
        (
            jax.ShapeDtypeStruct((1, side, side), F32),
            jax.ShapeDtypeStruct((pairs, 1, side, side), F32),
        ),
        [VMEM] * 5, [single], light, parts, c, mx, s0, u,
    )


def solution(mesh):
    in_specs = (
        P("sec"),
        P("sec", None, None),
        P("sec", None, None),
        P("ops", "sec", None, None),
        P("ops", "sec", None, None),
        P("ops", "sec"),
        P("sec"),
    )
    out_specs = (P("sec", None, None), P("ops", "sec", None, None))
    return jax.shard_map(local, mesh=mesh, in_specs=in_specs, out_specs=out_specs, check_vma=False)
```

```python
import functools

import jax
import jax.numpy as jnp
from jax import lax
from jax.experimental import pallas as pl
from jax.experimental.pallas import tpu as pltpu
from jax.sharding import PartitionSpec as P


LANES = 128
F32 = jnp.float32
BF16 = jnp.bfloat16
VMEM = pl.BlockSpec(memory_space=pltpu.VMEM)
HBM = pl.BlockSpec(memory_space=pltpu.HBM)
SMEM = pl.BlockSpec(memory_space=pltpu.SMEM)


def call(body, outs, in_specs, scratch, flops, *args):
    size = sum(a.size * a.dtype.itemsize for a in args)
    size += sum(o.size * o.dtype.itemsize for o in outs)
    return pl.pallas_call(
        body,
        out_shape=tuple(outs),
        in_specs=in_specs,
        out_specs=tuple(HBM if scratch and i == 1 and len(scratch) == 2 else VMEM for i in range(len(outs))),
        scratch_shapes=scratch,
        compiler_params=pltpu.CompilerParams(vmem_limit_bytes=8 * 1024 * 1024),
        cost_estimate=pl.CostEstimate(flops=flops, bytes_accessed=size, transcendentals=0),
    )(*args)


def pack(ref, lead, block, value):
    rc = value.shape[0] // block[0]
    for o in range(block[0]):
        for j in range(value.shape[1] // LANES):
            ref[lead + (o, slice(j * rc, (j + 1) * rc))] = value[
                o * rc : (o + 1) * rc, j * LANES : (j + 1) * LANES
            ]


def unpack(value):
    chunks, cw, _ = value.shape
    groups = int((cw * chunks // LANES) ** 0.5)
    rc = cw // groups
    return jnp.concatenate(
        [
            jnp.concatenate([value[o, j * rc : (j + 1) * rc] for j in range(groups)], axis=1)
            for o in range(chunks)
        ],
        axis=0,
    )


def halves(value):
    high = value.astype(BF16)
    low = (value - high.astype(F32)).astype(BF16)
    return high, low


def dot(a, b):
    return jnp.dot(a, b, preferred_element_type=F32)


def three(ah, al, bh, bl):
    return dot(
        jnp.concatenate([ah, ah, al], axis=1), jnp.concatenate([bh, bl, bh], axis=0)
    )


def mask(size, side):
    rows = lax.broadcasted_iota(jnp.int32, (side, side), 0)
    cols = lax.broadcasted_iota(jnp.int32, (side, side), 1)
    return (rows < size) & (cols < size)


def pick(slot, blocks):
    value = jnp.zeros(blocks[0].shape, F32)
    for k, block in enumerate(blocks):
        value = jnp.where(slot == float(k), block[...], value)
    return unpack(value)


def fold(mixed, rcat_ref):
    total = None
    for p, one in enumerate(mixed):
        high, low = halves(one)
        term = three(high, low, rcat_ref[p, 0], rcat_ref[p, 1])
        total = term if total is None else total + term
    return total


def rows(value):
    return jnp.sum(value.reshape(-1, LANES), axis=0, keepdims=True)


def tile(parts):
    parts = parts + [jnp.zeros((8 - len(parts), LANES), F32)]
    return jnp.concatenate(parts, axis=0)


def half_angle(middle, first, last):
    gap = last - first
    tilt = -2.0 * middle
    length = jnp.sqrt(gap * gap + tilt * tilt)
    safe = jnp.where(length > 0.0, length, 1.0)
    big = jnp.where(length > 0.0, jnp.sqrt(0.5 + 0.5 * jnp.abs(gap) / safe), 1.0)
    small = 0.5 * tilt / (safe * big)
    sign = jnp.where(tilt > 0.0, 1.0, -1.0)
    cosine = jnp.where(gap >= 0.0, big, jnp.abs(small))
    sine = jnp.where(gap >= 0.0, small, sign * big)
    return cosine, sine, 0.5 * (first + last) - 0.5 * length


def update(xx, first, xr, rr, rh, xhr, rhr):
    n = lax.rsqrt(rr - 2.0 * xr * xr + xr * xr * xx + 1e-06)
    middle = 0.5 * n * ((xhr - xr * first) + (rh - xr * first))
    last = n * n * (rhr - xr * rh - xr * xhr + xr * xr * first)
    cosine, sine, theta = half_angle(middle, first, last)
    on_r = sine * n
    on_x = cosine - on_r * xr
    xx = on_x * on_x * xx + 2.0 * on_x * on_r * xr + on_r * on_r * rr
    return on_x, on_r, theta, xx


def start_body(size_ref, psi_ref, x_ref):
    live = mask(size_ref[0], psi_ref.shape[1])
    pack(x_ref, (), x_ref.shape, jnp.where(live, psi_ref[0].astype(F32), 0.0))


def split_body(
    label_ref, couple_ref, left_ref, right_ref, lcat_ref, rcat_ref, flag_ref, slot_ref
):
    here = lax.axis_index("sec")
    for p in range(left_ref.shape[0]):
        lcat_ref[p, 0], lcat_ref[p, 1] = halves(left_ref[p, 0])
        rcat_ref[p, 0], rcat_ref[p, 1] = halves(right_ref[p, 0].T)
        source = couple_ref[p]
        near = here + 1 - 2 * (here % 2)
        slot = jnp.where(source == here, 0.0, jnp.where(source == near, 1.0, 2.0))
        slot_ref[p] = jnp.full(slot_ref.shape[1:], jnp.where(source >= 0, slot, -1.0))
    flag_ref[...] = jnp.full(flag_ref.shape, jnp.where(label_ref[0] == here, 1.0, 0.0))


def mix_all(slot_ref, blocks, lcat_ref):
    mixed = []
    for p in range(lcat_ref.shape[0]):
        high, low = halves(pick(slot_ref[p, 0:1, 0:1][None], blocks))
        mixed.append(three(lcat_ref[p, 0], lcat_ref[p, 1], high, low))
    return mixed


def save(mixed, room_ref, m_ref, sem):
    copies = []
    for p, one in enumerate(mixed):
        room_ref[p] = one
        copies.append(pltpu.make_async_copy(room_ref.at[p], m_ref.at[p], sem.at[p]))
        copies[-1].start()
    return copies


def fold_all(size_ref, mixed, rcat_ref, y_ref):
    y = fold(mixed, rcat_ref)
    pack(y_ref, (), y_ref.shape, jnp.where(mask(size_ref[0], y.shape[0]), y, 0.0))
    return y_ref[...]


def first_body(
    size_ref, slot_ref, x0, x1, x2, lcat_ref, rcat_ref, y_ref, m_ref, part_ref, room_ref, sem
):
    mixed = mix_all(slot_ref, (x0, x1, x2), lcat_ref)
    copies = save(mixed, room_ref, m_ref, sem)
    y = fold_all(size_ref, mixed, rcat_ref, y_ref)
    x = x0[lax.axis_index("ops")]
    part_ref[...] = tile([rows(x * x), rows(x0[...] * y)])
    for copy in copies:
        copy.wait()


def five(x0, r0, h0, y):
    o = lax.axis_index("ops")
    x, r, h = x0[o], r0[o], h0[o][: x0.shape[1]]
    return tile([rows(x * r), rows(r * r), rows(r * h), rows(x0[...] * y), rows(r0[...] * y)])


def second_body(
    size_ref, slot_ref, r0, r1, r2, x0, g0, lcat_ref, rcat_ref,
    y_ref, m_ref, part_ref, room_ref, sem,
):
    mixed = mix_all(slot_ref, (r0, r1, r2), lcat_ref)
    copies = save(mixed, room_ref, m_ref, sem)
    part_ref[...] = five(x0, r0, g0, fold_all(size_ref, mixed, rcat_ref, y_ref))
    for copy in copies:
        copy.wait()


def mix_body(slot_ref, r0, r1, r2, lcat_ref, m_ref):
    for p, one in enumerate(mix_all(slot_ref, (r0, r1, r2), lcat_ref)):
        m_ref[p] = one


def fold_body(size_ref, m_ref, r0, x0, h0, rcat_ref, part_ref, y_ref):
    mixed = [m_ref[p] for p in range(m_ref.shape[0])]
    part_ref[...] = five(x0, r0, h0, fold_all(size_ref, mixed, rcat_ref, y_ref))


def blend_body(c_in, a_ref, b_ref, x_ref, out_ref):
    pairs = a_ref.shape[0]
    out_ref[:pairs] = c_in[2:3, 0:1] * a_ref[...] + c_in[3:4, 0:1] * b_ref[...]
    out_ref[pairs] = unpack(x_ref[...])


def cross_body(flag_ref, b_ref, n_ref, m_ref, w_ref, s0, s1, u_ref):
    stay = flag_ref[0:1, 0:1] > 0.5
    pairs, side, _ = m_ref.shape
    new = unpack(jnp.where(stay[None], s0[...], s1[...]))
    x = jnp.where(stay, b_ref[pairs], n_ref[pairs])
    left = jnp.concatenate([x.T, new.T], axis=0)
    lh, ll = halves(left)
    for p in range(pairs):
        old, new = jnp.where(stay, b_ref[p], n_ref[p]), jnp.where(stay, m_ref[p], w_ref[p])
        rh, rl = halves(jnp.concatenate([old, new], axis=1))
        both = three(lh, ll, rh, rl)
        u_ref[0, p] = both[:side, :side]
        u_ref[1, p] = both[:side, side:] + both[side:, :side]
        u_ref[2, p] = both[side:, side:]


def sum_body(terms_ref, mine, *refs):
    others, out_ref = refs[:-1], refs[-1]
    cw = terms_ref.shape[1]
    block = jnp.sum(terms_ref[...], axis=0)
    scalars = mine[...]
    for one in others:
        scalars = scalars + one[...]
    for o in range(out_ref.shape[0]):
        out_ref[o, :cw] = block
        out_ref[o, cw:] = scalars


def numbers(tiles, count):
    total = jnp.sum(jnp.sum(tiles, axis=0), axis=1, keepdims=True)
    return [total[i : i + 1] for i in range(count)]


def store(out_ref, values):
    out_ref[...] = tile([jnp.broadcast_to(v, (1, LANES)) for v in values])


def first_residual_body(g_ref, x_ref, diag_ref, r_ref, c_ref, d_ref):
    pack(d_ref, (), d_ref.shape, diag_ref[0].astype(F32))
    cw = x_ref.shape[1]
    squares, energy = numbers(g_ref[:, cw:], 2)
    factor = lax.rsqrt(squares + 1e-06)
    theta = energy * factor * factor
    r = factor * (g_ref[:, :cw] - theta * x_ref[...]) / (jnp.abs(d_ref[...] - theta) + 1.0)
    r_ref[...] = r
    store(c_ref, [factor, theta, squares * factor * factor])


def second_residual_body(
    s_ref, g_ref, x_ref, diag_ref, r_in, c_in, x_out, h_out, r_ref, c_ref, d_ref
):
    pack(d_ref, (), d_ref.shape, diag_ref[0].astype(F32))
    cw = x_ref.shape[1]
    xr, rr, rh, xhr, rhr = numbers(s_ref[:, cw:], 5)
    factor, first, xx = c_in[0:1, 0:1], c_in[1:2, 0:1], c_in[2:3, 0:1]
    on_x, on_r, theta, xx = update(
        xx, first, factor * xr, rr, factor * rh, factor * xhr, rhr
    )
    on_x = on_x * factor
    x = on_x * x_ref[...] + on_r * r_in[...]
    h = on_x * g_ref[:, :cw] + on_r * s_ref[:, :cw]
    x_out[...] = x
    h_out[...] = h
    r_ref[...] = (h - theta * x) / (jnp.abs(d_ref[...] - theta) + 1.0)
    store(c_ref, [theta, xx, on_x, on_r])


def last_body(scale, parts_ref, c_in, b_ref, s0, u_ref, wave_ref, turn_ref):
    pairs, side = u_ref.shape[1:3]
    xr, rr, rh, xhr, rhr = numbers(parts_ref[...], 5)
    on_x, on_s, _, _ = update(c_in[1:2, 0:1], c_in[0:1, 0:1], xr, rr, rh, xhr, rhr)
    on_x = on_x * scale
    on_s = on_s * scale
    wave_ref[0] = on_x * b_ref[pairs] + unpack(on_s * s0[...])
    root = 1.0 / side**0.5
    xx, xs, ss = on_x * on_x * root, on_x * on_s * root, on_s * on_s * root
    for p in range(pairs):
        turn_ref[p, 0] = xx * u_ref[0, p] + xs * u_ref[1, p] + ss * u_ref[2, p]


def paired(value):
    count = lax.axis_size("sec")
    return lax.ppermute(value, "sec", [(i, i ^ 1) for i in range(count)])


def other(value):
    count, groups = lax.axis_size("sec"), lax.axis_size("ops")
    route = []
    for o in range(groups):
        for i in range(1, count - 1, 2):
            route += [(o * count + i, o * count + i + 1), (o * count + i + 1, o * count + i)]
        if groups % 2 == 0:
            route += [(o * count + i, (o ^ 1) * count + i) for i in (0, count - 1)]
    return lax.ppermute(value, ("ops", "sec"), route)


def over_sectors(value):
    count = lax.axis_size("sec")
    found = []
    for d in range(1, count):
        found.append(lax.ppermute(value, "sec", [(i, i ^ d) for i in range(count)]))
    return found


def exchange(value):
    return lax.all_to_all(value, "ops", 0, 0)


def local(sector_states, psi_guess, precond_diag, left_ops, right_ops, couple, new_sector):
    side = psi_guess.shape[1]
    pairs = left_ops.shape[0]
    couple = couple.reshape(pairs)
    chunks = lax.axis_size("ops")
    sectors = lax.axis_size("sec")
    cw = side // chunks * side // LANES
    block = jax.ShapeDtypeStruct((chunks, cw, LANES), F32)
    wide = jax.ShapeDtypeStruct((chunks, cw + 8, LANES), F32)
    small = jax.ShapeDtypeStruct((8, LANES), F32)
    inner = jax.ShapeDtypeStruct((pairs, side, side), F32)
    kept = [pltpu.VMEM(inner.shape, F32), pltpu.SemaphoreType.DMA((pairs,))]
    work = 12 * pairs * side**3
    light = 20 * side**2

    def gathered(y, part):
        others = over_sectors(part)
        (full,) = call(
            sum_body, (wide,), [VMEM] * (2 + len(others)), [], light,
            exchange(y), part, *others,
        )
        return exchange(full)

    (x0,) = call(start_body, (block,), [SMEM, VMEM], [], light, sector_states, psi_guess)
    x2, x1 = other(x0), paired(x0)
    lcat, rcat, flag, slots = call(
        split_body,
        (
            jax.ShapeDtypeStruct((pairs, 2, side, side), BF16),
            jax.ShapeDtypeStruct((pairs, 2, side, side), BF16),
            small,
            jax.ShapeDtypeStruct((pairs, 8, LANES), F32),
        ),
        [SMEM] * 2 + [VMEM] * 2, [], light * pairs, new_sector, couple, left_ops, right_ops,
    )
    y, mx, part = call(
        first_body, (block, inner, small), [SMEM] + [VMEM] * 6, kept, work,
        sector_states, slots, x0, x1, x2, lcat, rcat,
    )
    g = gathered(y, part)
    r0, c = call(
        first_residual_body, (block, small), [VMEM] * 3, [pltpu.VMEM(block.shape, F32)], light,
        g, x0, precond_diag,
    )
    r2, r1 = other(r0), paired(r0)
    y, mr, part = call(
        second_body, (block, inner, small), [SMEM] + [VMEM] * 8, kept, work,
        sector_states, slots, r0, r1, r2, x0, g, lcat, rcat,
    )
    s = gathered(y, part)
    x, h, s0, c = call(
        second_residual_body, (block, block, block, small), [VMEM] * 6,
        [pltpu.VMEM(block.shape, F32)], light, s, g, x0, precond_diag, r0, c,
    )
    s2, s1 = other(s0), paired(s0)
    (mx,) = call(
        blend_body, (jax.ShapeDtypeStruct((pairs + 1, side, side), F32),), [VMEM] * 4, [],
        light, c, mx, mr, x,
    )
    nx = paired(mx)
    (ms,) = call(
        mix_body, (inner,), [VMEM] * 5, [], work // 2,
        slots, s0, s1, s2, lcat,
    )
    ns = paired(ms)
    (part,) = call(
        fold_body, (small,), [SMEM] + [VMEM] * 5, [pltpu.VMEM(block.shape, F32)], work // 2,
        sector_states, ms, s0, x, h, rcat,
    )
    count = chunks * sectors
    parts = lax.all_to_all(jnp.broadcast_to(part[None], (count, 8, LANES)), ("ops", "sec"), 0, 0)
    (u,) = call(
        cross_body, (jax.ShapeDtypeStruct((3, pairs, side, side), F32),), [VMEM] * 7,
        [], work, flag, mx, nx, ms, ns, s0, s1,
    )
    return call(
        functools.partial(last_body, float((sectors * side * side) ** 0.5)),
        (
            jax.ShapeDtypeStruct((1, side, side), F32),
            jax.ShapeDtypeStruct((pairs, 1, side, side), F32),
        ),
        [VMEM] * 5, [], light, parts, c, mx, s0, u,
    )


def solution(mesh):
    in_specs = (
        P("sec"),
        P("sec", None, None),
        P("sec", None, None),
        P("ops", "sec", None, None),
        P("ops", "sec", None, None),
        P("ops", "sec"),
        P("sec"),
    )
    out_specs = (P("sec", None, None), P("ops", "sec", None, None))
    return jax.shard_map(local, mesh=mesh, in_specs=in_specs, out_specs=out_specs, check_vma=False)
```

```python
import functools

import jax
import jax.numpy as jnp
from jax import lax
from jax.experimental import pallas as pl
from jax.experimental.pallas import tpu as pltpu
from jax.sharding import PartitionSpec as P


LANES = 128
F32 = jnp.float32
BF16 = jnp.bfloat16
VMEM = pl.BlockSpec(memory_space=pltpu.VMEM)
ANY = pl.BlockSpec(memory_space=pl.ANY)
SMEM = pl.BlockSpec(memory_space=pltpu.SMEM)


def call(body, outs, in_specs, scratch, flops, *args, limit=8):
    size = sum(a.size * a.dtype.itemsize for a in args)
    size += sum(o.size * o.dtype.itemsize for o in outs)
    return pl.pallas_call(
        body,
        out_shape=tuple(outs),
        in_specs=in_specs,
        out_specs=tuple(VMEM for _ in outs),
        scratch_shapes=scratch,
        compiler_params=pltpu.CompilerParams(vmem_limit_bytes=int(limit * 1024 * 1024)),
        cost_estimate=pl.CostEstimate(flops=flops, bytes_accessed=size, transcendentals=0),
    )(*args)


def pack(ref, lead, block, value):
    rc = value.shape[0] // block[0]
    for o in range(block[0]):
        for j in range(value.shape[1] // LANES):
            ref[lead + (o, slice(j * rc, (j + 1) * rc))] = value[
                o * rc : (o + 1) * rc, j * LANES : (j + 1) * LANES
            ]


def unpack(value):
    chunks, cw, _ = value.shape
    groups = int((cw * chunks // LANES) ** 0.5)
    rc = cw // groups
    return jnp.concatenate(
        [
            jnp.concatenate([value[o, j * rc : (j + 1) * rc] for j in range(groups)], axis=1)
            for o in range(chunks)
        ],
        axis=0,
    )


def halves(value):
    high = value.astype(BF16)
    low = (value - high.astype(F32)).astype(BF16)
    return high, low


def dot(a, b):
    return jnp.dot(a, b, preferred_element_type=F32)


def three(ah, al, bh, bl):
    return dot(
        jnp.concatenate([ah, ah, al], axis=1), jnp.concatenate([bh, bl, bh], axis=0)
    )


def mask(size, side):
    rows = lax.broadcasted_iota(jnp.int32, (side, side), 0)
    cols = lax.broadcasted_iota(jnp.int32, (side, side), 1)
    return (rows < size) & (cols < size)


def pick(slot, blocks):
    value = jnp.zeros(blocks[0].shape, F32)
    for k, block in enumerate(blocks):
        value = jnp.where(slot == float(k), block[...], value)
    return unpack(value)


def fold(mixed, rcat_ref):
    total = None
    for p, one in enumerate(mixed):
        high, low = halves(one)
        term = three(high, low, rcat_ref[p, 0], rcat_ref[p, 1])
        total = term if total is None else total + term
    return total


def rows(value):
    return jnp.sum(value.reshape(-1, LANES), axis=0, keepdims=True)


def tile(parts):
    parts = parts + [jnp.zeros((8 - len(parts), LANES), F32)]
    return jnp.concatenate(parts, axis=0)


def half_angle(middle, first, last):
    gap = last - first
    tilt = -2.0 * middle
    length = jnp.sqrt(gap * gap + tilt * tilt)
    safe = jnp.where(length > 0.0, length, 1.0)
    big = jnp.where(length > 0.0, jnp.sqrt(0.5 + 0.5 * jnp.abs(gap) / safe), 1.0)
    small = 0.5 * tilt / (safe * big)
    sign = jnp.where(tilt > 0.0, 1.0, -1.0)
    cosine = jnp.where(gap >= 0.0, big, jnp.abs(small))
    sine = jnp.where(gap >= 0.0, small, sign * big)
    return cosine, sine, 0.5 * (first + last) - 0.5 * length


def update(xx, first, xr, rr, rh, xhr, rhr):
    n = lax.rsqrt(rr - 2.0 * xr * xr + xr * xr * xx + 1e-06)
    middle = 0.5 * n * ((xhr - xr * first) + (rh - xr * first))
    last = n * n * (rhr - xr * rh - xr * xhr + xr * xr * first)
    cosine, sine, theta = half_angle(middle, first, last)
    on_r = sine * n
    on_x = cosine - on_r * xr
    xx = on_x * on_x * xx + 2.0 * on_x * on_r * xr + on_r * on_r * rr
    return on_x, on_r, theta, xx


def start_body(size_ref, psi_ref, x_ref):
    live = mask(size_ref[0], psi_ref.shape[1])
    pack(x_ref, (), x_ref.shape, jnp.where(live, psi_ref[0].astype(F32), 0.0))


def split_pairs(left_ref, right_ref, lcat_ref, rcat_ref, left, right, sem):
    pairs = lcat_ref.shape[0]
    copies = []
    for p in range(pairs):
        copies.append(pltpu.make_async_copy(left_ref.at[p, 0], left.at[p], sem.at[2 * p]))
        copies.append(pltpu.make_async_copy(right_ref.at[p, 0], right.at[p], sem.at[2 * p + 1]))
    for copy in copies:
        copy.start()
    for p in range(pairs):
        copies[2 * p].wait()
        lcat_ref[p, 0], lcat_ref[p, 1] = halves(left[p])
        copies[2 * p + 1].wait()
        rcat_ref[p, 0], rcat_ref[p, 1] = halves(right[p].T)


def split_body(
    label_ref, couple_hbm, left_ref, right_ref, lcat_ref, rcat_ref, flag_ref, slot_ref,
    left, right, sem, couple_ref, mark,
):
    here = lax.axis_index("sec")
    copy = pltpu.make_async_copy(couple_hbm, couple_ref, mark)
    copy.start()
    split_pairs(left_ref, right_ref, lcat_ref, rcat_ref, left, right, sem)
    copy.wait()
    for p in range(lcat_ref.shape[0]):
        source = couple_ref[p]
        near = here + 1 - 2 * (here % 2)
        slot = jnp.where(source == here, 0.0, jnp.where(source == near, 1.0, 2.0))
        slot_ref[p] = jnp.full(slot_ref.shape[1:], jnp.where(source >= 0, slot, -1.0))
    flag_ref[...] = jnp.full(flag_ref.shape, jnp.where(label_ref[0] == here, 1.0, 0.0))


def mix_all(slot_ref, blocks, lcat_ref, m_ref):
    mixed = []
    for p in range(lcat_ref.shape[0]):
        high, low = halves(pick(slot_ref[p, 0:1, 0:1][None], blocks))
        mixed.append(three(lcat_ref[p, 0], lcat_ref[p, 1], high, low))
        m_ref[p] = mixed[p]
    return mixed


def fold_all(size_ref, mixed, rcat_ref, y_ref):
    y = fold(mixed, rcat_ref)
    pack(y_ref, (), y_ref.shape, jnp.where(mask(size_ref[0], y.shape[0]), y, 0.0))
    return y_ref[...]


def first_body(size_ref, slot_ref, x0, x1, x2, lcat_ref, rcat_ref, y_ref, m_ref, part_ref):
    mixed = mix_all(slot_ref, (x0, x1, x2), lcat_ref, m_ref)
    y = fold_all(size_ref, mixed, rcat_ref, y_ref)
    x = x0[lax.axis_index("ops")]
    part_ref[...] = tile([rows(x * x), rows(x0[...] * y)])


def five(x0, r0, h0, y):
    o = lax.axis_index("ops")
    x, r, h = x0[o], r0[o], h0[o][: x0.shape[1]]
    return tile([rows(x * r), rows(r * r), rows(r * h), rows(x0[...] * y), rows(r0[...] * y)])


def second_body(
    size_ref, slot_ref, r0, r1, r2, x0, g0, lcat_ref, rcat_ref, y_ref, m_ref, part_ref
):
    mixed = mix_all(slot_ref, (r0, r1, r2), lcat_ref, m_ref)
    part_ref[...] = five(x0, r0, g0, fold_all(size_ref, mixed, rcat_ref, y_ref))


def mix_body(slot_ref, r0, r1, r2, lcat_ref, m_ref):
    mix_all(slot_ref, (r0, r1, r2), lcat_ref, m_ref)


def fold_body(size_ref, m_ref, r0, x0, h0, rcat_ref, part_ref, y_ref):
    mixed = [m_ref[p] for p in range(m_ref.shape[0])]
    part = five(x0, r0, h0, fold_all(size_ref, mixed, rcat_ref, y_ref))
    part_ref[...] = jnp.broadcast_to(part[None], part_ref.shape)


def blend_body(c_in, a_ref, b_ref, x_ref, out_ref):
    pairs = a_ref.shape[0]
    out_ref[:pairs] = c_in[2:3, 0:1] * a_ref[...] + c_in[3:4, 0:1] * b_ref[...]
    out_ref[pairs] = unpack(x_ref[...])


def cross_body(flag_ref, b_ref, n_ref, m_ref, w_ref, s0, s1, u_ref):
    stay = flag_ref[0:1, 0:1] > 0.5
    pairs, side, _ = m_ref.shape
    new = unpack(jnp.where(stay[None], s0[...], s1[...]))
    x = jnp.where(stay, b_ref[pairs], n_ref[pairs])
    left = jnp.concatenate([x.T, new.T], axis=0)
    lh, ll = halves(left)
    for p in range(pairs):
        old, new = jnp.where(stay, b_ref[p], n_ref[p]), jnp.where(stay, m_ref[p], w_ref[p])
        rh, rl = halves(jnp.concatenate([old, new], axis=1))
        both = three(lh, ll, rh, rl)
        u_ref[0, p] = both[:side, :side]
        u_ref[1, p] = both[:side, side:] + both[side:, :side]
        u_ref[2, p] = both[side:, side:]


def sum_body(terms_ref, mine, *refs):
    others, out_ref = refs[:-1], refs[-1]
    cw = terms_ref.shape[1]
    block = jnp.sum(terms_ref[...], axis=0)
    scalars = mine[...]
    for one in others:
        scalars = scalars + one[...]
    for o in range(out_ref.shape[0]):
        out_ref[o, :cw] = block
        out_ref[o, cw:] = scalars


def numbers(tiles, count):
    total = jnp.sum(jnp.sum(tiles, axis=0), axis=1, keepdims=True)
    return [total[i : i + 1] for i in range(count)]


def store(out_ref, values):
    out_ref[...] = tile([jnp.broadcast_to(v, (1, LANES)) for v in values])


def first_residual_body(g_ref, x_ref, diag_ref, r_ref, c_ref, d_ref):
    pack(d_ref, (), d_ref.shape, diag_ref[0].astype(F32))
    cw = x_ref.shape[1]
    squares, energy = numbers(g_ref[:, cw:], 2)
    factor = lax.rsqrt(squares + 1e-06)
    theta = energy * factor * factor
    r = factor * (g_ref[:, :cw] - theta * x_ref[...]) / (jnp.abs(d_ref[...] - theta) + 1.0)
    r_ref[...] = r
    store(c_ref, [factor, theta, squares * factor * factor])


def second_residual_body(
    s_ref, g_ref, x_ref, diag_ref, r_in, c_in, x_out, h_out, r_ref, c_ref, d_ref
):
    pack(d_ref, (), d_ref.shape, diag_ref[0].astype(F32))
    cw = x_ref.shape[1]
    xr, rr, rh, xhr, rhr = numbers(s_ref[:, cw:], 5)
    factor, first, xx = c_in[0:1, 0:1], c_in[1:2, 0:1], c_in[2:3, 0:1]
    on_x, on_r, theta, xx = update(
        xx, first, factor * xr, rr, factor * rh, factor * xhr, rhr
    )
    on_x = on_x * factor
    x = on_x * x_ref[...] + on_r * r_in[...]
    h = on_x * g_ref[:, :cw] + on_r * s_ref[:, :cw]
    x_out[...] = x
    h_out[...] = h
    r_ref[...] = (h - theta * x) / (jnp.abs(d_ref[...] - theta) + 1.0)
    store(c_ref, [theta, xx, on_x, on_r])


def last_body(scale, parts_ref, c_in, b_ref, s0, u_ref, wave_ref, turn_ref):
    pairs, side = u_ref.shape[1:3]
    xr, rr, rh, xhr, rhr = numbers(parts_ref[...], 5)
    on_x, on_s, _, _ = update(c_in[1:2, 0:1], c_in[0:1, 0:1], xr, rr, rh, xhr, rhr)
    on_x = on_x * scale
    on_s = on_s * scale
    wave_ref[0] = on_x * b_ref[pairs] + unpack(on_s * s0[...])
    root = 1.0 / side**0.5
    xx, xs, ss = on_x * on_x * root, on_x * on_s * root, on_s * on_s * root
    for p in range(pairs):
        turn_ref[p, 0] = xx * u_ref[0, p] + xs * u_ref[1, p] + ss * u_ref[2, p]


def paired(value):
    count = lax.axis_size("sec")
    return lax.ppermute(value, "sec", [(i, i ^ 1) for i in range(count)])


def other(value):
    count, groups = lax.axis_size("sec"), lax.axis_size("ops")
    route = []
    for o in range(groups):
        for i in range(1, count - 1, 2):
            route += [(o * count + i, o * count + i + 1), (o * count + i + 1, o * count + i)]
        if groups % 2 == 0:
            route += [(o * count + i, (o ^ 1) * count + i) for i in (0, count - 1)]
    return lax.ppermute(value, ("ops", "sec"), route)


def over_sectors(value):
    count = lax.axis_size("sec")
    found = []
    for d in range(1, count):
        found.append(lax.ppermute(value, "sec", [(i, i ^ d) for i in range(count)]))
    return found


def exchange(value):
    return lax.all_to_all(value, "ops", 0, 0)


def local(sector_states, psi_guess, precond_diag, left_ops, right_ops, couple, new_sector):
    side = psi_guess.shape[1]
    pairs = left_ops.shape[0]
    couple = couple.reshape(pairs)
    chunks = lax.axis_size("ops")
    sectors = lax.axis_size("sec")
    cw = side // chunks * side // LANES
    block = jax.ShapeDtypeStruct((chunks, cw, LANES), F32)
    wide = jax.ShapeDtypeStruct((chunks, cw + 8, LANES), F32)
    small = jax.ShapeDtypeStruct((8, LANES), F32)
    inner = jax.ShapeDtypeStruct((pairs, side, side), F32)
    pieces = jax.ShapeDtypeStruct((pairs, 2, side, side), BF16)
    loads = [pltpu.VMEM((pairs, side, side), F32)] * 2 + [pltpu.SemaphoreType.DMA((2 * pairs,))]
    work = 12 * pairs * side**3
    light = 20 * side**2

    def gathered(y, part):
        others = over_sectors(part)
        (full,) = call(
            sum_body, (wide,), [VMEM] * (2 + len(others)), [], light,
            exchange(y), part, *others,
        )
        return exchange(full)

    (x0,) = call(start_body, (block,), [SMEM, VMEM], [], light, sector_states, psi_guess)
    x2, x1 = other(x0), paired(x0)
    lcat, rcat, flag, slots = call(
        split_body, (pieces, pieces, small, jax.ShapeDtypeStruct((pairs, 8, LANES), F32)),
        [SMEM] + [ANY] * 3,
        loads + [pltpu.SMEM((pairs,), jnp.int32), pltpu.SemaphoreType.DMA(())],
        light * pairs, new_sector, couple, left_ops, right_ops, limit=52.5,
    )
    y, mx, part = call(
        first_body, (block, inner, small), [SMEM] + [VMEM] * 6, [], work,
        sector_states, slots, x0, x1, x2, lcat, rcat,
    )
    g = gathered(y, part)
    r0, c = call(
        first_residual_body, (block, small), [VMEM] * 3, [pltpu.VMEM(block.shape, F32)], light,
        g, x0, precond_diag,
    )
    r2, r1 = other(r0), paired(r0)
    y, mr, part = call(
        second_body, (block, inner, small), [SMEM] + [VMEM] * 8, [], work,
        sector_states, slots, r0, r1, r2, x0, g, lcat, rcat,
    )
    s = gathered(y, part)
    x, h, s0, c = call(
        second_residual_body, (block, block, block, small), [VMEM] * 6,
        [pltpu.VMEM(block.shape, F32)], light, s, g, x0, precond_diag, r0, c,
    )
    s2, s1 = other(s0), paired(s0)
    (mx,) = call(
        blend_body, (jax.ShapeDtypeStruct((pairs + 1, side, side), F32),), [VMEM] * 4, [],
        light, c, mx, mr, x,
    )
    nx = paired(mx)
    (ms,) = call(
        mix_body, (inner,), [VMEM] * 5, [], work // 2,
        slots, s0, s1, s2, lcat,
    )
    ns = paired(ms)
    many = jax.ShapeDtypeStruct((chunks * sectors, 8, LANES), F32)
    (part,) = call(
        fold_body, (many,), [SMEM] + [VMEM] * 5, [pltpu.VMEM(block.shape, F32)], work // 2,
        sector_states, ms, s0, x, h, rcat,
    )
    parts = lax.all_to_all(part, ("ops", "sec"), 0, 0)
    (u,) = call(
        cross_body, (jax.ShapeDtypeStruct((3, pairs, side, side), F32),), [VMEM] * 7,
        [], work, flag, mx, nx, ms, ns, s0, s1,
    )
    return call(
        functools.partial(last_body, float((sectors * side * side) ** 0.5)),
        (
            jax.ShapeDtypeStruct((1, side, side), F32),
            jax.ShapeDtypeStruct((pairs, 1, side, side), F32),
        ),
        [VMEM] * 5, [], light, parts, c, mx, s0, u,
    )


def solution(mesh):
    in_specs = (
        P("sec"),
        P("sec", None, None),
        P("sec", None, None),
        P("ops", "sec", None, None),
        P("ops", "sec", None, None),
        P("ops", "sec"),
        P("sec"),
    )
    out_specs = (P("sec", None, None), P("ops", "sec", None, None))
    return jax.shard_map(local, mesh=mesh, in_specs=in_specs, out_specs=out_specs, check_vma=False)
```

```python
import functools

import jax
import jax.numpy as jnp
from jax import lax
from jax.experimental import pallas as pl
from jax.experimental.pallas import tpu as pltpu
from jax.sharding import PartitionSpec as P


LANES = 128
F32 = jnp.float32
BF16 = jnp.bfloat16
VMEM = pl.BlockSpec(memory_space=pltpu.VMEM)
ANY = pl.BlockSpec(memory_space=pl.ANY)
SMEM = pl.BlockSpec(memory_space=pltpu.SMEM)


def call(body, outs, in_specs, scratch, flops, *args, limit=8):
    size = sum(a.size * a.dtype.itemsize for a in args)
    size += sum(o.size * o.dtype.itemsize for o in outs)
    return pl.pallas_call(
        body,
        out_shape=tuple(outs),
        in_specs=in_specs,
        out_specs=tuple(VMEM for _ in outs),
        scratch_shapes=scratch,
        compiler_params=pltpu.CompilerParams(vmem_limit_bytes=int(limit * 1024 * 1024)),
        cost_estimate=pl.CostEstimate(flops=flops, bytes_accessed=size, transcendentals=0),
    )(*args)


def pack(ref, lead, block, value):
    rc = value.shape[0] // block[0]
    for o in range(block[0]):
        for j in range(value.shape[1] // LANES):
            ref[lead + (o, slice(j * rc, (j + 1) * rc))] = value[
                o * rc : (o + 1) * rc, j * LANES : (j + 1) * LANES
            ]


def unpack(value):
    chunks, cw, _ = value.shape
    groups = int((cw * chunks // LANES) ** 0.5)
    rc = cw // groups
    return jnp.concatenate(
        [
            jnp.concatenate([value[o, j * rc : (j + 1) * rc] for j in range(groups)], axis=1)
            for o in range(chunks)
        ],
        axis=0,
    )


def halves(value):
    high = value.astype(BF16)
    low = (value - high.astype(F32)).astype(BF16)
    return high, low


def dot(a, b):
    return jnp.dot(a, b, preferred_element_type=F32)


def three(ah, al, bh, bl):
    return dot(
        jnp.concatenate([ah, ah, al], axis=1), jnp.concatenate([bh, bl, bh], axis=0)
    )


def mask(size, side):
    rows = lax.broadcasted_iota(jnp.int32, (side, side), 0)
    cols = lax.broadcasted_iota(jnp.int32, (side, side), 1)
    return (rows < size) & (cols < size)


def pick(slot, blocks):
    value = jnp.zeros(blocks[0].shape, F32)
    for k, block in enumerate(blocks):
        value = jnp.where(slot == float(k), block[...], value)
    return unpack(value)


def fold(mixed, rcat_ref):
    total = None
    for p, one in enumerate(mixed):
        high, low = halves(one)
        term = three(high, low, rcat_ref[p, 0], rcat_ref[p, 1])
        total = term if total is None else total + term
    return total


def rows(value):
    return jnp.sum(value.reshape(-1, LANES), axis=0, keepdims=True)


def tile(parts):
    parts = parts + [jnp.zeros((8 - len(parts), LANES), F32)]
    return jnp.concatenate(parts, axis=0)


def half_angle(middle, first, last):
    gap = last - first
    tilt = -2.0 * middle
    length = jnp.sqrt(gap * gap + tilt * tilt)
    safe = jnp.where(length > 0.0, length, 1.0)
    big = jnp.where(length > 0.0, jnp.sqrt(0.5 + 0.5 * jnp.abs(gap) / safe), 1.0)
    small = 0.5 * tilt / (safe * big)
    sign = jnp.where(tilt > 0.0, 1.0, -1.0)
    cosine = jnp.where(gap >= 0.0, big, jnp.abs(small))
    sine = jnp.where(gap >= 0.0, small, sign * big)
    return cosine, sine, 0.5 * (first + last) - 0.5 * length


def update(xx, first, xr, rr, rh, xhr, rhr):
    n = lax.rsqrt(rr - 2.0 * xr * xr + xr * xr * xx + 1e-06)
    middle = 0.5 * n * ((xhr - xr * first) + (rh - xr * first))
    last = n * n * (rhr - xr * rh - xr * xhr + xr * xr * first)
    cosine, sine, theta = half_angle(middle, first, last)
    on_r = sine * n
    on_x = cosine - on_r * xr
    xx = on_x * on_x * xx + 2.0 * on_x * on_r * xr + on_r * on_r * rr
    return on_x, on_r, theta, xx


def start_body(size_ref, psi_ref, x_ref):
    live = mask(size_ref[0], psi_ref.shape[1])
    pack(x_ref, (), x_ref.shape, jnp.where(live, psi_ref[0].astype(F32), 0.0))


def split_pairs(left_ref, right_ref, lcat_ref, rcat_ref, left, right, sem):
    pairs = lcat_ref.shape[0]
    copies = []
    for p in range(pairs):
        copies.append(pltpu.make_async_copy(left_ref.at[p, 0], left.at[p], sem.at[2 * p]))
        copies.append(pltpu.make_async_copy(right_ref.at[p, 0], right.at[p], sem.at[2 * p + 1]))
    for copy in copies:
        copy.start()
    for p in range(pairs):
        copies[2 * p].wait()
        lcat_ref[p, 0], lcat_ref[p, 1] = halves(left[p])
        copies[2 * p + 1].wait()
        rcat_ref[p, 0], rcat_ref[p, 1] = halves(right[p].T)


def split_body(
    label_ref, couple_hbm, left_ref, right_ref, lcat_ref, rcat_ref, flag_ref, slot_ref,
    left, right, sem, couple_ref, mark,
):
    here = lax.axis_index("sec")
    copy = pltpu.make_async_copy(couple_hbm, couple_ref, mark)
    copy.start()
    split_pairs(left_ref, right_ref, lcat_ref, rcat_ref, left, right, sem)
    copy.wait()
    for p in range(lcat_ref.shape[0]):
        source = couple_ref[p]
        near = here + 1 - 2 * (here % 2)
        slot = jnp.where(source == here, 0.0, jnp.where(source == near, 1.0, 2.0))
        slot_ref[p] = jnp.full(slot_ref.shape[1:], jnp.where(source >= 0, slot, -1.0))
    flag_ref[...] = jnp.full(flag_ref.shape, jnp.where(label_ref[0] == here, 1.0, 0.0))


def mix_all(slot_ref, blocks, lcat_ref, m_ref):
    mixed = []
    for p in range(lcat_ref.shape[0]):
        high, low = halves(pick(slot_ref[p, 0:1, 0:1][None], blocks))
        mixed.append(three(lcat_ref[p, 0], lcat_ref[p, 1], high, low))
        m_ref[p] = mixed[p]
    return mixed


def fold_all(size_ref, mixed, rcat_ref, y_ref):
    y = fold(mixed, rcat_ref)
    pack(y_ref, (), y_ref.shape, jnp.where(mask(size_ref[0], y.shape[0]), y, 0.0))
    return y_ref[...]


def first_body(size_ref, slot_ref, x0, x1, x2, lcat_ref, rcat_ref, y_ref, m_ref, part_ref):
    mixed = mix_all(slot_ref, (x0, x1, x2), lcat_ref, m_ref)
    y = fold_all(size_ref, mixed, rcat_ref, y_ref)
    x = x0[lax.axis_index("ops")]
    part_ref[...] = tile([rows(x * x), rows(x0[...] * y)])


def five(x0, r0, h0, y):
    o = lax.axis_index("ops")
    x, r, h = x0[o], r0[o], h0[o][: x0.shape[1]]
    return tile([rows(x * r), rows(r * r), rows(r * h), rows(x0[...] * y), rows(r0[...] * y)])


def second_body(
    size_ref, slot_ref, r0, r1, r2, x0, g0, lcat_ref, rcat_ref, y_ref, m_ref, part_ref
):
    mixed = mix_all(slot_ref, (r0, r1, r2), lcat_ref, m_ref)
    part_ref[...] = five(x0, r0, g0, fold_all(size_ref, mixed, rcat_ref, y_ref))


def mix_body(slot_ref, r0, r1, r2, lcat_ref, m_ref):
    mix_all(slot_ref, (r0, r1, r2), lcat_ref, m_ref)


def fold_body(size_ref, m_ref, r0, x0, h0, rcat_ref, part_ref, y_ref):
    mixed = [m_ref[p] for p in range(m_ref.shape[0])]
    part = five(x0, r0, h0, fold_all(size_ref, mixed, rcat_ref, y_ref))
    part_ref[...] = jnp.broadcast_to(part[None], part_ref.shape)


def blend_body(c_in, a_ref, b_ref, x_ref, out_ref):
    pairs = a_ref.shape[0]
    out_ref[:pairs] = c_in[2:3, 0:1] * a_ref[...] + c_in[3:4, 0:1] * b_ref[...]
    out_ref[pairs] = unpack(x_ref[...])


def cross_body(flag_ref, b_ref, n_ref, m_ref, w_ref, s0, s1, u_ref):
    stay = flag_ref[0:1, 0:1] > 0.5
    pairs, side, _ = m_ref.shape
    new = unpack(jnp.where(stay[None], s0[...], s1[...]))
    x = jnp.where(stay, b_ref[pairs], n_ref[pairs])
    left = jnp.concatenate([x.T, new.T], axis=0)
    lh, ll = halves(left)
    for p in range(pairs):
        old, new = jnp.where(stay, b_ref[p], n_ref[p]), jnp.where(stay, m_ref[p], w_ref[p])
        rh, rl = halves(jnp.concatenate([old, new], axis=1))
        both = three(lh, ll, rh, rl)
        u_ref[0, p] = both[:side, :side]
        u_ref[1, p] = both[:side, side:] + both[side:, :side]
        u_ref[2, p] = both[side:, side:]


def chunk_body(terms_ref, out_ref):
    out_ref[...] = jnp.sum(terms_ref[...], axis=0)


def fan_body(block_ref, mine, *refs):
    others, out_ref = refs[:-1], refs[-1]
    cw = block_ref.shape[0]
    block = block_ref[...]
    scalars = mine[...]
    for one in others:
        scalars = scalars + one[...]
    for o in range(out_ref.shape[0]):
        out_ref[o, :cw] = block
        out_ref[o, cw:] = scalars


def numbers(tiles, count):
    total = jnp.sum(jnp.sum(tiles, axis=0), axis=1, keepdims=True)
    return [total[i : i + 1] for i in range(count)]


def store(out_ref, values):
    out_ref[...] = tile([jnp.broadcast_to(v, (1, LANES)) for v in values])


def first_residual_body(g_ref, x_ref, diag_ref, r_ref, c_ref, d_ref):
    pack(d_ref, (), d_ref.shape, diag_ref[0].astype(F32))
    cw = x_ref.shape[1]
    squares, energy = numbers(g_ref[:, cw:], 2)
    factor = lax.rsqrt(squares + 1e-06)
    theta = energy * factor * factor
    r = factor * (g_ref[:, :cw] - theta * x_ref[...]) / (jnp.abs(d_ref[...] - theta) + 1.0)
    r_ref[...] = r
    store(c_ref, [factor, theta, squares * factor * factor])


def second_residual_body(
    s_ref, g_ref, x_ref, diag_ref, r_in, c_in, x_out, h_out, r_ref, c_ref, d_ref
):
    pack(d_ref, (), d_ref.shape, diag_ref[0].astype(F32))
    cw = x_ref.shape[1]
    xr, rr, rh, xhr, rhr = numbers(s_ref[:, cw:], 5)
    factor, first, xx = c_in[0:1, 0:1], c_in[1:2, 0:1], c_in[2:3, 0:1]
    on_x, on_r, theta, xx = update(
        xx, first, factor * xr, rr, factor * rh, factor * xhr, rhr
    )
    on_x = on_x * factor
    x = on_x * x_ref[...] + on_r * r_in[...]
    h = on_x * g_ref[:, :cw] + on_r * s_ref[:, :cw]
    x_out[...] = x
    h_out[...] = h
    r_ref[...] = (h - theta * x) / (jnp.abs(d_ref[...] - theta) + 1.0)
    store(c_ref, [theta, xx, on_x, on_r])


def last_body(scale, parts_ref, c_in, b_ref, s0, u_ref, wave_ref, turn_ref):
    pairs, side = u_ref.shape[1:3]
    xr, rr, rh, xhr, rhr = numbers(parts_ref[...], 5)
    on_x, on_s, _, _ = update(c_in[1:2, 0:1], c_in[0:1, 0:1], xr, rr, rh, xhr, rhr)
    on_x = on_x * scale
    on_s = on_s * scale
    wave_ref[0] = on_x * b_ref[pairs] + unpack(on_s * s0[...])
    root = 1.0 / side**0.5
    xx, xs, ss = on_x * on_x * root, on_x * on_s * root, on_s * on_s * root
    for p in range(pairs):
        turn_ref[p, 0] = xx * u_ref[0, p] + xs * u_ref[1, p] + ss * u_ref[2, p]


def paired(value):
    count = lax.axis_size("sec")
    return lax.ppermute(value, "sec", [(i, i ^ 1) for i in range(count)])


def other(value):
    count, groups = lax.axis_size("sec"), lax.axis_size("ops")
    route = []
    for o in range(groups):
        for i in range(1, count - 1, 2):
            route += [(o * count + i, o * count + i + 1), (o * count + i + 1, o * count + i)]
        if groups % 2 == 0:
            route += [(o * count + i, (o ^ 1) * count + i) for i in (0, count - 1)]
    return lax.ppermute(value, ("ops", "sec"), route)


def last_step(count):
    step = 1
    while step * 4 < count:
        step *= 4
    return step


def over_sectors(value):
    count = lax.axis_size("sec")
    step = 1
    while True:
        last = step == last_step(count)
        found = []
        for d in range(1, min(4, count // step)):
            route = [(i, i ^ (d * step)) for i in range(count)]
            found.append(lax.ppermute(value, "sec", route))
        if last:
            return value, found
        for one in found:
            value = value + one
        step *= 4


def exchange(value):
    return lax.all_to_all(value, "ops", 0, 0)


def local(sector_states, psi_guess, precond_diag, left_ops, right_ops, couple, new_sector):
    side = psi_guess.shape[1]
    pairs = left_ops.shape[0]
    couple = couple.reshape(pairs)
    chunks = lax.axis_size("ops")
    sectors = lax.axis_size("sec")
    cw = side // chunks * side // LANES
    block = jax.ShapeDtypeStruct((chunks, cw, LANES), F32)
    wide = jax.ShapeDtypeStruct((chunks, cw + 8, LANES), F32)
    small = jax.ShapeDtypeStruct((8, LANES), F32)
    inner = jax.ShapeDtypeStruct((pairs, side, side), F32)
    pieces = jax.ShapeDtypeStruct((pairs, 2, side, side), BF16)
    loads = [pltpu.VMEM((pairs, side, side), F32)] * 2 + [pltpu.SemaphoreType.DMA((2 * pairs,))]
    work = 12 * pairs * side**3
    light = 20 * side**2

    def gathered(y, part):
        part, others = over_sectors(part)
        terms = exchange(y)
        (one,) = call(
            chunk_body, (jax.ShapeDtypeStruct((cw, LANES), F32),), [VMEM], [], light, terms
        )
        (full,) = call(
            fan_body, (wide,), [VMEM] * (2 + len(others)), [], light, one, part, *others
        )
        return exchange(full)

    (x0,) = call(start_body, (block,), [SMEM, VMEM], [], light, sector_states, psi_guess)
    x2, x1 = other(x0), paired(x0)
    lcat, rcat, flag, slots = call(
        split_body, (pieces, pieces, small, jax.ShapeDtypeStruct((pairs, 8, LANES), F32)),
        [SMEM] + [ANY] * 3,
        loads + [pltpu.SMEM((pairs,), jnp.int32), pltpu.SemaphoreType.DMA(())],
        light * pairs, new_sector, couple, left_ops, right_ops, limit=52.5,
    )
    y, mx, part = call(
        first_body, (block, inner, small), [SMEM] + [VMEM] * 6, [], work,
        sector_states, slots, x0, x1, x2, lcat, rcat,
    )
    g = gathered(y, part)
    r0, c = call(
        first_residual_body, (block, small), [VMEM] * 3, [pltpu.VMEM(block.shape, F32)], light,
        g, x0, precond_diag,
    )
    r2, r1 = other(r0), paired(r0)
    y, mr, part = call(
        second_body, (block, inner, small), [SMEM] + [VMEM] * 8, [], work,
        sector_states, slots, r0, r1, r2, x0, g, lcat, rcat,
    )
    s = gathered(y, part)
    x, h, s0, c = call(
        second_residual_body, (block, block, block, small), [VMEM] * 6,
        [pltpu.VMEM(block.shape, F32)], light, s, g, x0, precond_diag, r0, c,
    )
    s2, s1 = other(s0), paired(s0)
    (mx,) = call(
        blend_body, (jax.ShapeDtypeStruct((pairs + 1, side, side), F32),), [VMEM] * 4, [],
        light, c, mx, mr, x,
    )
    nx = paired(mx)
    (ms,) = call(
        mix_body, (inner,), [VMEM] * 5, [], work // 2,
        slots, s0, s1, s2, lcat,
    )
    ns = paired(ms)
    many = jax.ShapeDtypeStruct((chunks * sectors, 8, LANES), F32)
    (part,) = call(
        fold_body, (many,), [SMEM] + [VMEM] * 5, [pltpu.VMEM(block.shape, F32)], work // 2,
        sector_states, ms, s0, x, h, rcat,
    )
    parts = lax.all_to_all(part, ("ops", "sec"), 0, 0)
    (u,) = call(
        cross_body, (jax.ShapeDtypeStruct((3, pairs, side, side), F32),), [VMEM] * 7,
        [], work, flag, mx, nx, ms, ns, s0, s1,
    )
    return call(
        functools.partial(last_body, float((sectors * side * side) ** 0.5)),
        (
            jax.ShapeDtypeStruct((1, side, side), F32),
            jax.ShapeDtypeStruct((pairs, 1, side, side), F32),
        ),
        [VMEM] * 5, [], light, parts, c, mx, s0, u,
    )


def solution(mesh):
    in_specs = (
        P("sec"),
        P("sec", None, None),
        P("sec", None, None),
        P("ops", "sec", None, None),
        P("ops", "sec", None, None),
        P("ops", "sec"),
        P("sec"),
    )
    out_specs = (P("sec", None, None), P("ops", "sec", None, None))
    return jax.shard_map(local, mesh=mesh, in_specs=in_specs, out_specs=out_specs, check_vma=False)
```

```python
import functools

import jax
import jax.numpy as jnp
from jax import lax
from jax.experimental import pallas as pl
from jax.experimental.pallas import tpu as pltpu
from jax.sharding import PartitionSpec as P


LANES = 128
F32 = jnp.float32
BF16 = jnp.bfloat16
VMEM = pl.BlockSpec(memory_space=pltpu.VMEM)
ANY = pl.BlockSpec(memory_space=pl.ANY)
SMEM = pl.BlockSpec(memory_space=pltpu.SMEM)


def call(body, outs, in_specs, scratch, flops, *args, limit=8):
    size = sum(a.size * a.dtype.itemsize for a in args)
    size += sum(o.size * o.dtype.itemsize for o in outs)
    return pl.pallas_call(
        body,
        out_shape=tuple(outs),
        in_specs=in_specs,
        out_specs=tuple(VMEM for _ in outs),
        scratch_shapes=scratch,
        compiler_params=pltpu.CompilerParams(vmem_limit_bytes=int(limit * 1024 * 1024)),
        cost_estimate=pl.CostEstimate(flops=flops, bytes_accessed=size, transcendentals=0),
    )(*args)


def pack(ref, lead, block, value):
    rc = value.shape[0] // block[0]
    for o in range(block[0]):
        for j in range(value.shape[1] // LANES):
            ref[lead + (o, slice(j * rc, (j + 1) * rc))] = value[
                o * rc : (o + 1) * rc, j * LANES : (j + 1) * LANES
            ]


def unpack(value):
    chunks, cw, _ = value.shape
    groups = int((cw * chunks // LANES) ** 0.5)
    rc = cw // groups
    return jnp.concatenate(
        [
            jnp.concatenate([value[o, j * rc : (j + 1) * rc] for j in range(groups)], axis=1)
            for o in range(chunks)
        ],
        axis=0,
    )


def halves(value):
    high = value.astype(BF16)
    low = (value - high.astype(F32)).astype(BF16)
    return high, low


def dot(a, b):
    return jnp.dot(a, b, preferred_element_type=F32)


def three(ah, al, bh, bl):
    return dot(
        jnp.concatenate([ah, ah, al], axis=1), jnp.concatenate([bh, bl, bh], axis=0)
    )


def mask(size, side):
    rows = lax.broadcasted_iota(jnp.int32, (side, side), 0)
    cols = lax.broadcasted_iota(jnp.int32, (side, side), 1)
    return (rows < size) & (cols < size)


def pick(slot, blocks):
    value = jnp.zeros(blocks[0].shape, F32)
    for k, block in enumerate(blocks):
        value = jnp.where(slot == float(k), block[...], value)
    return unpack(value)


def fold(mixed, rcat_ref):
    total = None
    for p, one in enumerate(mixed):
        high, low = halves(one)
        term = three(high, low, rcat_ref[p, 0], rcat_ref[p, 1])
        total = term if total is None else total + term
    return total


def rows(value):
    return jnp.sum(value.reshape(-1, LANES), axis=0, keepdims=True)


def tile(parts):
    parts = parts + [jnp.zeros((8 - len(parts), LANES), F32)]
    return jnp.concatenate(parts, axis=0)


def lanes(value, out_ref):
    place = lax.broadcasted_iota(jnp.int32, (1, LANES), 1)
    sums = jnp.sum(value, axis=1, keepdims=True)
    row = jnp.zeros((1, LANES), F32)
    for k in range(value.shape[0]):
        row = jnp.where(place == k, sums[k : k + 1], row)
    out_ref[...] = jnp.broadcast_to(row, out_ref.shape)


def half_angle(middle, first, last):
    gap = last - first
    tilt = -2.0 * middle
    length = jnp.sqrt(gap * gap + tilt * tilt)
    safe = jnp.where(length > 0.0, length, 1.0)
    big = jnp.where(length > 0.0, jnp.sqrt(0.5 + 0.5 * jnp.abs(gap) / safe), 1.0)
    small = 0.5 * tilt / (safe * big)
    sign = jnp.where(tilt > 0.0, 1.0, -1.0)
    cosine = jnp.where(gap >= 0.0, big, jnp.abs(small))
    sine = jnp.where(gap >= 0.0, small, sign * big)
    return cosine, sine, 0.5 * (first + last) - 0.5 * length


def update(xx, first, xr, rr, rh, xhr, rhr):
    n = lax.rsqrt(rr - 2.0 * xr * xr + xr * xr * xx + 1e-06)
    middle = 0.5 * n * ((xhr - xr * first) + (rh - xr * first))
    last = n * n * (rhr - xr * rh - xr * xhr + xr * xr * first)
    cosine, sine, theta = half_angle(middle, first, last)
    on_r = sine * n
    on_x = cosine - on_r * xr
    xx = on_x * on_x * xx + 2.0 * on_x * on_r * xr + on_r * on_r * rr
    return on_x, on_r, theta, xx


def start_body(size_ref, psi_ref, x_ref):
    live = mask(size_ref[0], psi_ref.shape[1])
    pack(x_ref, (), x_ref.shape, jnp.where(live, psi_ref[0].astype(F32), 0.0))


def split_pairs(left_ref, right_ref, lcat_ref, rcat_ref, left, right, sem):
    pairs = lcat_ref.shape[0]
    copies = []
    for p in range(pairs):
        copies.append(pltpu.make_async_copy(left_ref.at[p, 0], left.at[p], sem.at[2 * p]))
        copies.append(pltpu.make_async_copy(right_ref.at[p, 0], right.at[p], sem.at[2 * p + 1]))
    for copy in copies:
        copy.start()
    for p in range(pairs):
        copies[2 * p].wait()
        lcat_ref[p, 0], lcat_ref[p, 1] = halves(left[p])
        copies[2 * p + 1].wait()
        rcat_ref[p, 0], rcat_ref[p, 1] = halves(right[p].T)


def split_body(
    label_ref, couple_hbm, left_ref, right_ref, lcat_ref, rcat_ref, flag_ref, slot_ref,
    left, right, sem, couple_ref, mark,
):
    here = lax.axis_index("sec")
    copy = pltpu.make_async_copy(couple_hbm, couple_ref, mark)
    copy.start()
    split_pairs(left_ref, right_ref, lcat_ref, rcat_ref, left, right, sem)
    copy.wait()
    for p in range(lcat_ref.shape[0]):
        source = couple_ref[p]
        near = here + 1 - 2 * (here % 2)
        slot = jnp.where(source == here, 0.0, jnp.where(source == near, 1.0, 2.0))
        slot_ref[p] = jnp.full(slot_ref.shape[1:], jnp.where(source >= 0, slot, -1.0))
    flag_ref[...] = jnp.full(flag_ref.shape, jnp.where(label_ref[0] == here, 1.0, 0.0))


def mix_all(slot_ref, blocks, lcat_ref, m_ref):
    mixed = []
    for p in range(lcat_ref.shape[0]):
        high, low = halves(pick(slot_ref[p, 0:1, 0:1][None], blocks))
        mixed.append(three(lcat_ref[p, 0], lcat_ref[p, 1], high, low))
        m_ref[p] = mixed[p]
    return mixed


def fold_all(size_ref, mixed, rcat_ref, y_ref):
    y = fold(mixed, rcat_ref)
    pack(y_ref, (), y_ref.shape, jnp.where(mask(size_ref[0], y.shape[0]), y, 0.0))
    return y_ref[...]


def first_body(size_ref, slot_ref, x0, x1, x2, lcat_ref, rcat_ref, y_ref, m_ref, part_ref):
    mixed = mix_all(slot_ref, (x0, x1, x2), lcat_ref, m_ref)
    y = fold_all(size_ref, mixed, rcat_ref, y_ref)
    x = x0[lax.axis_index("ops")]
    part_ref[...] = tile([rows(x * x), rows(x0[...] * y)])


def five(x0, r0, h0, y):
    o = lax.axis_index("ops")
    x, r, h = x0[o], r0[o], h0[o][: x0.shape[1]]
    return tile([rows(x * r), rows(r * r), rows(r * h), rows(x0[...] * y), rows(r0[...] * y)])


def second_body(
    size_ref, slot_ref, r0, r1, r2, x0, g0, lcat_ref, rcat_ref, y_ref, m_ref, part_ref
):
    mixed = mix_all(slot_ref, (r0, r1, r2), lcat_ref, m_ref)
    part_ref[...] = five(x0, r0, g0, fold_all(size_ref, mixed, rcat_ref, y_ref))


def mix_body(slot_ref, r0, r1, r2, lcat_ref, m_ref):
    mix_all(slot_ref, (r0, r1, r2), lcat_ref, m_ref)


def fold_body(size_ref, m_ref, r0, x0, h0, rcat_ref, part_ref, y_ref):
    mixed = [m_ref[p] for p in range(m_ref.shape[0])]
    lanes(five(x0, r0, h0, fold_all(size_ref, mixed, rcat_ref, y_ref)), part_ref)


def blend_body(c_in, a_ref, b_ref, x_ref, out_ref):
    pairs = a_ref.shape[0]
    out_ref[:pairs] = c_in[2:3, 0:1] * a_ref[...] + c_in[3:4, 0:1] * b_ref[...]
    out_ref[pairs] = unpack(x_ref[...])


def cross_body(flag_ref, b_ref, n_ref, m_ref, w_ref, s0, s1, u_ref):
    stay = flag_ref[0:1, 0:1] > 0.5
    pairs, side, _ = m_ref.shape
    new = unpack(jnp.where(stay[None], s0[...], s1[...]))
    x = jnp.where(stay, b_ref[pairs], n_ref[pairs])
    left = jnp.concatenate([x.T, new.T], axis=0)
    lh, ll = halves(left)
    for p in range(pairs):
        old, new = jnp.where(stay, b_ref[p], n_ref[p]), jnp.where(stay, m_ref[p], w_ref[p])
        rh, rl = halves(jnp.concatenate([old, new], axis=1))
        both = three(lh, ll, rh, rl)
        u_ref[0, p] = both[:side, :side]
        u_ref[1, p] = both[:side, side:] + both[side:, :side]
        u_ref[2, p] = both[side:, side:]


def sum_body(terms_ref, mine, *refs):
    others, out_ref = refs[:-1], refs[-1]
    cw = terms_ref.shape[1]
    block = jnp.sum(terms_ref[...], axis=0)
    scalars = mine[...]
    for one in others:
        scalars = scalars + one[...]
    for o in range(out_ref.shape[0]):
        out_ref[o, :cw] = block
        out_ref[o, cw:] = scalars


def numbers(tiles, count):
    total = jnp.sum(jnp.sum(tiles, axis=0), axis=1, keepdims=True)
    return [total[i : i + 1] for i in range(count)]


def store(out_ref, values):
    out_ref[...] = tile([jnp.broadcast_to(v, (1, LANES)) for v in values])


def first_residual_body(g_ref, x_ref, diag_ref, r_ref, c_ref, d_ref):
    pack(d_ref, (), d_ref.shape, diag_ref[0].astype(F32))
    cw = x_ref.shape[1]
    squares, energy = numbers(g_ref[:, cw:], 2)
    factor = lax.rsqrt(squares + 1e-06)
    theta = energy * factor * factor
    r = factor * (g_ref[:, :cw] - theta * x_ref[...]) / (jnp.abs(d_ref[...] - theta) + 1.0)
    r_ref[...] = r
    store(c_ref, [factor, theta, squares * factor * factor])


def second_residual_body(
    s_ref, g_ref, x_ref, diag_ref, r_in, c_in, x_out, h_out, r_ref, c_ref, d_ref
):
    pack(d_ref, (), d_ref.shape, diag_ref[0].astype(F32))
    cw = x_ref.shape[1]
    xr, rr, rh, xhr, rhr = numbers(s_ref[:, cw:], 5)
    factor, first, xx = c_in[0:1, 0:1], c_in[1:2, 0:1], c_in[2:3, 0:1]
    on_x, on_r, theta, xx = update(
        xx, first, factor * xr, rr, factor * rh, factor * xhr, rhr
    )
    on_x = on_x * factor
    x = on_x * x_ref[...] + on_r * r_in[...]
    h = on_x * g_ref[:, :cw] + on_r * s_ref[:, :cw]
    x_out[...] = x
    h_out[...] = h
    r_ref[...] = (h - theta * x) / (jnp.abs(d_ref[...] - theta) + 1.0)
    store(c_ref, [theta, xx, on_x, on_r])


def last_body(scale, parts_ref, c_in, b_ref, s0, u_ref, wave_ref, turn_ref):
    pairs, side = u_ref.shape[1:3]
    total = jnp.sum(parts_ref[...], axis=0, keepdims=True)
    xr, rr, rh, xhr, rhr = [total[:, k : k + 1] for k in range(5)]
    on_x, on_s, _, _ = update(c_in[1:2, 0:1], c_in[0:1, 0:1], xr, rr, rh, xhr, rhr)
    on_x = on_x * scale
    on_s = on_s * scale
    wave_ref[0] = on_x * b_ref[pairs] + unpack(on_s * s0[...])
    root = 1.0 / side**0.5
    xx, xs, ss = on_x * on_x * root, on_x * on_s * root, on_s * on_s * root
    for p in range(pairs):
        turn_ref[p, 0] = xx * u_ref[0, p] + xs * u_ref[1, p] + ss * u_ref[2, p]


def paired(value):
    count = lax.axis_size("sec")
    return lax.ppermute(value, "sec", [(i, i ^ 1) for i in range(count)])


def other(value):
    count, groups = lax.axis_size("sec"), lax.axis_size("ops")
    route = []
    for o in range(groups):
        for i in range(1, count - 1, 2):
            route += [(o * count + i, o * count + i + 1), (o * count + i + 1, o * count + i)]
        if groups % 2 == 0:
            route += [(o * count + i, (o ^ 1) * count + i) for i in (0, count - 1)]
    return lax.ppermute(value, ("ops", "sec"), route)


def last_step(count):
    step = 1
    while step * 4 < count:
        step *= 4
    return step


def over_sectors(value):
    count = lax.axis_size("sec")
    step = 1
    while True:
        last = step == last_step(count)
        found = []
        for d in range(1, min(4, count // step)):
            route = [(i, i ^ (d * step)) for i in range(count)]
            found.append(lax.ppermute(value, "sec", route))
        if last:
            return value, found
        for one in found:
            value = value + one
        step *= 4


def exchange(value):
    return lax.all_to_all(value, "ops", 0, 0)


def local(sector_states, psi_guess, precond_diag, left_ops, right_ops, couple, new_sector):
    side = psi_guess.shape[1]
    pairs = left_ops.shape[0]
    couple = couple.reshape(pairs)
    chunks = lax.axis_size("ops")
    sectors = lax.axis_size("sec")
    cw = side // chunks * side // LANES
    block = jax.ShapeDtypeStruct((chunks, cw, LANES), F32)
    wide = jax.ShapeDtypeStruct((chunks, cw + 8, LANES), F32)
    small = jax.ShapeDtypeStruct((8, LANES), F32)
    inner = jax.ShapeDtypeStruct((pairs, side, side), F32)
    pieces = jax.ShapeDtypeStruct((pairs, 2, side, side), BF16)
    loads = [pltpu.VMEM((pairs, side, side), F32)] * 2 + [pltpu.SemaphoreType.DMA((2 * pairs,))]
    work = 12 * pairs * side**3
    light = 20 * side**2

    def gathered(y, part):
        part, others = over_sectors(part)
        (full,) = call(
            sum_body, (wide,), [VMEM] * (2 + len(others)), [], light,
            exchange(y), part, *others,
        )
        return exchange(full)

    (x0,) = call(start_body, (block,), [SMEM, VMEM], [], light, sector_states, psi_guess)
    x2, x1 = other(x0), paired(x0)
    lcat, rcat, flag, slots = call(
        split_body, (pieces, pieces, small, jax.ShapeDtypeStruct((pairs, 8, LANES), F32)),
        [SMEM] + [ANY] * 3,
        loads + [pltpu.SMEM((pairs,), jnp.int32), pltpu.SemaphoreType.DMA(())],
        light * pairs, new_sector, couple, left_ops, right_ops, limit=52.5,
    )
    y, mx, part = call(
        first_body, (block, inner, small), [SMEM] + [VMEM] * 6, [], work,
        sector_states, slots, x0, x1, x2, lcat, rcat, limit=52,
    )
    g = gathered(y, part)
    r0, c = call(
        first_residual_body, (block, small), [VMEM] * 3, [pltpu.VMEM(block.shape, F32)], light,
        g, x0, precond_diag,
    )
    r2, r1 = other(r0), paired(r0)
    y, mr, part = call(
        second_body, (block, inner, small), [SMEM] + [VMEM] * 8, [], work,
        sector_states, slots, r0, r1, r2, x0, g, lcat, rcat, limit=51.5,
    )
    s = gathered(y, part)
    x, h, s0, c = call(
        second_residual_body, (block, block, block, small), [VMEM] * 6,
        [pltpu.VMEM(block.shape, F32)], light, s, g, x0, precond_diag, r0, c,
    )
    s2, s1 = other(s0), paired(s0)
    (mx,) = call(
        blend_body, (jax.ShapeDtypeStruct((pairs + 1, side, side), F32),), [VMEM] * 4, [],
        light, c, mx, mr, x,
    )
    nx = paired(mx)
    (ms,) = call(
        mix_body, (inner,), [VMEM] * 5, [], work // 2,
        slots, s0, s1, s2, lcat,
    )
    ns = paired(ms)
    many = jax.ShapeDtypeStruct((chunks * sectors, LANES), F32)
    (part,) = call(
        fold_body, (many,), [SMEM] + [VMEM] * 5, [pltpu.VMEM(block.shape, F32)], work // 2,
        sector_states, ms, s0, x, h, rcat,
    )
    parts = lax.all_to_all(part, ("ops", "sec"), 0, 0)
    (u,) = call(
        cross_body, (jax.ShapeDtypeStruct((3, pairs, side, side), F32),), [VMEM] * 7,
        [], work, flag, mx, nx, ms, ns, s0, s1,
    )
    return call(
        functools.partial(last_body, float((sectors * side * side) ** 0.5)),
        (
            jax.ShapeDtypeStruct((1, side, side), F32),
            jax.ShapeDtypeStruct((pairs, 1, side, side), F32),
        ),
        [VMEM] * 5, [], light, parts, c, mx, s0, u,
    )


def solution(mesh):
    in_specs = (
        P("sec"),
        P("sec", None, None),
        P("sec", None, None),
        P("ops", "sec", None, None),
        P("ops", "sec", None, None),
        P("ops", "sec"),
        P("sec"),
    )
    out_specs = (P("sec", None, None), P("ops", "sec", None, None))
    return jax.shard_map(local, mesh=mesh, in_specs=in_specs, out_specs=out_specs, check_vma=False)
```

```python
import functools

import jax
import jax.numpy as jnp
from jax import lax
from jax.experimental import pallas as pl
from jax.experimental.pallas import tpu as pltpu
from jax.sharding import PartitionSpec as P


LANES = 128
F32 = jnp.float32
BF16 = jnp.bfloat16
VMEM = pl.BlockSpec(memory_space=pltpu.VMEM)
ANY = pl.BlockSpec(memory_space=pl.ANY)
SMEM = pl.BlockSpec(memory_space=pltpu.SMEM)


def call(body, outs, in_specs, scratch, flops, *args, limit=8, away=()):
    size = sum(a.size * a.dtype.itemsize for a in args)
    size += sum(o.size * o.dtype.itemsize for o in outs)
    return pl.pallas_call(
        body,
        out_shape=tuple(outs),
        in_specs=in_specs,
        out_specs=tuple(ANY if k in away else VMEM for k in range(len(outs))),
        scratch_shapes=scratch,
        compiler_params=pltpu.CompilerParams(vmem_limit_bytes=int(limit * 1024 * 1024)),
        cost_estimate=pl.CostEstimate(flops=flops, bytes_accessed=size, transcendentals=0),
    )(*args)


def pack(ref, lead, block, value):
    rc = value.shape[0] // block[0]
    for o in range(block[0]):
        for j in range(value.shape[1] // LANES):
            ref[lead + (o, slice(j * rc, (j + 1) * rc))] = value[
                o * rc : (o + 1) * rc, j * LANES : (j + 1) * LANES
            ]


def unpack(value):
    chunks, cw, _ = value.shape
    groups = int((cw * chunks // LANES) ** 0.5)
    rc = cw // groups
    return jnp.concatenate(
        [
            jnp.concatenate([value[o, j * rc : (j + 1) * rc] for j in range(groups)], axis=1)
            for o in range(chunks)
        ],
        axis=0,
    )


def halves(value):
    high = value.astype(BF16)
    low = (value - high.astype(F32)).astype(BF16)
    return high, low


def dot(a, b):
    return jnp.dot(a, b, preferred_element_type=F32)


def three(ah, al, bh, bl):
    return dot(
        jnp.concatenate([ah, ah, al], axis=1), jnp.concatenate([bh, bl, bh], axis=0)
    )


def mask(size, side):
    rows = lax.broadcasted_iota(jnp.int32, (side, side), 0)
    cols = lax.broadcasted_iota(jnp.int32, (side, side), 1)
    return (rows < size) & (cols < size)


def pick(slot, blocks):
    value = jnp.zeros(blocks[0].shape, F32)
    for k, block in enumerate(blocks):
        value = jnp.where(slot == float(k), block[...], value)
    return unpack(value)


def fold(mixed, rcat_ref):
    total = None
    for p, one in enumerate(mixed):
        high, low = halves(one)
        term = three(high, low, rcat_ref[p, 0], rcat_ref[p, 1])
        total = term if total is None else total + term
    return total


def rows(value):
    return jnp.sum(value.reshape(-1, LANES), axis=0, keepdims=True)


def tile(parts):
    parts = parts + [jnp.zeros((8 - len(parts), LANES), F32)]
    return jnp.concatenate(parts, axis=0)


def lanes(value, out_ref):
    place = lax.broadcasted_iota(jnp.int32, (1, LANES), 1)
    sums = jnp.sum(value, axis=1, keepdims=True)
    row = jnp.zeros((1, LANES), F32)
    for k in range(value.shape[0]):
        row = jnp.where(place == k, sums[k : k + 1], row)
    out_ref[...] = jnp.broadcast_to(row, out_ref.shape)


def half_angle(middle, first, last):
    gap = last - first
    tilt = -2.0 * middle
    length = jnp.sqrt(gap * gap + tilt * tilt)
    safe = jnp.where(length > 0.0, length, 1.0)
    big = jnp.where(length > 0.0, jnp.sqrt(0.5 + 0.5 * jnp.abs(gap) / safe), 1.0)
    small = 0.5 * tilt / (safe * big)
    sign = jnp.where(tilt > 0.0, 1.0, -1.0)
    cosine = jnp.where(gap >= 0.0, big, jnp.abs(small))
    sine = jnp.where(gap >= 0.0, small, sign * big)
    return cosine, sine, 0.5 * (first + last) - 0.5 * length


def update(xx, first, xr, rr, rh, xhr, rhr):
    n = lax.rsqrt(rr - 2.0 * xr * xr + xr * xr * xx + 1e-06)
    middle = 0.5 * n * ((xhr - xr * first) + (rh - xr * first))
    last = n * n * (rhr - xr * rh - xr * xhr + xr * xr * first)
    cosine, sine, theta = half_angle(middle, first, last)
    on_r = sine * n
    on_x = cosine - on_r * xr
    xx = on_x * on_x * xx + 2.0 * on_x * on_r * xr + on_r * on_r * rr
    return on_x, on_r, theta, xx


def start_body(size_ref, psi_ref, x_ref):
    live = mask(size_ref[0], psi_ref.shape[1])
    pack(x_ref, (), x_ref.shape, jnp.where(live, psi_ref[0].astype(F32), 0.0))


def split_pairs(left_ref, right_ref, lcat_ref, rcat_ref, left, right, sem):
    pairs = lcat_ref.shape[0]
    copies = []
    for p in range(pairs):
        copies.append(pltpu.make_async_copy(left_ref.at[p, 0], left.at[p], sem.at[2 * p]))
        copies.append(pltpu.make_async_copy(right_ref.at[p, 0], right.at[p], sem.at[2 * p + 1]))
    for copy in copies:
        copy.start()
    for p in range(pairs):
        copies[2 * p].wait()
        lcat_ref[p, 0], lcat_ref[p, 1] = halves(left[p])
        copies[2 * p + 1].wait()
        rcat_ref[p, 0], rcat_ref[p, 1] = halves(right[p].T)


def split_body(
    label_ref, couple_hbm, left_ref, right_ref, lcat_ref, rcat_ref, flag_ref, slot_ref,
    left, right, sem, couple_ref, mark,
):
    here = lax.axis_index("sec")
    copy = pltpu.make_async_copy(couple_hbm, couple_ref, mark)
    copy.start()
    split_pairs(left_ref, right_ref, lcat_ref, rcat_ref, left, right, sem)
    copy.wait()
    for p in range(lcat_ref.shape[0]):
        source = couple_ref[p]
        near = here + 1 - 2 * (here % 2)
        slot = jnp.where(source == here, 0.0, jnp.where(source == near, 1.0, 2.0))
        slot_ref[p] = jnp.full(slot_ref.shape[1:], jnp.where(source >= 0, slot, -1.0))
    flag_ref[...] = jnp.full(flag_ref.shape, jnp.where(label_ref[0] == here, 1.0, 0.0))


def mix_all(slot_ref, blocks, lcat_ref, m_ref):
    mixed = []
    for p in range(lcat_ref.shape[0]):
        high, low = halves(pick(slot_ref[p, 0:1, 0:1][None], blocks))
        mixed.append(three(lcat_ref[p, 0], lcat_ref[p, 1], high, low))
        m_ref[p] = mixed[p]
    return mixed


def fold_all(size_ref, mixed, rcat_ref, y_ref):
    y = fold(mixed, rcat_ref)
    pack(y_ref, (), y_ref.shape, jnp.where(mask(size_ref[0], y.shape[0]), y, 0.0))


def first_body(
    size_ref, slot_ref, x0, x1, x2, lcat_ref, rcat_ref, y_out, m_ref, part_ref, y_ref, sem
):
    fold_all(size_ref, mix_all(slot_ref, (x0, x1, x2), lcat_ref, m_ref), rcat_ref, y_ref)
    copy = pltpu.make_async_copy(y_ref, y_out, sem)
    copy.start()
    x = x0[lax.axis_index("ops")]
    part_ref[...] = tile([rows(x * x), rows(x0[...] * y_ref[...])])
    copy.wait()


def five(x0, r0, h0, y):
    o = lax.axis_index("ops")
    x, r, h = x0[o], r0[o], h0[o][: x0.shape[1]]
    return tile([rows(x * r), rows(r * r), rows(r * h), rows(x0[...] * y), rows(r0[...] * y)])


def second_body(
    size_ref, slot_ref, r0, r1, r2, x0, g0, lcat_ref, rcat_ref, y_out, m_ref, part_ref,
    y_ref, sem,
):
    fold_all(size_ref, mix_all(slot_ref, (r0, r1, r2), lcat_ref, m_ref), rcat_ref, y_ref)
    copy = pltpu.make_async_copy(y_ref, y_out, sem)
    copy.start()
    part_ref[...] = five(x0, r0, g0, y_ref[...])
    copy.wait()


def mix_body(slot_ref, r0, r1, r2, lcat_ref, m_ref):
    mix_all(slot_ref, (r0, r1, r2), lcat_ref, m_ref)


def fold_body(size_ref, m_ref, r0, x0, h0, rcat_ref, part_ref, y_ref):
    mixed = [m_ref[p] for p in range(m_ref.shape[0])]
    fold_all(size_ref, mixed, rcat_ref, y_ref)
    lanes(five(x0, r0, h0, y_ref[...]), part_ref)


def blend_body(c_in, a_ref, b_ref, x_ref, out_ref):
    pairs = a_ref.shape[0]
    out_ref[:pairs] = c_in[2:3, 0:1] * a_ref[...] + c_in[3:4, 0:1] * b_ref[...]
    out_ref[pairs] = unpack(x_ref[...])


def cross_body(flag_ref, b_ref, n_ref, m_ref, w_ref, s0, s1, u_ref):
    stay = flag_ref[0:1, 0:1] > 0.5
    pairs, side, _ = m_ref.shape
    new = unpack(jnp.where(stay[None], s0[...], s1[...]))
    x = jnp.where(stay, b_ref[pairs], n_ref[pairs])
    left = jnp.concatenate([x.T, new.T], axis=0)
    lh, ll = halves(left)
    for p in range(pairs):
        old, new = jnp.where(stay, b_ref[p], n_ref[p]), jnp.where(stay, m_ref[p], w_ref[p])
        rh, rl = halves(jnp.concatenate([old, new], axis=1))
        both = three(lh, ll, rh, rl)
        u_ref[0, p] = both[:side, :side]
        u_ref[1, p] = both[:side, side:] + both[side:, :side]
        u_ref[2, p] = both[side:, side:]


def sum_body(terms_ref, mine, *refs):
    others, out_ref = refs[:-1], refs[-1]
    cw = terms_ref.shape[1]
    block = jnp.sum(terms_ref[...], axis=0)
    scalars = mine[...]
    for one in others:
        scalars = scalars + one[...]
    for o in range(out_ref.shape[0]):
        out_ref[o, :cw] = block
        out_ref[o, cw:] = scalars


def numbers(tiles, count):
    total = jnp.sum(jnp.sum(tiles, axis=0), axis=1, keepdims=True)
    return [total[i : i + 1] for i in range(count)]


def store(out_ref, values):
    out_ref[...] = tile([jnp.broadcast_to(v, (1, LANES)) for v in values])


def first_residual_body(g_ref, x_ref, diag_ref, r_ref, c_ref, d_ref):
    pack(d_ref, (), d_ref.shape, diag_ref[0].astype(F32))
    cw = x_ref.shape[1]
    squares, energy = numbers(g_ref[:, cw:], 2)
    factor = lax.rsqrt(squares + 1e-06)
    theta = energy * factor * factor
    r = factor * (g_ref[:, :cw] - theta * x_ref[...]) / (jnp.abs(d_ref[...] - theta) + 1.0)
    r_ref[...] = r
    store(c_ref, [factor, theta, squares * factor * factor])


def second_residual_body(
    s_ref, g_ref, x_ref, diag_ref, r_in, c_in, x_out, h_out, r_ref, c_ref, d_ref
):
    pack(d_ref, (), d_ref.shape, diag_ref[0].astype(F32))
    cw = x_ref.shape[1]
    xr, rr, rh, xhr, rhr = numbers(s_ref[:, cw:], 5)
    factor, first, xx = c_in[0:1, 0:1], c_in[1:2, 0:1], c_in[2:3, 0:1]
    on_x, on_r, theta, xx = update(
        xx, first, factor * xr, rr, factor * rh, factor * xhr, rhr
    )
    on_x = on_x * factor
    x = on_x * x_ref[...] + on_r * r_in[...]
    h = on_x * g_ref[:, :cw] + on_r * s_ref[:, :cw]
    x_out[...] = x
    h_out[...] = h
    r_ref[...] = (h - theta * x) / (jnp.abs(d_ref[...] - theta) + 1.0)
    store(c_ref, [theta, xx, on_x, on_r])


def last_body(
    scale, parts_ref, c_in, b_ref, s0, u_ref, wave_out, turn_out, wave_ref, turn_ref, sem
):
    pairs, side = u_ref.shape[1:3]
    total = jnp.sum(parts_ref[...], axis=0, keepdims=True)
    xr, rr, rh, xhr, rhr = [total[:, k : k + 1] for k in range(5)]
    on_x, on_s, _, _ = update(c_in[1:2, 0:1], c_in[0:1, 0:1], xr, rr, rh, xhr, rhr)
    on_x = on_x * scale
    on_s = on_s * scale
    root = 1.0 / side**0.5
    xx, xs, ss = on_x * on_x * root, on_x * on_s * root, on_s * on_s * root
    copies = []
    for p in range(pairs):
        turn_ref[p] = xx * u_ref[0, p] + xs * u_ref[1, p] + ss * u_ref[2, p]
        copies.append(pltpu.make_async_copy(turn_ref.at[p], turn_out.at[p, 0], sem.at[p]))
        copies[p].start()
    wave_ref[...] = on_x * b_ref[pairs] + unpack(on_s * s0[...])
    copies.append(pltpu.make_async_copy(wave_ref, wave_out.at[0], sem.at[pairs]))
    copies[pairs].start()
    for copy in copies:
        copy.wait()


def paired(value):
    count = lax.axis_size("sec")
    return lax.ppermute(value, "sec", [(i, i ^ 1) for i in range(count)])


def other(value):
    count, groups = lax.axis_size("sec"), lax.axis_size("ops")
    route = []
    for o in range(groups):
        for i in range(1, count - 1, 2):
            route += [(o * count + i, o * count + i + 1), (o * count + i + 1, o * count + i)]
        if groups % 2 == 0:
            route += [(o * count + i, (o ^ 1) * count + i) for i in (0, count - 1)]
    return lax.ppermute(value, ("ops", "sec"), route)


def last_step(count):
    step = 1
    while step * 4 < count:
        step *= 4
    return step


def over_sectors(value):
    count = lax.axis_size("sec")
    step = 1
    while True:
        last = step == last_step(count)
        found = []
        for d in range(1, min(4, count // step)):
            route = [(i, i ^ (d * step)) for i in range(count)]
            found.append(lax.ppermute(value, "sec", route))
        if last:
            return value, found
        for one in found:
            value = value + one
        step *= 4


def exchange(value):
    return lax.all_to_all(value, "ops", 0, 0)


def local(sector_states, psi_guess, precond_diag, left_ops, right_ops, couple, new_sector):
    side = psi_guess.shape[1]
    pairs = left_ops.shape[0]
    couple = couple.reshape(pairs)
    chunks = lax.axis_size("ops")
    sectors = lax.axis_size("sec")
    cw = side // chunks * side // LANES
    block = jax.ShapeDtypeStruct((chunks, cw, LANES), F32)
    wide = jax.ShapeDtypeStruct((chunks, cw + 8, LANES), F32)
    small = jax.ShapeDtypeStruct((8, LANES), F32)
    inner = jax.ShapeDtypeStruct((pairs, side, side), F32)
    room = [pltpu.VMEM(block.shape, F32), pltpu.SemaphoreType.DMA(())]
    pieces = jax.ShapeDtypeStruct((pairs, 2, side, side), BF16)
    loads = [pltpu.VMEM((pairs, side, side), F32)] * 2 + [pltpu.SemaphoreType.DMA((2 * pairs,))]
    work = 12 * pairs * side**3
    light = 20 * side**2

    def gathered(y, part):
        part, others = over_sectors(part)
        (full,) = call(
            sum_body, (wide,), [VMEM] * (2 + len(others)), [], light,
            exchange(y), part, *others,
        )
        return exchange(full)

    (x0,) = call(start_body, (block,), [SMEM, VMEM], [], light, sector_states, psi_guess)
    x2, x1 = other(x0), paired(x0)
    lcat, rcat, flag, slots = call(
        split_body, (pieces, pieces, small, jax.ShapeDtypeStruct((pairs, 8, LANES), F32)),
        [SMEM] + [ANY] * 3,
        loads + [pltpu.SMEM((pairs,), jnp.int32), pltpu.SemaphoreType.DMA(())],
        light * pairs, new_sector, couple, left_ops, right_ops, limit=52.5,
    )
    y, mx, part = call(
        first_body, (block, inner, small), [SMEM] + [VMEM] * 6, room, work,
        sector_states, slots, x0, x1, x2, lcat, rcat, away=(0,),
    )
    g = gathered(y, part)
    r0, c = call(
        first_residual_body, (block, small), [VMEM] * 3, [pltpu.VMEM(block.shape, F32)], light,
        g, x0, precond_diag,
    )
    r2, r1 = other(r0), paired(r0)
    y, mr, part = call(
        second_body, (block, inner, small), [SMEM] + [VMEM] * 8, room, work,
        sector_states, slots, r0, r1, r2, x0, g, lcat, rcat, away=(0,),
    )
    s = gathered(y, part)
    x, h, s0, c = call(
        second_residual_body, (block, block, block, small), [VMEM] * 6,
        [pltpu.VMEM(block.shape, F32)], light, s, g, x0, precond_diag, r0, c,
    )
    s2, s1 = other(s0), paired(s0)
    (mx,) = call(
        blend_body, (jax.ShapeDtypeStruct((pairs + 1, side, side), F32),), [VMEM] * 4, [],
        light, c, mx, mr, x,
    )
    nx = paired(mx)
    (ms,) = call(
        mix_body, (inner,), [VMEM] * 5, [], work // 2,
        slots, s0, s1, s2, lcat,
    )
    ns = paired(ms)
    many = jax.ShapeDtypeStruct((chunks * sectors, LANES), F32)
    (part,) = call(
        fold_body, (many,), [SMEM] + [VMEM] * 5, [pltpu.VMEM(block.shape, F32)], work // 2,
        sector_states, ms, s0, x, h, rcat,
    )
    parts = lax.all_to_all(part, ("ops", "sec"), 0, 0)
    (u,) = call(
        cross_body, (jax.ShapeDtypeStruct((3, pairs, side, side), F32),), [VMEM] * 7,
        [], work, flag, mx, nx, ms, ns, s0, s1,
    )
    return call(
        functools.partial(last_body, float((sectors * side * side) ** 0.5)),
        (
            jax.ShapeDtypeStruct((1, side, side), F32),
            jax.ShapeDtypeStruct((pairs, 1, side, side), F32),
        ),
        [VMEM] * 5,
        [
            pltpu.VMEM((side, side), F32),
            pltpu.VMEM((pairs, side, side), F32),
            pltpu.SemaphoreType.DMA((pairs + 1,)),
        ],
        light, parts, c, mx, s0, u, away=(0, 1),
    )


def solution(mesh):
    in_specs = (
        P("sec"),
        P("sec", None, None),
        P("sec", None, None),
        P("ops", "sec", None, None),
        P("ops", "sec", None, None),
        P("ops", "sec"),
        P("sec"),
    )
    out_specs = (P("sec", None, None), P("ops", "sec", None, None))
    return jax.shard_map(local, mesh=mesh, in_specs=in_specs, out_specs=out_specs, check_vma=False)
```

```python
import functools

import jax
import jax.numpy as jnp
from jax import lax
from jax.experimental import pallas as pl
from jax.experimental.pallas import tpu as pltpu
from jax.sharding import PartitionSpec as P


LANES = 128
F32 = jnp.float32
BF16 = jnp.bfloat16
VMEM = pl.BlockSpec(memory_space=pltpu.VMEM)
ANY = pl.BlockSpec(memory_space=pl.ANY)
SMEM = pl.BlockSpec(memory_space=pltpu.SMEM)


def call(body, outs, in_specs, scratch, flops, *args, limit=8, away=()):
    size = sum(a.size * a.dtype.itemsize for a in args)
    size += sum(o.size * o.dtype.itemsize for o in outs)
    return pl.pallas_call(
        body,
        out_shape=tuple(pltpu.HBM(o.shape, o.dtype) if k in away else o for k, o in enumerate(outs)),
        in_specs=in_specs,
        out_specs=tuple(pl.BlockSpec(memory_space=pltpu.HBM) if k in away else VMEM for k in range(len(outs))),
        scratch_shapes=scratch,
        compiler_params=pltpu.CompilerParams(vmem_limit_bytes=int(limit * 1024 * 1024)),
        cost_estimate=pl.CostEstimate(flops=flops, bytes_accessed=size, transcendentals=0),
    )(*args)


def pack(ref, lead, block, value):
    rc = value.shape[0] // block[0]
    for o in range(block[0]):
        for j in range(value.shape[1] // LANES):
            ref[lead + (o, slice(j * rc, (j + 1) * rc))] = value[
                o * rc : (o + 1) * rc, j * LANES : (j + 1) * LANES
            ]


def unpack(value):
    chunks, cw, _ = value.shape
    groups = int((cw * chunks // LANES) ** 0.5)
    rc = cw // groups
    return jnp.concatenate(
        [
            jnp.concatenate([value[o, j * rc : (j + 1) * rc] for j in range(groups)], axis=1)
            for o in range(chunks)
        ],
        axis=0,
    )


def halves(value):
    high = value.astype(BF16)
    low = (value - high.astype(F32)).astype(BF16)
    return high, low


def dot(a, b):
    return jnp.dot(a, b, preferred_element_type=F32)


def three(ah, al, bh, bl):
    return dot(
        jnp.concatenate([ah, ah, al], axis=1), jnp.concatenate([bh, bl, bh], axis=0)
    )


def mask(size, side):
    rows = lax.broadcasted_iota(jnp.int32, (side, side), 0)
    cols = lax.broadcasted_iota(jnp.int32, (side, side), 1)
    return (rows < size) & (cols < size)


def pick(slot, blocks):
    value = jnp.zeros(blocks[0].shape, F32)
    for k, block in enumerate(blocks):
        value = jnp.where(slot == float(k), block[...], value)
    return unpack(value)


def fold(mixed, rcat_ref):
    total = None
    for p, one in enumerate(mixed):
        high, low = halves(one)
        term = three(high, low, rcat_ref[p, 0], rcat_ref[p, 1])
        total = term if total is None else total + term
    return total


def rows(value):
    return jnp.sum(value.reshape(-1, LANES), axis=0, keepdims=True)


def tile(parts):
    parts = parts + [jnp.zeros((8 - len(parts), LANES), F32)]
    return jnp.concatenate(parts, axis=0)


def lanes(value, out_ref):
    place = lax.broadcasted_iota(jnp.int32, (1, LANES), 1)
    sums = jnp.sum(value, axis=1, keepdims=True)
    row = jnp.zeros((1, LANES), F32)
    for k in range(value.shape[0]):
        row = jnp.where(place == k, sums[k : k + 1], row)
    out_ref[...] = jnp.broadcast_to(row, out_ref.shape)


def half_angle(middle, first, last):
    gap = last - first
    tilt = -2.0 * middle
    length = jnp.sqrt(gap * gap + tilt * tilt)
    safe = jnp.where(length > 0.0, length, 1.0)
    big = jnp.where(length > 0.0, jnp.sqrt(0.5 + 0.5 * jnp.abs(gap) / safe), 1.0)
    small = 0.5 * tilt / (safe * big)
    sign = jnp.where(tilt > 0.0, 1.0, -1.0)
    cosine = jnp.where(gap >= 0.0, big, jnp.abs(small))
    sine = jnp.where(gap >= 0.0, small, sign * big)
    return cosine, sine, 0.5 * (first + last) - 0.5 * length


def update(xx, first, xr, rr, rh, xhr, rhr):
    n = lax.rsqrt(rr - 2.0 * xr * xr + xr * xr * xx + 1e-06)
    middle = 0.5 * n * ((xhr - xr * first) + (rh - xr * first))
    last = n * n * (rhr - xr * rh - xr * xhr + xr * xr * first)
    cosine, sine, theta = half_angle(middle, first, last)
    on_r = sine * n
    on_x = cosine - on_r * xr
    xx = on_x * on_x * xx + 2.0 * on_x * on_r * xr + on_r * on_r * rr
    return on_x, on_r, theta, xx


def start_body(size_ref, psi_ref, x_ref):
    live = mask(size_ref[0], psi_ref.shape[1])
    pack(x_ref, (), x_ref.shape, jnp.where(live, psi_ref[0].astype(F32), 0.0))


def split_pairs(left_ref, right_ref, lcat_ref, rcat_ref, left, right, sem):
    pairs = lcat_ref.shape[0]
    copies = []
    for p in range(pairs):
        copies.append(pltpu.make_async_copy(left_ref.at[p, 0], left.at[p], sem.at[2 * p]))
        copies.append(pltpu.make_async_copy(right_ref.at[p, 0], right.at[p], sem.at[2 * p + 1]))
    for copy in copies:
        copy.start()
    for p in range(pairs):
        copies[2 * p].wait()
        lcat_ref[p, 0], lcat_ref[p, 1] = halves(left[p])
        copies[2 * p + 1].wait()
        rcat_ref[p, 0], rcat_ref[p, 1] = halves(right[p].T)


def split_body(
    label_ref, couple_hbm, left_ref, right_ref, lcat_ref, rcat_ref, flag_ref, slot_ref,
    left, right, sem, couple_ref, mark,
):
    here = lax.axis_index("sec")
    copy = pltpu.make_async_copy(couple_hbm, couple_ref, mark)
    copy.start()
    split_pairs(left_ref, right_ref, lcat_ref, rcat_ref, left, right, sem)
    copy.wait()
    for p in range(lcat_ref.shape[0]):
        source = couple_ref[p]
        near = here + 1 - 2 * (here % 2)
        slot = jnp.where(source == here, 0.0, jnp.where(source == near, 1.0, 2.0))
        slot_ref[p] = jnp.full(slot_ref.shape[1:], jnp.where(source >= 0, slot, -1.0))
    flag_ref[...] = jnp.full(flag_ref.shape, jnp.where(label_ref[0] == here, 1.0, 0.0))


def mix_all(slot_ref, blocks, lcat_ref, m_ref):
    mixed = []
    for p in range(lcat_ref.shape[0]):
        high, low = halves(pick(slot_ref[p, 0:1, 0:1][None], blocks))
        mixed.append(three(lcat_ref[p, 0], lcat_ref[p, 1], high, low))
        m_ref[p] = mixed[p]
    return mixed


def fold_all(size_ref, mixed, rcat_ref, y_ref):
    y = fold(mixed, rcat_ref)
    pack(y_ref, (), y_ref.shape, jnp.where(mask(size_ref[0], y.shape[0]), y, 0.0))
    return y_ref[...]


def first_body(size_ref, slot_ref, x0, x1, x2, lcat_ref, rcat_ref, y_ref, m_ref, part_ref):
    mixed = mix_all(slot_ref, (x0, x1, x2), lcat_ref, m_ref)
    y = fold_all(size_ref, mixed, rcat_ref, y_ref)
    x = x0[lax.axis_index("ops")]
    part_ref[...] = tile([rows(x * x), rows(x0[...] * y)])


def five(x0, r0, h0, y):
    o = lax.axis_index("ops")
    x, r, h = x0[o], r0[o], h0[o][: x0.shape[1]]
    return tile([rows(x * r), rows(r * r), rows(r * h), rows(x0[...] * y), rows(r0[...] * y)])


def second_body(
    size_ref, slot_ref, r0, r1, r2, x0, g0, lcat_ref, rcat_ref, y_ref, m_out, part_ref,
    m_ref, sem,
):
    mixed = mix_all(slot_ref, (r0, r1, r2), lcat_ref, m_ref)
    copy = pltpu.make_async_copy(m_ref, m_out, sem)
    copy.start()
    part_ref[...] = five(x0, r0, g0, fold_all(size_ref, mixed, rcat_ref, y_ref))
    copy.wait()


def mix_body(slot_ref, r0, r1, r2, lcat_ref, m_ref):
    mix_all(slot_ref, (r0, r1, r2), lcat_ref, m_ref)


def fold_body(size_ref, m_ref, r0, x0, h0, rcat_ref, part_ref, y_ref):
    mixed = [m_ref[p] for p in range(m_ref.shape[0])]
    lanes(five(x0, r0, h0, fold_all(size_ref, mixed, rcat_ref, y_ref)), part_ref)


def blend_body(c_in, a_ref, b_ref, x_ref, out_ref):
    pairs = a_ref.shape[0]
    out_ref[:pairs] = c_in[2:3, 0:1] * a_ref[...] + c_in[3:4, 0:1] * b_ref[...]
    out_ref[pairs] = unpack(x_ref[...])


def cross_body(flag_ref, b_ref, n_ref, m_ref, w_ref, s0, s1, u_ref):
    stay = flag_ref[0:1, 0:1] > 0.5
    pairs, side, _ = m_ref.shape
    new = unpack(jnp.where(stay[None], s0[...], s1[...]))
    x = jnp.where(stay, b_ref[pairs], n_ref[pairs])
    left = jnp.concatenate([x.T, new.T], axis=0)
    lh, ll = halves(left)
    for p in range(pairs):
        old, new = jnp.where(stay, b_ref[p], n_ref[p]), jnp.where(stay, m_ref[p], w_ref[p])
        rh, rl = halves(jnp.concatenate([old, new], axis=1))
        both = three(lh, ll, rh, rl)
        u_ref[0, p] = both[:side, :side]
        u_ref[1, p] = both[:side, side:] + both[side:, :side]
        u_ref[2, p] = both[side:, side:]


def sum_body(terms_ref, mine, *refs):
    others, out_ref = refs[:-1], refs[-1]
    cw = terms_ref.shape[1]
    block = jnp.sum(terms_ref[...], axis=0)
    scalars = mine[...]
    for one in others:
        scalars = scalars + one[...]
    for o in range(out_ref.shape[0]):
        out_ref[o, :cw] = block
        out_ref[o, cw:] = scalars


def numbers(tiles, count):
    total = jnp.sum(jnp.sum(tiles, axis=0), axis=1, keepdims=True)
    return [total[i : i + 1] for i in range(count)]


def store(out_ref, values):
    out_ref[...] = tile([jnp.broadcast_to(v, (1, LANES)) for v in values])


def first_residual_body(g_ref, x_ref, diag_ref, r_ref, c_ref, d_ref):
    pack(d_ref, (), d_ref.shape, diag_ref[0].astype(F32))
    cw = x_ref.shape[1]
    squares, energy = numbers(g_ref[:, cw:], 2)
    factor = lax.rsqrt(squares + 1e-06)
    theta = energy * factor * factor
    r = factor * (g_ref[:, :cw] - theta * x_ref[...]) / (jnp.abs(d_ref[...] - theta) + 1.0)
    r_ref[...] = r
    store(c_ref, [factor, theta, squares * factor * factor])


def second_residual_body(
    s_ref, g_ref, x_ref, diag_ref, r_in, c_in, x_out, h_out, r_ref, c_ref, d_ref
):
    pack(d_ref, (), d_ref.shape, diag_ref[0].astype(F32))
    cw = x_ref.shape[1]
    xr, rr, rh, xhr, rhr = numbers(s_ref[:, cw:], 5)
    factor, first, xx = c_in[0:1, 0:1], c_in[1:2, 0:1], c_in[2:3, 0:1]
    on_x, on_r, theta, xx = update(
        xx, first, factor * xr, rr, factor * rh, factor * xhr, rhr
    )
    on_x = on_x * factor
    x = on_x * x_ref[...] + on_r * r_in[...]
    h = on_x * g_ref[:, :cw] + on_r * s_ref[:, :cw]
    x_out[...] = x
    h_out[...] = h
    r_ref[...] = (h - theta * x) / (jnp.abs(d_ref[...] - theta) + 1.0)
    store(c_ref, [theta, xx, on_x, on_r])


def last_body(scale, parts_ref, c_in, b_ref, s0, u_ref, wave_ref, turn_ref):
    pairs, side = u_ref.shape[1:3]
    total = jnp.sum(parts_ref[...], axis=0, keepdims=True)
    xr, rr, rh, xhr, rhr = [total[:, k : k + 1] for k in range(5)]
    on_x, on_s, _, _ = update(c_in[1:2, 0:1], c_in[0:1, 0:1], xr, rr, rh, xhr, rhr)
    on_x = on_x * scale
    on_s = on_s * scale
    wave_ref[0] = on_x * b_ref[pairs] + unpack(on_s * s0[...])
    root = 1.0 / side**0.5
    xx, xs, ss = on_x * on_x * root, on_x * on_s * root, on_s * on_s * root
    for p in range(pairs):
        turn_ref[p, 0] = xx * u_ref[0, p] + xs * u_ref[1, p] + ss * u_ref[2, p]


def paired(value):
    count = lax.axis_size("sec")
    return lax.ppermute(value, "sec", [(i, i ^ 1) for i in range(count)])


def other(value):
    count, groups = lax.axis_size("sec"), lax.axis_size("ops")
    route = []
    for o in range(groups):
        for i in range(1, count - 1, 2):
            route += [(o * count + i, o * count + i + 1), (o * count + i + 1, o * count + i)]
        if groups % 2 == 0:
            route += [(o * count + i, (o ^ 1) * count + i) for i in (0, count - 1)]
    return lax.ppermute(value, ("ops", "sec"), route)


def last_step(count):
    step = 1
    while step * 4 < count:
        step *= 4
    return step


def over_sectors(value):
    count = lax.axis_size("sec")
    step = 1
    while True:
        last = step == last_step(count)
        found = []
        for d in range(1, min(4, count // step)):
            route = [(i, i ^ (d * step)) for i in range(count)]
            found.append(lax.ppermute(value, "sec", route))
        if last:
            return value, found
        for one in found:
            value = value + one
        step *= 4


def exchange(value):
    return lax.all_to_all(value, "ops", 0, 0)


def local(sector_states, psi_guess, precond_diag, left_ops, right_ops, couple, new_sector):
    side = psi_guess.shape[1]
    pairs = left_ops.shape[0]
    couple = couple.reshape(pairs)
    chunks = lax.axis_size("ops")
    sectors = lax.axis_size("sec")
    cw = side // chunks * side // LANES
    block = jax.ShapeDtypeStruct((chunks, cw, LANES), F32)
    wide = jax.ShapeDtypeStruct((chunks, cw + 8, LANES), F32)
    small = jax.ShapeDtypeStruct((8, LANES), F32)
    inner = jax.ShapeDtypeStruct((pairs, side, side), F32)
    room = [pltpu.VMEM(inner.shape, F32), pltpu.SemaphoreType.DMA(())]
    pieces = jax.ShapeDtypeStruct((pairs, 2, side, side), BF16)
    loads = [pltpu.VMEM((pairs, side, side), F32)] * 2 + [pltpu.SemaphoreType.DMA((2 * pairs,))]
    work = 12 * pairs * side**3
    light = 20 * side**2

    def gathered(y, part):
        part, others = over_sectors(part)
        (full,) = call(
            sum_body, (wide,), [VMEM] * (2 + len(others)), [], light,
            exchange(y), part, *others,
        )
        return exchange(full)

    (x0,) = call(start_body, (block,), [SMEM, VMEM], [], light, sector_states, psi_guess)
    x2, x1 = other(x0), paired(x0)
    lcat, rcat, flag, slots = call(
        split_body, (pieces, pieces, small, jax.ShapeDtypeStruct((pairs, 8, LANES), F32)),
        [SMEM] + [ANY] * 3,
        loads + [pltpu.SMEM((pairs,), jnp.int32), pltpu.SemaphoreType.DMA(())],
        light * pairs, new_sector, couple, left_ops, right_ops, limit=52.5,
    )
    y, mx, part = call(
        first_body, (block, inner, small), [SMEM] + [VMEM] * 6, [], work,
        sector_states, slots, x0, x1, x2, lcat, rcat,
    )
    g = gathered(y, part)
    r0, c = call(
        first_residual_body, (block, small), [VMEM] * 3, [pltpu.VMEM(block.shape, F32)], light,
        g, x0, precond_diag,
    )
    r2, r1 = other(r0), paired(r0)
    y, mr, part = call(
        second_body, (block, inner, small), [SMEM] + [VMEM] * 8, room, work,
        sector_states, slots, r0, r1, r2, x0, g, lcat, rcat, away=(1,),
    )
    s = gathered(y, part)
    x, h, s0, c = call(
        second_residual_body, (block, block, block, small), [VMEM] * 6,
        [pltpu.VMEM(block.shape, F32)], light, s, g, x0, precond_diag, r0, c,
    )
    s2, s1 = other(s0), paired(s0)
    (mx,) = call(
        blend_body, (jax.ShapeDtypeStruct((pairs + 1, side, side), F32),), [VMEM] * 4, [],
        light, c, mx, mr, x,
    )
    nx = paired(mx)
    (ms,) = call(
        mix_body, (inner,), [VMEM] * 5, [], work // 2,
        slots, s0, s1, s2, lcat,
    )
    ns = paired(ms)
    many = jax.ShapeDtypeStruct((chunks * sectors, LANES), F32)
    (part,) = call(
        fold_body, (many,), [SMEM] + [VMEM] * 5, [pltpu.VMEM(block.shape, F32)], work // 2,
        sector_states, ms, s0, x, h, rcat,
    )
    parts = lax.all_to_all(part, ("ops", "sec"), 0, 0)
    (u,) = call(
        cross_body, (jax.ShapeDtypeStruct((3, pairs, side, side), F32),), [VMEM] * 7,
        [], work, flag, mx, nx, ms, ns, s0, s1,
    )
    return call(
        functools.partial(last_body, float((sectors * side * side) ** 0.5)),
        (
            jax.ShapeDtypeStruct((1, side, side), F32),
            jax.ShapeDtypeStruct((pairs, 1, side, side), F32),
        ),
        [VMEM] * 5, [], light, parts, c, mx, s0, u,
    )


def solution(mesh):
    in_specs = (
        P("sec"),
        P("sec", None, None),
        P("sec", None, None),
        P("ops", "sec", None, None),
        P("ops", "sec", None, None),
        P("ops", "sec"),
        P("sec"),
    )
    out_specs = (P("sec", None, None), P("ops", "sec", None, None))
    return jax.shard_map(local, mesh=mesh, in_specs=in_specs, out_specs=out_specs, check_vma=False)
```

```python
import functools

import jax
import jax.numpy as jnp
from jax import lax
from jax.experimental import pallas as pl
from jax.experimental.pallas import tpu as pltpu
from jax.sharding import PartitionSpec as P


LANES = 128
F32 = jnp.float32
BF16 = jnp.bfloat16
VMEM = pl.BlockSpec(memory_space=pltpu.VMEM)
ANY = pl.BlockSpec(memory_space=pl.ANY)
SMEM = pl.BlockSpec(memory_space=pltpu.SMEM)


def call(body, outs, in_specs, scratch, flops, *args, limit=8, away=()):
    size = sum(a.size * a.dtype.itemsize for a in args)
    size += sum(o.size * o.dtype.itemsize for o in outs)
    return pl.pallas_call(
        body,
        out_shape=tuple(pltpu.HBM(o.shape, o.dtype) if k in away else o for k, o in enumerate(outs)),
        in_specs=in_specs,
        out_specs=tuple(pl.BlockSpec(memory_space=pltpu.HBM) if k in away else VMEM for k in range(len(outs))),
        scratch_shapes=scratch,
        compiler_params=pltpu.CompilerParams(vmem_limit_bytes=int(limit * 1024 * 1024)),
        cost_estimate=pl.CostEstimate(flops=flops, bytes_accessed=size, transcendentals=0),
    )(*args)


def pack(ref, lead, block, value):
    rc = value.shape[0] // block[0]
    for o in range(block[0]):
        for j in range(value.shape[1] // LANES):
            ref[lead + (o, slice(j * rc, (j + 1) * rc))] = value[
                o * rc : (o + 1) * rc, j * LANES : (j + 1) * LANES
            ]


def unpack(value):
    chunks, cw, _ = value.shape
    groups = int((cw * chunks // LANES) ** 0.5)
    rc = cw // groups
    return jnp.concatenate(
        [
            jnp.concatenate([value[o, j * rc : (j + 1) * rc] for j in range(groups)], axis=1)
            for o in range(chunks)
        ],
        axis=0,
    )


def halves(value):
    high = value.astype(BF16)
    low = (value - high.astype(F32)).astype(BF16)
    return high, low


def dot(a, b):
    return jnp.dot(a, b, preferred_element_type=F32)


def three(ah, al, bh, bl):
    return dot(
        jnp.concatenate([ah, ah, al], axis=1), jnp.concatenate([bh, bl, bh], axis=0)
    )


def mask(size, side):
    rows = lax.broadcasted_iota(jnp.int32, (side, side), 0)
    cols = lax.broadcasted_iota(jnp.int32, (side, side), 1)
    return (rows < size) & (cols < size)


def pick(slot, blocks):
    value = jnp.zeros(blocks[0].shape, F32)
    for k, block in enumerate(blocks):
        value = jnp.where(slot == float(k), block[...], value)
    return unpack(value)


def fold(mixed, rcat_ref):
    total = None
    for p, one in enumerate(mixed):
        high, low = halves(one)
        term = three(high, low, rcat_ref[p, 0], rcat_ref[p, 1])
        total = term if total is None else total + term
    return total


def rows(value):
    return jnp.sum(value.reshape(-1, LANES), axis=0, keepdims=True)


def tile(parts):
    parts = parts + [jnp.zeros((8 - len(parts), LANES), F32)]
    return jnp.concatenate(parts, axis=0)


def lanes(value, out_ref):
    place = lax.broadcasted_iota(jnp.int32, (1, LANES), 1)
    sums = jnp.sum(value, axis=1, keepdims=True)
    row = jnp.zeros((1, LANES), F32)
    for k in range(value.shape[0]):
        row = jnp.where(place == k, sums[k : k + 1], row)
    out_ref[...] = jnp.broadcast_to(row, out_ref.shape)


def half_angle(middle, first, last):
    gap = last - first
    tilt = -2.0 * middle
    length = jnp.sqrt(gap * gap + tilt * tilt)
    safe = jnp.where(length > 0.0, length, 1.0)
    big = jnp.where(length > 0.0, jnp.sqrt(0.5 + 0.5 * jnp.abs(gap) / safe), 1.0)
    small = 0.5 * tilt / (safe * big)
    sign = jnp.where(tilt > 0.0, 1.0, -1.0)
    cosine = jnp.where(gap >= 0.0, big, jnp.abs(small))
    sine = jnp.where(gap >= 0.0, small, sign * big)
    return cosine, sine, 0.5 * (first + last) - 0.5 * length


def update(xx, first, xr, rr, rh, xhr, rhr):
    n = lax.rsqrt(rr - 2.0 * xr * xr + xr * xr * xx + 1e-06)
    middle = 0.5 * n * ((xhr - xr * first) + (rh - xr * first))
    last = n * n * (rhr - xr * rh - xr * xhr + xr * xr * first)
    cosine, sine, theta = half_angle(middle, first, last)
    on_r = sine * n
    on_x = cosine - on_r * xr
    xx = on_x * on_x * xx + 2.0 * on_x * on_r * xr + on_r * on_r * rr
    return on_x, on_r, theta, xx


def start_body(size_ref, psi_ref, x_ref, q_ref):
    live = mask(size_ref[0], psi_ref.shape[1])
    pack(x_ref, (), x_ref.shape, jnp.where(live, psi_ref[0].astype(F32), 0.0))
    x = x_ref[lax.axis_index("ops")]
    q_ref[...] = tile([rows(x * x)])


def split_pairs(left_ref, right_ref, lcat_ref, rcat_ref, left, right, sem):
    pairs = lcat_ref.shape[0]
    copies = []
    for p in range(pairs):
        copies.append(pltpu.make_async_copy(left_ref.at[p, 0], left.at[p], sem.at[2 * p]))
        copies.append(pltpu.make_async_copy(right_ref.at[p, 0], right.at[p], sem.at[2 * p + 1]))
    for copy in copies:
        copy.start()
    for p in range(pairs):
        copies[2 * p].wait()
        lcat_ref[p, 0], lcat_ref[p, 1] = halves(left[p])
        copies[2 * p + 1].wait()
        rcat_ref[p, 0], rcat_ref[p, 1] = halves(right[p].T)


def split_body(
    label_ref, couple_hbm, left_ref, right_ref, lcat_ref, rcat_ref, flag_ref, slot_ref,
    left, right, sem, couple_ref, mark,
):
    here = lax.axis_index("sec")
    copy = pltpu.make_async_copy(couple_hbm, couple_ref, mark)
    copy.start()
    split_pairs(left_ref, right_ref, lcat_ref, rcat_ref, left, right, sem)
    copy.wait()
    for p in range(lcat_ref.shape[0]):
        source = couple_ref[p]
        near = here + 1 - 2 * (here % 2)
        slot = jnp.where(source == here, 0.0, jnp.where(source == near, 1.0, 2.0))
        slot_ref[p] = jnp.full(slot_ref.shape[1:], jnp.where(source >= 0, slot, -1.0))
    flag_ref[...] = jnp.full(flag_ref.shape, jnp.where(label_ref[0] == here, 1.0, 0.0))


def mix_all(slot_ref, blocks, lcat_ref, m_ref):
    mixed = []
    for p in range(lcat_ref.shape[0]):
        high, low = halves(pick(slot_ref[p, 0:1, 0:1][None], blocks))
        mixed.append(three(lcat_ref[p, 0], lcat_ref[p, 1], high, low))
        m_ref[p] = mixed[p]
    return mixed


def fold_all(size_ref, mixed, rcat_ref, y_ref):
    y = fold(mixed, rcat_ref)
    pack(y_ref, (), y_ref.shape, jnp.where(mask(size_ref[0], y.shape[0]), y, 0.0))
    return y_ref[...]


def first_body(
    size_ref, slot_ref, x0, x1, x2, q_ref, p_ref, lcat_ref, rcat_ref, y_ref, m_ref, part_ref
):
    mixed = mix_all(slot_ref, (x0, x1, x2), lcat_ref, m_ref)
    y = fold_all(size_ref, mixed, rcat_ref, y_ref)
    squares = 0.5 * (q_ref[0:1] + p_ref[0:1])
    part_ref[...] = tile([squares, rows(x0[...] * y)])


def five(x0, r0, h0, y):
    o = lax.axis_index("ops")
    x, r, h = x0[o], r0[o], h0[o][: x0.shape[1]]
    return tile([rows(x * r), rows(r * r), rows(r * h), rows(x0[...] * y), rows(r0[...] * y)])


def second_body(
    size_ref, slot_ref, r0, r1, r2, x0, g0, lcat_ref, rcat_ref, y_ref, m_out, part_ref,
    m_ref, sem,
):
    mixed = mix_all(slot_ref, (r0, r1, r2), lcat_ref, m_ref)
    copy = pltpu.make_async_copy(m_ref, m_out, sem)
    copy.start()
    part_ref[...] = five(x0, r0, g0, fold_all(size_ref, mixed, rcat_ref, y_ref))
    copy.wait()


def mix_body(slot_ref, r0, r1, r2, lcat_ref, m_ref):
    mix_all(slot_ref, (r0, r1, r2), lcat_ref, m_ref)


def fold_body(size_ref, m_ref, r0, x0, h0, rcat_ref, part_ref, y_ref):
    mixed = [m_ref[p] for p in range(m_ref.shape[0])]
    lanes(five(x0, r0, h0, fold_all(size_ref, mixed, rcat_ref, y_ref)), part_ref)


def blend_body(c_in, a_ref, b_ref, x_ref, out_ref):
    pairs = a_ref.shape[0]
    out_ref[:pairs] = c_in[2:3, 0:1] * a_ref[...] + c_in[3:4, 0:1] * b_ref[...]
    out_ref[pairs] = unpack(x_ref[...])


def cross_body(flag_ref, b_ref, n_ref, m_ref, w_ref, s0, s1, u_ref):
    stay = flag_ref[0:1, 0:1] > 0.5
    pairs, side, _ = m_ref.shape
    new = unpack(jnp.where(stay[None], s0[...], s1[...]))
    x = jnp.where(stay, b_ref[pairs], n_ref[pairs])
    left = jnp.concatenate([x.T, new.T], axis=0)
    lh, ll = halves(left)
    for p in range(pairs):
        old, new = jnp.where(stay, b_ref[p], n_ref[p]), jnp.where(stay, m_ref[p], w_ref[p])
        rh, rl = halves(jnp.concatenate([old, new], axis=1))
        both = three(lh, ll, rh, rl)
        u_ref[0, p] = both[:side, :side]
        u_ref[1, p] = both[:side, side:] + both[side:, :side]
        u_ref[2, p] = both[side:, side:]


def sum_body(terms_ref, mine, *refs):
    others, out_ref = refs[:-1], refs[-1]
    cw = terms_ref.shape[1]
    block = jnp.sum(terms_ref[...], axis=0)
    scalars = mine[...]
    for one in others:
        scalars = scalars + one[...]
    for o in range(out_ref.shape[0]):
        out_ref[o, :cw] = block
        out_ref[o, cw:] = scalars


def numbers(tiles, count):
    total = jnp.sum(jnp.sum(tiles, axis=0), axis=1, keepdims=True)
    return [total[i : i + 1] for i in range(count)]


def store(out_ref, values):
    out_ref[...] = tile([jnp.broadcast_to(v, (1, LANES)) for v in values])


def first_residual_body(g_ref, x_ref, diag_ref, r_ref, c_ref, d_ref):
    pack(d_ref, (), d_ref.shape, diag_ref[0].astype(F32))
    cw = x_ref.shape[1]
    squares, energy = numbers(g_ref[:, cw:], 2)
    factor = lax.rsqrt(squares + 1e-06)
    theta = energy * factor * factor
    r = factor * (g_ref[:, :cw] - theta * x_ref[...]) / (jnp.abs(d_ref[...] - theta) + 1.0)
    r_ref[...] = r
    store(c_ref, [factor, theta, squares * factor * factor])


def second_residual_body(
    s_ref, g_ref, x_ref, diag_ref, r_in, c_in, x_out, h_out, r_ref, c_ref, d_ref
):
    pack(d_ref, (), d_ref.shape, diag_ref[0].astype(F32))
    cw = x_ref.shape[1]
    xr, rr, rh, xhr, rhr = numbers(s_ref[:, cw:], 5)
    factor, first, xx = c_in[0:1, 0:1], c_in[1:2, 0:1], c_in[2:3, 0:1]
    on_x, on_r, theta, xx = update(
        xx, first, factor * xr, rr, factor * rh, factor * xhr, rhr
    )
    on_x = on_x * factor
    x = on_x * x_ref[...] + on_r * r_in[...]
    h = on_x * g_ref[:, :cw] + on_r * s_ref[:, :cw]
    x_out[...] = x
    h_out[...] = h
    r_ref[...] = (h - theta * x) / (jnp.abs(d_ref[...] - theta) + 1.0)
    store(c_ref, [theta, xx, on_x, on_r])


def last_body(scale, parts_ref, c_in, b_ref, s0, u_ref, wave_ref, turn_ref):
    pairs, side = u_ref.shape[1:3]
    total = jnp.sum(parts_ref[...], axis=0, keepdims=True)
    xr, rr, rh, xhr, rhr = [total[:, k : k + 1] for k in range(5)]
    on_x, on_s, _, _ = update(c_in[1:2, 0:1], c_in[0:1, 0:1], xr, rr, rh, xhr, rhr)
    on_x = on_x * scale
    on_s = on_s * scale
    wave_ref[0] = on_x * b_ref[pairs] + unpack(on_s * s0[...])
    root = 1.0 / side**0.5
    xx, xs, ss = on_x * on_x * root, on_x * on_s * root, on_s * on_s * root
    for p in range(pairs):
        turn_ref[p, 0] = xx * u_ref[0, p] + xs * u_ref[1, p] + ss * u_ref[2, p]


def paired(value):
    count = lax.axis_size("sec")
    return lax.ppermute(value, "sec", [(i, i ^ 1) for i in range(count)])


def other(value):
    count, groups = lax.axis_size("sec"), lax.axis_size("ops")
    route = []
    for o in range(groups):
        for i in range(1, count - 1, 2):
            route += [(o * count + i, o * count + i + 1), (o * count + i + 1, o * count + i)]
        if groups % 2 == 0:
            route += [(o * count + i, (o ^ 1) * count + i) for i in (0, count - 1)]
    return lax.ppermute(value, ("ops", "sec"), route)


def across(value):
    count = lax.axis_size("ops")
    return lax.ppermute(value, "ops", [(i, (i + count // 2) % count) for i in range(count)])


def last_step(count):
    step = 1
    while step * 4 < count:
        step *= 4
    return step


def over_sectors(value):
    count = lax.axis_size("sec")
    step = 1
    while True:
        last = step == last_step(count)
        found = []
        for d in range(1, min(4, count // step)):
            route = [(i, i ^ (d * step)) for i in range(count)]
            found.append(lax.ppermute(value, "sec", route))
        if last:
            return value, found
        for one in found:
            value = value + one
        step *= 4


def exchange(value):
    return lax.all_to_all(value, "ops", 0, 0)


def local(sector_states, psi_guess, precond_diag, left_ops, right_ops, couple, new_sector):
    side = psi_guess.shape[1]
    pairs = left_ops.shape[0]
    couple = couple.reshape(pairs)
    chunks = lax.axis_size("ops")
    sectors = lax.axis_size("sec")
    cw = side // chunks * side // LANES
    block = jax.ShapeDtypeStruct((chunks, cw, LANES), F32)
    wide = jax.ShapeDtypeStruct((chunks, cw + 8, LANES), F32)
    small = jax.ShapeDtypeStruct((8, LANES), F32)
    inner = jax.ShapeDtypeStruct((pairs, side, side), F32)
    room = [pltpu.VMEM(inner.shape, F32), pltpu.SemaphoreType.DMA(())]
    pieces = jax.ShapeDtypeStruct((pairs, 2, side, side), BF16)
    loads = [pltpu.VMEM((pairs, side, side), F32)] * 2 + [pltpu.SemaphoreType.DMA((2 * pairs,))]
    work = 12 * pairs * side**3
    light = 20 * side**2

    def gathered(y, part):
        part, others = over_sectors(part)
        (full,) = call(
            sum_body, (wide,), [VMEM] * (2 + len(others)), [], light,
            exchange(y), part, *others,
        )
        return exchange(full)

    x0, q = call(start_body, (block, small), [SMEM, VMEM], [], light, sector_states, psi_guess)
    x2, x1 = other(x0), paired(x0)
    p = across(q)
    lcat, rcat, flag, slots = call(
        split_body, (pieces, pieces, small, jax.ShapeDtypeStruct((pairs, 8, LANES), F32)),
        [SMEM] + [ANY] * 3,
        loads + [pltpu.SMEM((pairs,), jnp.int32), pltpu.SemaphoreType.DMA(())],
        light * pairs, new_sector, couple, left_ops, right_ops, limit=52.5,
    )
    y, mx, part = call(
        first_body, (block, inner, small), [SMEM] + [VMEM] * 8, [], work,
        sector_states, slots, x0, x1, x2, q, p, lcat, rcat,
    )
    g = gathered(y, part)
    r0, c = call(
        first_residual_body, (block, small), [VMEM] * 3, [pltpu.VMEM(block.shape, F32)], light,
        g, x0, precond_diag,
    )
    r2, r1 = other(r0), paired(r0)
    y, mr, part = call(
        second_body, (block, inner, small), [SMEM] + [VMEM] * 8, room, work,
        sector_states, slots, r0, r1, r2, x0, g, lcat, rcat, away=(1,),
    )
    s = gathered(y, part)
    x, h, s0, c = call(
        second_residual_body, (block, block, block, small), [VMEM] * 6,
        [pltpu.VMEM(block.shape, F32)], light, s, g, x0, precond_diag, r0, c,
    )
    s2, s1 = other(s0), paired(s0)
    (mx,) = call(
        blend_body, (jax.ShapeDtypeStruct((pairs + 1, side, side), F32),), [VMEM] * 4, [],
        light, c, mx, mr, x,
    )
    nx = paired(mx)
    (ms,) = call(
        mix_body, (inner,), [VMEM] * 5, [], work // 2,
        slots, s0, s1, s2, lcat,
    )
    ns = paired(ms)
    many = jax.ShapeDtypeStruct((chunks * sectors, LANES), F32)
    (part,) = call(
        fold_body, (many,), [SMEM] + [VMEM] * 5, [pltpu.VMEM(block.shape, F32)], work // 2,
        sector_states, ms, s0, x, h, rcat,
    )
    parts = lax.all_to_all(part, ("ops", "sec"), 0, 0)
    (u,) = call(
        cross_body, (jax.ShapeDtypeStruct((3, pairs, side, side), F32),), [VMEM] * 7,
        [], work, flag, mx, nx, ms, ns, s0, s1,
    )
    return call(
        functools.partial(last_body, float((sectors * side * side) ** 0.5)),
        (
            jax.ShapeDtypeStruct((1, side, side), F32),
            jax.ShapeDtypeStruct((pairs, 1, side, side), F32),
        ),
        [VMEM] * 5, [], light, parts, c, mx, s0, u,
    )


def solution(mesh):
    in_specs = (
        P("sec"),
        P("sec", None, None),
        P("sec", None, None),
        P("ops", "sec", None, None),
        P("ops", "sec", None, None),
        P("ops", "sec"),
        P("sec"),
    )
    out_specs = (P("sec", None, None), P("ops", "sec", None, None))
    return jax.shard_map(local, mesh=mesh, in_specs=in_specs, out_specs=out_specs, check_vma=False)
```

```python
import functools

import jax
import jax.numpy as jnp
from jax import lax
from jax.experimental import pallas as pl
from jax.experimental.pallas import tpu as pltpu
from jax.sharding import PartitionSpec as P


LANES = 128
F32 = jnp.float32
BF16 = jnp.bfloat16
VMEM = pl.BlockSpec(memory_space=pltpu.VMEM)
ANY = pl.BlockSpec(memory_space=pl.ANY)
SMEM = pl.BlockSpec(memory_space=pltpu.SMEM)


def call(body, outs, in_specs, scratch, flops, *args, limit=8, away=()):
    size = sum(a.size * a.dtype.itemsize for a in args)
    size += sum(o.size * o.dtype.itemsize for o in outs)
    return pl.pallas_call(
        body,
        out_shape=tuple(pltpu.HBM(o.shape, o.dtype) if k in away else o for k, o in enumerate(outs)),
        in_specs=in_specs,
        out_specs=tuple(pl.BlockSpec(memory_space=pltpu.HBM) if k in away else VMEM for k in range(len(outs))),
        scratch_shapes=scratch,
        compiler_params=pltpu.CompilerParams(vmem_limit_bytes=int(limit * 1024 * 1024)),
        cost_estimate=pl.CostEstimate(flops=flops, bytes_accessed=size, transcendentals=0),
    )(*args)


def pack(ref, lead, block, value):
    rc = value.shape[0] // block[0]
    for o in range(block[0]):
        for j in range(value.shape[1] // LANES):
            ref[lead + (o, slice(j * rc, (j + 1) * rc))] = value[
                o * rc : (o + 1) * rc, j * LANES : (j + 1) * LANES
            ]


def unpack(value):
    chunks, cw, _ = value.shape
    groups = int((cw * chunks // LANES) ** 0.5)
    rc = cw // groups
    return jnp.concatenate(
        [
            jnp.concatenate([value[o, j * rc : (j + 1) * rc] for j in range(groups)], axis=1)
            for o in range(chunks)
        ],
        axis=0,
    )


def halves(value):
    high = value.astype(BF16)
    low = (value - high.astype(F32)).astype(BF16)
    return high, low


def dot(a, b):
    return jnp.dot(a, b, preferred_element_type=F32)


def three(ah, al, bh, bl):
    return dot(
        jnp.concatenate([ah, ah, al], axis=1), jnp.concatenate([bh, bl, bh], axis=0)
    )


def mask(size, side):
    rows = lax.broadcasted_iota(jnp.int32, (side, side), 0)
    cols = lax.broadcasted_iota(jnp.int32, (side, side), 1)
    return (rows < size) & (cols < size)


def pick(slot, blocks):
    value = jnp.zeros(blocks[0].shape, F32)
    for k, block in enumerate(blocks):
        value = jnp.where(slot == float(k), block[...], value)
    return unpack(value)


def fold(mixed, rcat_ref):
    total = None
    for p, one in enumerate(mixed):
        high, low = halves(one)
        term = three(high, low, rcat_ref[p, 0], rcat_ref[p, 1])
        total = term if total is None else total + term
    return total


def rows(value):
    return jnp.sum(value.reshape(-1, LANES), axis=0, keepdims=True)


def tile(parts):
    parts = parts + [jnp.zeros((8 - len(parts), LANES), F32)]
    return jnp.concatenate(parts, axis=0)


def lanes(value, out_ref):
    place = lax.broadcasted_iota(jnp.int32, (1, LANES), 1)
    sums = jnp.sum(value, axis=1, keepdims=True)
    row = jnp.zeros((1, LANES), F32)
    for k in range(value.shape[0]):
        row = jnp.where(place == k, sums[k : k + 1], row)
    out_ref[...] = jnp.broadcast_to(row, out_ref.shape)


def half_angle(middle, first, last):
    gap = last - first
    tilt = -2.0 * middle
    length = jnp.sqrt(gap * gap + tilt * tilt)
    safe = jnp.where(length > 0.0, length, 1.0)
    big = jnp.where(length > 0.0, jnp.sqrt(0.5 + 0.5 * jnp.abs(gap) / safe), 1.0)
    small = 0.5 * tilt / (safe * big)
    sign = jnp.where(tilt > 0.0, 1.0, -1.0)
    cosine = jnp.where(gap >= 0.0, big, jnp.abs(small))
    sine = jnp.where(gap >= 0.0, small, sign * big)
    return cosine, sine, 0.5 * (first + last) - 0.5 * length


def update(xx, first, xr, rr, rh, xhr, rhr):
    n = lax.rsqrt(rr - 2.0 * xr * xr + xr * xr * xx + 1e-06)
    middle = 0.5 * n * ((xhr - xr * first) + (rh - xr * first))
    last = n * n * (rhr - xr * rh - xr * xhr + xr * xr * first)
    cosine, sine, theta = half_angle(middle, first, last)
    on_r = sine * n
    on_x = cosine - on_r * xr
    xx = on_x * on_x * xx + 2.0 * on_x * on_r * xr + on_r * on_r * rr
    return on_x, on_r, theta, xx


def start_body(size_ref, psi_ref, x_ref):
    live = mask(size_ref[0], psi_ref.shape[1])
    pack(x_ref, (), x_ref.shape, jnp.where(live, psi_ref[0].astype(F32), 0.0))


def split_pairs(left_ref, right_ref, lcat_ref, rcat_ref, left, right, sem):
    pairs = lcat_ref.shape[0]
    copies = []
    for p in range(pairs):
        copies.append(pltpu.make_async_copy(left_ref.at[p, 0], left.at[p], sem.at[2 * p]))
        copies.append(pltpu.make_async_copy(right_ref.at[p, 0], right.at[p], sem.at[2 * p + 1]))
    for copy in copies:
        copy.start()
    for p in range(pairs):
        copies[2 * p].wait()
        lcat_ref[p, 0], lcat_ref[p, 1] = halves(left[p])
        copies[2 * p + 1].wait()
        rcat_ref[p, 0], rcat_ref[p, 1] = halves(right[p].T)


def split_body(
    label_ref, couple_hbm, left_ref, right_ref, lcat_ref, rcat_ref, flag_ref, slot_ref,
    left, right, sem, couple_ref, mark,
):
    here = lax.axis_index("sec")
    copy = pltpu.make_async_copy(couple_hbm, couple_ref, mark)
    copy.start()
    split_pairs(left_ref, right_ref, lcat_ref, rcat_ref, left, right, sem)
    copy.wait()
    for p in range(lcat_ref.shape[0]):
        source = couple_ref[p]
        near = here + 1 - 2 * (here % 2)
        slot = jnp.where(source == here, 0.0, jnp.where(source == near, 1.0, 2.0))
        slot_ref[p] = jnp.full(slot_ref.shape[1:], jnp.where(source >= 0, slot, -1.0))
    flag_ref[...] = jnp.full(flag_ref.shape, jnp.where(label_ref[0] == here, 1.0, 0.0))


def mix_all(slot_ref, blocks, lcat_ref, m_ref):
    mixed = []
    for p in range(lcat_ref.shape[0]):
        high, low = halves(pick(slot_ref[p, 0:1, 0:1][None], blocks))
        mixed.append(three(lcat_ref[p, 0], lcat_ref[p, 1], high, low))
        m_ref[p] = mixed[p]
    return mixed


def fold_all(size_ref, mixed, rcat_ref, y_ref):
    y = fold(mixed, rcat_ref)
    pack(y_ref, (), y_ref.shape, jnp.where(mask(size_ref[0], y.shape[0]), y, 0.0))
    return y_ref[...]


def first_body(size_ref, slot_ref, x0, x1, x2, lcat_ref, rcat_ref, y_ref, m_ref, part_ref):
    mixed = mix_all(slot_ref, (x0, x1, x2), lcat_ref, m_ref)
    y = fold_all(size_ref, mixed, rcat_ref, y_ref)
    x = x0[lax.axis_index("ops")]
    part_ref[...] = tile([rows(x * x), rows(x0[...] * y)])


def five(x0, r0, h0, y):
    o = lax.axis_index("ops")
    x, r, h = x0[o], r0[o], h0[o][: x0.shape[1]]
    return tile([rows(x * r), rows(r * r), rows(r * h), rows(x0[...] * y), rows(r0[...] * y)])


def second_body(
    size_ref, slot_ref, r0, r1, r2, x0, g0, lcat_ref, rcat_ref, y_ref, m_out, part_ref,
    m_ref, sem,
):
    mixed = mix_all(slot_ref, (r0, r1, r2), lcat_ref, m_ref)
    copy = pltpu.make_async_copy(m_ref, m_out, sem)
    copy.start()
    part_ref[...] = five(x0, r0, g0, fold_all(size_ref, mixed, rcat_ref, y_ref))
    copy.wait()


def mix_body(slot_ref, r0, r1, r2, lcat_ref, m_ref):
    mix_all(slot_ref, (r0, r1, r2), lcat_ref, m_ref)


def fold_body(size_ref, m_ref, r0, x0, h0, rcat_ref, part_ref, y_ref):
    mixed = [m_ref[p] for p in range(m_ref.shape[0])]
    lanes(five(x0, r0, h0, fold_all(size_ref, mixed, rcat_ref, y_ref)), part_ref)


def blend_body(c_in, a_ref, b_ref, x_ref, out_ref):
    pairs = a_ref.shape[0]
    out_ref[:pairs] = c_in[2:3, 0:1] * a_ref[...] + c_in[3:4, 0:1] * b_ref[...]
    out_ref[pairs] = unpack(x_ref[...])


def cross_body(flag_ref, b_ref, n_ref, m_ref, w_ref, s0, s1, u_ref):
    stay = flag_ref[0:1, 0:1] > 0.5
    pairs, side, _ = m_ref.shape
    new = unpack(jnp.where(stay[None], s0[...], s1[...]))
    x = jnp.where(stay, b_ref[pairs], n_ref[pairs])
    left = jnp.concatenate([x.T, new.T], axis=0)
    lh, ll = halves(left)
    for p in range(pairs):
        old, new = jnp.where(stay, b_ref[p], n_ref[p]), jnp.where(stay, m_ref[p], w_ref[p])
        rh, rl = halves(jnp.concatenate([old, new], axis=1))
        both = three(lh, ll, rh, rl)
        u_ref[0, p] = both[:side, :side]
        u_ref[1, p] = both[:side, side:] + both[side:, :side]
        u_ref[2, p] = both[side:, side:]


def sum_body(terms_ref, mine, *refs):
    others, out_ref = refs[:-1], refs[-1]
    cw = terms_ref.shape[1]
    block = jnp.sum(terms_ref[...], axis=0)
    scalars = mine[...]
    for one in others:
        scalars = scalars + one[...]
    for o in range(out_ref.shape[0]):
        out_ref[o, :cw] = block
        out_ref[o, cw:] = scalars


def numbers(tiles, count):
    total = jnp.sum(jnp.sum(tiles, axis=0), axis=1, keepdims=True)
    return [total[i : i + 1] for i in range(count)]


def store(out_ref, values):
    out_ref[...] = tile([jnp.broadcast_to(v, (1, LANES)) for v in values])


def first_residual_body(g_ref, x_ref, diag_ref, r_ref, c_ref, d_ref):
    pack(d_ref, (), d_ref.shape, diag_ref[0].astype(F32))
    cw = x_ref.shape[1]
    squares, energy = numbers(g_ref[:, cw:], 2)
    factor = lax.rsqrt(squares + 1e-06)
    theta = energy * factor * factor
    r = factor * (g_ref[:, :cw] - theta * x_ref[...]) / (jnp.abs(d_ref[...] - theta) + 1.0)
    r_ref[...] = r
    store(c_ref, [factor, theta, squares * factor * factor])


def second_residual_body(
    s_ref, g_ref, x_ref, diag_ref, r_in, c_in, x_out, h_out, r_ref, c_ref, d_ref
):
    pack(d_ref, (), d_ref.shape, diag_ref[0].astype(F32))
    cw = x_ref.shape[1]
    xr, rr, rh, xhr, rhr = numbers(s_ref[:, cw:], 5)
    factor, first, xx = c_in[0:1, 0:1], c_in[1:2, 0:1], c_in[2:3, 0:1]
    on_x, on_r, theta, xx = update(
        xx, first, factor * xr, rr, factor * rh, factor * xhr, rhr
    )
    on_x = on_x * factor
    x = on_x * x_ref[...] + on_r * r_in[...]
    h = on_x * g_ref[:, :cw] + on_r * s_ref[:, :cw]
    x_out[...] = x
    h_out[...] = h
    r_ref[...] = (h - theta * x) / (jnp.abs(d_ref[...] - theta) + 1.0)
    store(c_ref, [theta, xx, on_x, on_r])


def last_body(scale, parts_ref, c_in, b_ref, s0, u_ref, wave_ref, turn_ref):
    pairs, side = u_ref.shape[1:3]
    total = jnp.sum(parts_ref[...], axis=0, keepdims=True)
    xr, rr, rh, xhr, rhr = [total[:, k : k + 1] for k in range(5)]
    on_x, on_s, _, _ = update(c_in[1:2, 0:1], c_in[0:1, 0:1], xr, rr, rh, xhr, rhr)
    on_x = on_x * scale
    on_s = on_s * scale
    wave_ref[0] = on_x * b_ref[pairs] + unpack(on_s * s0[...])
    root = 1.0 / side**0.5
    xx, xs, ss = on_x * on_x * root, on_x * on_s * root, on_s * on_s * root
    for p in range(pairs):
        turn_ref[p, 0] = xx * u_ref[0, p] + xs * u_ref[1, p] + ss * u_ref[2, p]


def paired(value):
    count = lax.axis_size("sec")
    return lax.ppermute(value, "sec", [(i, i ^ 1) for i in range(count)])


def other(value, stage):
    count, groups = lax.axis_size("sec"), lax.axis_size("ops")
    route = []
    for o in range(groups):
        for i in range(1, count - 1, 2):
            route += [(o * count + i, o * count + i + 1), (o * count + i + 1, o * count + i)]
        if groups % 2 == 0 and stage < 2:
            route += [(o * count + i, (o ^ 1) * count + i) for i in (0, count - 1)]
    return lax.ppermute(value, ("ops", "sec"), route)


def last_step(count):
    step = 1
    while step * 4 < count:
        step *= 4
    return step


def over_sectors(value):
    count = lax.axis_size("sec")
    step = 1
    while True:
        last = step == last_step(count)
        found = []
        for d in range(1, min(4, count // step)):
            route = [(i, i ^ (d * step)) for i in range(count)]
            found.append(lax.ppermute(value, "sec", route))
        if last:
            return value, found
        for one in found:
            value = value + one
        step *= 4


def exchange(value):
    return lax.all_to_all(value, "ops", 0, 0)


def local(sector_states, psi_guess, precond_diag, left_ops, right_ops, couple, new_sector):
    side = psi_guess.shape[1]
    pairs = left_ops.shape[0]
    couple = couple.reshape(pairs)
    chunks = lax.axis_size("ops")
    sectors = lax.axis_size("sec")
    cw = side // chunks * side // LANES
    block = jax.ShapeDtypeStruct((chunks, cw, LANES), F32)
    wide = jax.ShapeDtypeStruct((chunks, cw + 8, LANES), F32)
    small = jax.ShapeDtypeStruct((8, LANES), F32)
    inner = jax.ShapeDtypeStruct((pairs, side, side), F32)
    room = [pltpu.VMEM(inner.shape, F32), pltpu.SemaphoreType.DMA(())]
    pieces = jax.ShapeDtypeStruct((pairs, 2, side, side), BF16)
    loads = [pltpu.VMEM((pairs, side, side), F32)] * 2 + [pltpu.SemaphoreType.DMA((2 * pairs,))]
    work = 12 * pairs * side**3
    light = 20 * side**2

    def gathered(y, part):
        part, others = over_sectors(part)
        (full,) = call(
            sum_body, (wide,), [VMEM] * (2 + len(others)), [], light,
            exchange(y), part, *others,
        )
        return exchange(full)

    (x0,) = call(start_body, (block,), [SMEM, VMEM], [], light, sector_states, psi_guess)
    x2, x1 = other(x0, 0), paired(x0)
    lcat, rcat, flag, slots = call(
        split_body, (pieces, pieces, small, jax.ShapeDtypeStruct((pairs, 8, LANES), F32)),
        [SMEM] + [ANY] * 3,
        loads + [pltpu.SMEM((pairs,), jnp.int32), pltpu.SemaphoreType.DMA(())],
        light * pairs, new_sector, couple, left_ops, right_ops, limit=52.5,
    )
    y, mx, part = call(
        first_body, (block, inner, small), [SMEM] + [VMEM] * 6, [], work,
        sector_states, slots, x0, x1, x2, lcat, rcat,
    )
    g = gathered(y, part)
    r0, c = call(
        first_residual_body, (block, small), [VMEM] * 3, [pltpu.VMEM(block.shape, F32)], light,
        g, x0, precond_diag,
    )
    r2, r1 = other(r0, 1), paired(r0)
    y, mr, part = call(
        second_body, (block, inner, small), [SMEM] + [VMEM] * 8, room, work,
        sector_states, slots, r0, r1, r2, x0, g, lcat, rcat, away=(1,),
    )
    s = gathered(y, part)
    x, h, s0, c = call(
        second_residual_body, (block, block, block, small), [VMEM] * 6,
        [pltpu.VMEM(block.shape, F32)], light, s, g, x0, precond_diag, r0, c,
    )
    s2, s1 = other(s0, 2), paired(s0)
    (mx,) = call(
        blend_body, (jax.ShapeDtypeStruct((pairs + 1, side, side), F32),), [VMEM] * 4, [],
        light, c, mx, mr, x,
    )
    nx = paired(mx)
    (ms,) = call(
        mix_body, (inner,), [VMEM] * 5, [], work // 2,
        slots, s0, s1, s2, lcat,
    )
    ns = paired(ms)
    many = jax.ShapeDtypeStruct((chunks * sectors, LANES), F32)
    (part,) = call(
        fold_body, (many,), [SMEM] + [VMEM] * 5, [pltpu.VMEM(block.shape, F32)], work // 2,
        sector_states, ms, s0, x, h, rcat,
    )
    parts = lax.all_to_all(part, ("ops", "sec"), 0, 0)
    (u,) = call(
        cross_body, (jax.ShapeDtypeStruct((3, pairs, side, side), F32),), [VMEM] * 7,
        [], work, flag, mx, nx, ms, ns, s0, s1,
    )
    return call(
        functools.partial(last_body, float((sectors * side * side) ** 0.5)),
        (
            jax.ShapeDtypeStruct((1, side, side), F32),
            jax.ShapeDtypeStruct((pairs, 1, side, side), F32),
        ),
        [VMEM] * 5, [], light, parts, c, mx, s0, u,
    )


def solution(mesh):
    in_specs = (
        P("sec"),
        P("sec", None, None),
        P("sec", None, None),
        P("ops", "sec", None, None),
        P("ops", "sec", None, None),
        P("ops", "sec"),
        P("sec"),
    )
    out_specs = (P("sec", None, None), P("ops", "sec", None, None))
    return jax.shard_map(local, mesh=mesh, in_specs=in_specs, out_specs=out_specs, check_vma=False)
```

```python
import functools

import jax
import jax.numpy as jnp
from jax import lax
from jax.experimental import pallas as pl
from jax.experimental.pallas import tpu as pltpu
from jax.sharding import PartitionSpec as P


LANES = 128
F32 = jnp.float32
BF16 = jnp.bfloat16
VMEM = pl.BlockSpec(memory_space=pltpu.VMEM)
ANY = pl.BlockSpec(memory_space=pl.ANY)
SMEM = pl.BlockSpec(memory_space=pltpu.SMEM)


def call(body, outs, in_specs, scratch, flops, *args, limit=8, away=()):
    size = sum(a.size * a.dtype.itemsize for a in args)
    size += sum(o.size * o.dtype.itemsize for o in outs)
    return pl.pallas_call(
        body,
        out_shape=tuple(pltpu.HBM(o.shape, o.dtype) if k in away else o for k, o in enumerate(outs)),
        in_specs=in_specs,
        out_specs=tuple(pl.BlockSpec(memory_space=pltpu.HBM) if k in away else VMEM for k in range(len(outs))),
        scratch_shapes=scratch,
        compiler_params=pltpu.CompilerParams(vmem_limit_bytes=int(limit * 1024 * 1024)),
        cost_estimate=pl.CostEstimate(flops=flops, bytes_accessed=size, transcendentals=0),
    )(*args)


def pack(ref, lead, block, value):
    rc = value.shape[0] // block[0]
    for o in range(block[0]):
        for j in range(value.shape[1] // LANES):
            ref[lead + (o, slice(j * rc, (j + 1) * rc))] = value[
                o * rc : (o + 1) * rc, j * LANES : (j + 1) * LANES
            ]


def unpack(value):
    chunks, cw, _ = value.shape
    groups = int((cw * chunks // LANES) ** 0.5)
    rc = cw // groups
    return jnp.concatenate(
        [
            jnp.concatenate([value[o, j * rc : (j + 1) * rc] for j in range(groups)], axis=1)
            for o in range(chunks)
        ],
        axis=0,
    )


def halves(value):
    high = value.astype(BF16)
    low = (value - high.astype(F32)).astype(BF16)
    return high, low


def dot(a, b):
    return jnp.dot(a, b, preferred_element_type=F32)


def three(ah, al, bh, bl):
    return dot(
        jnp.concatenate([ah, ah, al], axis=1), jnp.concatenate([bh, bl, bh], axis=0)
    )


def mask(size, side):
    rows = lax.broadcasted_iota(jnp.int32, (side, side), 0)
    cols = lax.broadcasted_iota(jnp.int32, (side, side), 1)
    return (rows < size) & (cols < size)


def pick(slot, blocks):
    value = jnp.zeros(blocks[0].shape, F32)
    for k, block in enumerate(blocks):
        value = jnp.where(slot == float(k), block[...], value)
    return unpack(value)


def fold(mixed, rcat_ref):
    total = None
    for p, one in enumerate(mixed):
        high, low = halves(one)
        term = three(high, low, rcat_ref[p, 0], rcat_ref[p, 1])
        total = term if total is None else total + term
    return total


def rows(value):
    return jnp.sum(value.reshape(-1, LANES), axis=0, keepdims=True)


def tile(parts):
    parts = parts + [jnp.zeros((8 - len(parts), LANES), F32)]
    return jnp.concatenate(parts, axis=0)


def lanes(value, out_ref):
    place = lax.broadcasted_iota(jnp.int32, (1, LANES), 1)
    sums = jnp.sum(value, axis=1, keepdims=True)
    row = jnp.zeros((1, LANES), F32)
    for k in range(value.shape[0]):
        row = jnp.where(place == k, sums[k : k + 1], row)
    out_ref[...] = jnp.broadcast_to(row, out_ref.shape)


def half_angle(middle, first, last):
    gap = last - first
    tilt = -2.0 * middle
    length = jnp.sqrt(gap * gap + tilt * tilt)
    safe = jnp.where(length > 0.0, length, 1.0)
    big = jnp.where(length > 0.0, jnp.sqrt(0.5 + 0.5 * jnp.abs(gap) / safe), 1.0)
    small = 0.5 * tilt / (safe * big)
    sign = jnp.where(tilt > 0.0, 1.0, -1.0)
    cosine = jnp.where(gap >= 0.0, big, jnp.abs(small))
    sine = jnp.where(gap >= 0.0, small, sign * big)
    return cosine, sine, 0.5 * (first + last) - 0.5 * length


def update(xx, first, xr, rr, rh, xhr, rhr):
    n = lax.rsqrt(rr - 2.0 * xr * xr + xr * xr * xx + 1e-06)
    middle = 0.5 * n * ((xhr - xr * first) + (rh - xr * first))
    last = n * n * (rhr - xr * rh - xr * xhr + xr * xr * first)
    cosine, sine, theta = half_angle(middle, first, last)
    on_r = sine * n
    on_x = cosine - on_r * xr
    xx = on_x * on_x * xx + 2.0 * on_x * on_r * xr + on_r * on_r * rr
    return on_x, on_r, theta, xx


def start_body(size_ref, psi_hbm, x_ref, psi_ref, sem):
    copy = pltpu.make_async_copy(psi_hbm.at[0], psi_ref, sem)
    copy.start()
    live = mask(size_ref[0], psi_ref.shape[0])
    copy.wait()
    pack(x_ref, (), x_ref.shape, jnp.where(live, psi_ref[...].astype(F32), 0.0))


def split_pairs(left_ref, right_ref, lcat_ref, rcat_ref, left, right, sem):
    pairs = lcat_ref.shape[0]
    copies = []
    for p in range(pairs):
        copies.append(pltpu.make_async_copy(left_ref.at[p, 0], left.at[p], sem.at[2 * p]))
        copies.append(pltpu.make_async_copy(right_ref.at[p, 0], right.at[p], sem.at[2 * p + 1]))
    for copy in copies:
        copy.start()
    for p in range(pairs):
        copies[2 * p].wait()
        lcat_ref[p, 0], lcat_ref[p, 1] = halves(left[p])
        copies[2 * p + 1].wait()
        rcat_ref[p, 0], rcat_ref[p, 1] = halves(right[p].T)


def split_body(
    label_ref, couple_hbm, left_ref, right_ref, lcat_ref, rcat_ref, flag_ref, slot_ref,
    left, right, sem, couple_ref, mark,
):
    here = lax.axis_index("sec")
    copy = pltpu.make_async_copy(couple_hbm, couple_ref, mark)
    copy.start()
    split_pairs(left_ref, right_ref, lcat_ref, rcat_ref, left, right, sem)
    copy.wait()
    for p in range(lcat_ref.shape[0]):
        source = couple_ref[p]
        near = here + 1 - 2 * (here % 2)
        slot = jnp.where(source == here, 0.0, jnp.where(source == near, 1.0, 2.0))
        slot_ref[p] = jnp.full(slot_ref.shape[1:], jnp.where(source >= 0, slot, -1.0))
    flag_ref[...] = jnp.full(flag_ref.shape, jnp.where(label_ref[0] == here, 1.0, 0.0))


def mix_all(slot_ref, blocks, lcat_ref, m_ref):
    mixed = []
    for p in range(lcat_ref.shape[0]):
        high, low = halves(pick(slot_ref[p, 0:1, 0:1][None], blocks))
        mixed.append(three(lcat_ref[p, 0], lcat_ref[p, 1], high, low))
        m_ref[p] = mixed[p]
    return mixed


def fold_all(size_ref, mixed, rcat_ref, y_ref):
    y = fold(mixed, rcat_ref)
    pack(y_ref, (), y_ref.shape, jnp.where(mask(size_ref[0], y.shape[0]), y, 0.0))
    return y_ref[...]


def first_body(size_ref, slot_ref, x0, x1, x2, lcat_ref, rcat_ref, y_ref, m_ref, part_ref):
    mixed = mix_all(slot_ref, (x0, x1, x2), lcat_ref, m_ref)
    y = fold_all(size_ref, mixed, rcat_ref, y_ref)
    x = x0[lax.axis_index("ops")]
    part_ref[...] = tile([rows(x * x), rows(x0[...] * y)])


def five(x0, r0, h0, y):
    o = lax.axis_index("ops")
    x, r, h = x0[o], r0[o], h0[o][: x0.shape[1]]
    return tile([rows(x * r), rows(r * r), rows(r * h), rows(x0[...] * y), rows(r0[...] * y)])


def second_body(
    size_ref, slot_ref, r0, r1, r2, x0, g0, lcat_ref, rcat_ref, y_ref, m_out, part_ref,
    m_ref, sem,
):
    mixed = mix_all(slot_ref, (r0, r1, r2), lcat_ref, m_ref)
    copy = pltpu.make_async_copy(m_ref, m_out, sem)
    copy.start()
    part_ref[...] = five(x0, r0, g0, fold_all(size_ref, mixed, rcat_ref, y_ref))
    copy.wait()


def mix_body(slot_ref, r0, r1, r2, lcat_ref, m_ref):
    mix_all(slot_ref, (r0, r1, r2), lcat_ref, m_ref)


def fold_body(size_ref, m_ref, r0, x0, h0, rcat_ref, part_ref, y_ref):
    mixed = [m_ref[p] for p in range(m_ref.shape[0])]
    lanes(five(x0, r0, h0, fold_all(size_ref, mixed, rcat_ref, y_ref)), part_ref)


def blend_body(c_in, a_ref, b_ref, x_ref, out_ref):
    pairs = a_ref.shape[0]
    out_ref[:pairs] = c_in[2:3, 0:1] * a_ref[...] + c_in[3:4, 0:1] * b_ref[...]
    out_ref[pairs] = unpack(x_ref[...])


def cross_body(flag_ref, b_ref, n_ref, m_ref, w_ref, s0, s1, u_ref):
    stay = flag_ref[0:1, 0:1] > 0.5
    pairs, side, _ = m_ref.shape
    new = unpack(jnp.where(stay[None], s0[...], s1[...]))
    x = jnp.where(stay, b_ref[pairs], n_ref[pairs])
    left = jnp.concatenate([x.T, new.T], axis=0)
    lh, ll = halves(left)
    for p in range(pairs):
        old, new = jnp.where(stay, b_ref[p], n_ref[p]), jnp.where(stay, m_ref[p], w_ref[p])
        rh, rl = halves(jnp.concatenate([old, new], axis=1))
        both = three(lh, ll, rh, rl)
        u_ref[0, p] = both[:side, :side]
        u_ref[1, p] = both[:side, side:] + both[side:, :side]
        u_ref[2, p] = both[side:, side:]


def sum_body(terms_ref, mine, *refs):
    others, out_ref = refs[:-1], refs[-1]
    cw = terms_ref.shape[1]
    block = jnp.sum(terms_ref[...], axis=0)
    scalars = mine[...]
    for one in others:
        scalars = scalars + one[...]
    for o in range(out_ref.shape[0]):
        out_ref[o, :cw] = block
        out_ref[o, cw:] = scalars


def numbers(tiles, count):
    total = jnp.sum(jnp.sum(tiles, axis=0), axis=1, keepdims=True)
    return [total[i : i + 1] for i in range(count)]


def store(out_ref, values):
    out_ref[...] = tile([jnp.broadcast_to(v, (1, LANES)) for v in values])


def first_residual_body(g_ref, x_ref, diag_ref, r_ref, c_ref, d_ref):
    pack(d_ref, (), d_ref.shape, diag_ref[0].astype(F32))
    cw = x_ref.shape[1]
    squares, energy = numbers(g_ref[:, cw:], 2)
    factor = lax.rsqrt(squares + 1e-06)
    theta = energy * factor * factor
    r = factor * (g_ref[:, :cw] - theta * x_ref[...]) / (jnp.abs(d_ref[...] - theta) + 1.0)
    r_ref[...] = r
    store(c_ref, [factor, theta, squares * factor * factor])


def second_residual_body(
    s_ref, g_ref, x_ref, diag_ref, r_in, c_in, x_out, h_out, r_ref, c_ref, d_ref
):
    pack(d_ref, (), d_ref.shape, diag_ref[0].astype(F32))
    cw = x_ref.shape[1]
    xr, rr, rh, xhr, rhr = numbers(s_ref[:, cw:], 5)
    factor, first, xx = c_in[0:1, 0:1], c_in[1:2, 0:1], c_in[2:3, 0:1]
    on_x, on_r, theta, xx = update(
        xx, first, factor * xr, rr, factor * rh, factor * xhr, rhr
    )
    on_x = on_x * factor
    x = on_x * x_ref[...] + on_r * r_in[...]
    h = on_x * g_ref[:, :cw] + on_r * s_ref[:, :cw]
    x_out[...] = x
    h_out[...] = h
    r_ref[...] = (h - theta * x) / (jnp.abs(d_ref[...] - theta) + 1.0)
    store(c_ref, [theta, xx, on_x, on_r])


def last_body(scale, parts_ref, c_in, b_ref, s0, u_ref, wave_ref, turn_ref):
    pairs, side = u_ref.shape[1:3]
    total = jnp.sum(parts_ref[...], axis=0, keepdims=True)
    xr, rr, rh, xhr, rhr = [total[:, k : k + 1] for k in range(5)]
    on_x, on_s, _, _ = update(c_in[1:2, 0:1], c_in[0:1, 0:1], xr, rr, rh, xhr, rhr)
    on_x = on_x * scale
    on_s = on_s * scale
    wave_ref[0] = on_x * b_ref[pairs] + unpack(on_s * s0[...])
    root = 1.0 / side**0.5
    xx, xs, ss = on_x * on_x * root, on_x * on_s * root, on_s * on_s * root
    for p in range(pairs):
        turn_ref[p, 0] = xx * u_ref[0, p] + xs * u_ref[1, p] + ss * u_ref[2, p]


def paired(value):
    count = lax.axis_size("sec")
    return lax.ppermute(value, "sec", [(i, i ^ 1) for i in range(count)])


def other(value, stage):
    count, groups = lax.axis_size("sec"), lax.axis_size("ops")
    route = []
    for o in range(groups):
        for i in range(1, count - 1, 2):
            route += [(o * count + i, o * count + i + 1), (o * count + i + 1, o * count + i)]
        if groups % 2 == 0 and stage < 2:
            route += [(o * count + i, (o ^ 1) * count + i) for i in (0, count - 1)]
    return lax.ppermute(value, ("ops", "sec"), route)


def last_step(count):
    step = 1
    while step * 4 < count:
        step *= 4
    return step


def over_sectors(value):
    count = lax.axis_size("sec")
    step = 1
    while True:
        last = step == last_step(count)
        found = []
        for d in range(1, min(4, count // step)):
            route = [(i, i ^ (d * step)) for i in range(count)]
            found.append(lax.ppermute(value, "sec", route))
        if last:
            return value, found
        for one in found:
            value = value + one
        step *= 4


def exchange(value):
    return lax.all_to_all(value, "ops", 0, 0)


def local(sector_states, psi_guess, precond_diag, left_ops, right_ops, couple, new_sector):
    side = psi_guess.shape[1]
    pairs = left_ops.shape[0]
    couple = couple.reshape(pairs)
    chunks = lax.axis_size("ops")
    sectors = lax.axis_size("sec")
    cw = side // chunks * side // LANES
    block = jax.ShapeDtypeStruct((chunks, cw, LANES), F32)
    wide = jax.ShapeDtypeStruct((chunks, cw + 8, LANES), F32)
    small = jax.ShapeDtypeStruct((8, LANES), F32)
    inner = jax.ShapeDtypeStruct((pairs, side, side), F32)
    room = [pltpu.VMEM(inner.shape, F32), pltpu.SemaphoreType.DMA(())]
    pieces = jax.ShapeDtypeStruct((pairs, 2, side, side), BF16)
    loads = [pltpu.VMEM((pairs, side, side), F32)] * 2 + [pltpu.SemaphoreType.DMA((2 * pairs,))]
    work = 12 * pairs * side**3
    light = 20 * side**2

    def gathered(y, part):
        part, others = over_sectors(part)
        (full,) = call(
            sum_body, (wide,), [VMEM] * (2 + len(others)), [], light,
            exchange(y), part, *others,
        )
        return exchange(full)

    (x0,) = call(
        start_body, (block,), [SMEM, pl.BlockSpec(memory_space=pltpu.HBM)],
        [pltpu.VMEM((side, side), BF16), pltpu.SemaphoreType.DMA(())], light,
        sector_states, pltpu.with_memory_space_constraint(psi_guess, pltpu.HBM),
    )
    x2, x1 = other(x0, 0), paired(x0)
    lcat, rcat, flag, slots = call(
        split_body, (pieces, pieces, small, jax.ShapeDtypeStruct((pairs, 8, LANES), F32)),
        [SMEM] + [ANY] * 3,
        loads + [pltpu.SMEM((pairs,), jnp.int32), pltpu.SemaphoreType.DMA(())],
        light * pairs, new_sector, couple, left_ops, right_ops, limit=52.5,
    )
    y, mx, part = call(
        first_body, (block, inner, small), [SMEM] + [VMEM] * 6, [], work,
        sector_states, slots, x0, x1, x2, lcat, rcat,
    )
    g = gathered(y, part)
    r0, c = call(
        first_residual_body, (block, small), [VMEM] * 3, [pltpu.VMEM(block.shape, F32)], light,
        g, x0, precond_diag,
    )
    r2, r1 = other(r0, 1), paired(r0)
    y, mr, part = call(
        second_body, (block, inner, small), [SMEM] + [VMEM] * 8, room, work,
        sector_states, slots, r0, r1, r2, x0, g, lcat, rcat, away=(1,),
    )
    s = gathered(y, part)
    x, h, s0, c = call(
        second_residual_body, (block, block, block, small), [VMEM] * 6,
        [pltpu.VMEM(block.shape, F32)], light, s, g, x0, precond_diag, r0, c,
    )
    s2, s1 = other(s0, 2), paired(s0)
    (mx,) = call(
        blend_body, (jax.ShapeDtypeStruct((pairs + 1, side, side), F32),), [VMEM] * 4, [],
        light, c, mx, mr, x,
    )
    nx = paired(mx)
    (ms,) = call(
        mix_body, (inner,), [VMEM] * 5, [], work // 2,
        slots, s0, s1, s2, lcat,
    )
    ns = paired(ms)
    many = jax.ShapeDtypeStruct((chunks * sectors, LANES), F32)
    (part,) = call(
        fold_body, (many,), [SMEM] + [VMEM] * 5, [pltpu.VMEM(block.shape, F32)], work // 2,
        sector_states, ms, s0, x, h, rcat,
    )
    parts = lax.all_to_all(part, ("ops", "sec"), 0, 0)
    (u,) = call(
        cross_body, (jax.ShapeDtypeStruct((3, pairs, side, side), F32),), [VMEM] * 7,
        [], work, flag, mx, nx, ms, ns, s0, s1,
    )
    return call(
        functools.partial(last_body, float((sectors * side * side) ** 0.5)),
        (
            jax.ShapeDtypeStruct((1, side, side), F32),
            jax.ShapeDtypeStruct((pairs, 1, side, side), F32),
        ),
        [VMEM] * 5, [], light, parts, c, mx, s0, u,
    )


def solution(mesh):
    in_specs = (
        P("sec"),
        P("sec", None, None),
        P("sec", None, None),
        P("ops", "sec", None, None),
        P("ops", "sec", None, None),
        P("ops", "sec"),
        P("sec"),
    )
    out_specs = (P("sec", None, None), P("ops", "sec", None, None))
    return jax.shard_map(local, mesh=mesh, in_specs=in_specs, out_specs=out_specs, check_vma=False)
```

```python
import functools

import jax
import jax.numpy as jnp
from jax import lax
from jax.experimental import pallas as pl
from jax.experimental.pallas import tpu as pltpu
from jax.sharding import PartitionSpec as P


LANES = 128
F32 = jnp.float32
BF16 = jnp.bfloat16
VMEM = pl.BlockSpec(memory_space=pltpu.VMEM)
ANY = pl.BlockSpec(memory_space=pl.ANY)
SMEM = pl.BlockSpec(memory_space=pltpu.SMEM)


def call(body, outs, in_specs, scratch, flops, *args, limit=8, away=()):
    size = sum(a.size * a.dtype.itemsize for a in args)
    size += sum(o.size * o.dtype.itemsize for o in outs)
    return pl.pallas_call(
        body,
        out_shape=tuple(pltpu.HBM(o.shape, o.dtype) if k in away else o for k, o in enumerate(outs)),
        in_specs=in_specs,
        out_specs=tuple(pl.BlockSpec(memory_space=pltpu.HBM) if k in away else VMEM for k in range(len(outs))),
        scratch_shapes=scratch,
        compiler_params=pltpu.CompilerParams(vmem_limit_bytes=int(limit * 1024 * 1024)),
        cost_estimate=pl.CostEstimate(flops=flops, bytes_accessed=size, transcendentals=0),
    )(*args)


def pack(ref, lead, block, value):
    rc = value.shape[0] // block[0]
    for o in range(block[0]):
        for j in range(value.shape[1] // LANES):
            ref[lead + (o, slice(j * rc, (j + 1) * rc))] = value[
                o * rc : (o + 1) * rc, j * LANES : (j + 1) * LANES
            ]


def unpack(value):
    chunks, cw, _ = value.shape
    groups = int((cw * chunks // LANES) ** 0.5)
    rc = cw // groups
    return jnp.concatenate(
        [
            jnp.concatenate([value[o, j * rc : (j + 1) * rc] for j in range(groups)], axis=1)
            for o in range(chunks)
        ],
        axis=0,
    )


def halves(value):
    high = value.astype(BF16)
    low = (value - high.astype(F32)).astype(BF16)
    return high, low


def dot(a, b):
    return jnp.dot(a, b, preferred_element_type=F32)


def three(ah, al, bh, bl):
    return dot(
        jnp.concatenate([ah, ah, al], axis=1), jnp.concatenate([bh, bl, bh], axis=0)
    )


def mask(size, side):
    rows = lax.broadcasted_iota(jnp.int32, (side, side), 0)
    cols = lax.broadcasted_iota(jnp.int32, (side, side), 1)
    return (rows < size) & (cols < size)


def pick(slot, blocks):
    value = jnp.zeros(blocks[0].shape, F32)
    for k, block in enumerate(blocks):
        value = jnp.where(slot == float(k), block[...], value)
    return unpack(value)


def fold(mixed, rcat_ref):
    total = None
    for p, one in enumerate(mixed):
        high, low = halves(one)
        term = three(high, low, rcat_ref[p, 0], rcat_ref[p, 1])
        total = term if total is None else total + term
    return total


def rows(value):
    return jnp.sum(value.reshape(-1, LANES), axis=0, keepdims=True)


def tile(parts):
    parts = parts + [jnp.zeros((8 - len(parts), LANES), F32)]
    return jnp.concatenate(parts, axis=0)


def lanes(value, out_ref):
    place = lax.broadcasted_iota(jnp.int32, (1, LANES), 1)
    sums = jnp.sum(value, axis=1, keepdims=True)
    row = jnp.zeros((1, LANES), F32)
    for k in range(value.shape[0]):
        row = jnp.where(place == k, sums[k : k + 1], row)
    out_ref[...] = jnp.broadcast_to(row, out_ref.shape)


def half_angle(middle, first, last):
    gap = last - first
    tilt = -2.0 * middle
    length = jnp.sqrt(gap * gap + tilt * tilt)
    safe = jnp.where(length > 0.0, length, 1.0)
    big = jnp.where(length > 0.0, jnp.sqrt(0.5 + 0.5 * jnp.abs(gap) / safe), 1.0)
    small = 0.5 * tilt / (safe * big)
    sign = jnp.where(tilt > 0.0, 1.0, -1.0)
    cosine = jnp.where(gap >= 0.0, big, jnp.abs(small))
    sine = jnp.where(gap >= 0.0, small, sign * big)
    return cosine, sine, 0.5 * (first + last) - 0.5 * length


def update(xx, first, xr, rr, rh, xhr, rhr):
    n = lax.rsqrt(rr - 2.0 * xr * xr + xr * xr * xx + 1e-06)
    middle = 0.5 * n * ((xhr - xr * first) + (rh - xr * first))
    last = n * n * (rhr - xr * rh - xr * xhr + xr * xr * first)
    cosine, sine, theta = half_angle(middle, first, last)
    on_r = sine * n
    on_x = cosine - on_r * xr
    xx = on_x * on_x * xx + 2.0 * on_x * on_r * xr + on_r * on_r * rr
    return on_x, on_r, theta, xx


def start_body(size_ref, psi_ref, x_ref):
    live = mask(size_ref[0], psi_ref.shape[1])
    pack(x_ref, (), x_ref.shape, jnp.where(live, psi_ref[0].astype(F32), 0.0))


def split_pairs(left_ref, right_ref, lcat_ref, rcat_ref, left, right, sem):
    pairs = lcat_ref.shape[0]
    copies = []
    for p in range(pairs):
        copies.append(pltpu.make_async_copy(left_ref.at[p, 0], left.at[p], sem.at[2 * p]))
        copies.append(pltpu.make_async_copy(right_ref.at[p, 0], right.at[p], sem.at[2 * p + 1]))
    for copy in copies:
        copy.start()
    for p in range(pairs):
        copies[2 * p].wait()
        lcat_ref[p, 0], lcat_ref[p, 1] = halves(left[p])
        copies[2 * p + 1].wait()
        rcat_ref[p, 0], rcat_ref[p, 1] = halves(right[p].T)


def split_body(
    label_ref, couple_hbm, left_ref, right_ref, lcat_ref, rcat_ref, flag_ref, slot_ref,
    left, right, sem, couple_ref, mark,
):
    here = lax.axis_index("sec")
    copy = pltpu.make_async_copy(couple_hbm, couple_ref, mark)
    copy.start()
    split_pairs(left_ref, right_ref, lcat_ref, rcat_ref, left, right, sem)
    copy.wait()
    for p in range(lcat_ref.shape[0]):
        source = couple_ref[p]
        near = here + 1 - 2 * (here % 2)
        slot = jnp.where(source == here, 0.0, jnp.where(source == near, 1.0, 2.0))
        slot_ref[p] = jnp.full(slot_ref.shape[1:], jnp.where(source >= 0, slot, -1.0))
    flag_ref[...] = jnp.full(flag_ref.shape, jnp.where(label_ref[0] == here, 1.0, 0.0))


def mix_all(slot_ref, blocks, lcat_ref, m_ref):
    mixed = []
    for p in range(lcat_ref.shape[0]):
        high, low = halves(pick(slot_ref[p, 0:1, 0:1][None], blocks))
        mixed.append(three(lcat_ref[p, 0], lcat_ref[p, 1], high, low))
        m_ref[p] = mixed[p]
    return mixed


def fold_all(size_ref, mixed, rcat_ref, y_ref):
    y = fold(mixed, rcat_ref)
    pack(y_ref, (), y_ref.shape, jnp.where(mask(size_ref[0], y.shape[0]), y, 0.0))
    return y_ref[...]


def first_body(
    size_ref, slot_ref, x0, x1, x2, lcat_ref, rcat_ref, y_ref, m_out, part_ref, m_ref, sem
):
    mixed = mix_all(slot_ref, (x0, x1, x2), lcat_ref, m_ref)
    copy = pltpu.make_async_copy(m_ref, m_out, sem)
    copy.start()
    y = fold_all(size_ref, mixed, rcat_ref, y_ref)
    x = x0[lax.axis_index("ops")]
    part_ref[...] = tile([rows(x * x), rows(x0[...] * y)])
    copy.wait()


def five(x0, r0, h0, y):
    o = lax.axis_index("ops")
    x, r, h = x0[o], r0[o], h0[o][: x0.shape[1]]
    return tile([rows(x * r), rows(r * r), rows(r * h), rows(x0[...] * y), rows(r0[...] * y)])


def second_body(
    size_ref, slot_ref, r0, r1, r2, x0, g0, lcat_ref, rcat_ref, y_ref, m_out, part_ref,
    m_ref, sem,
):
    mixed = mix_all(slot_ref, (r0, r1, r2), lcat_ref, m_ref)
    copy = pltpu.make_async_copy(m_ref, m_out, sem)
    copy.start()
    part_ref[...] = five(x0, r0, g0, fold_all(size_ref, mixed, rcat_ref, y_ref))
    copy.wait()


def mix_body(slot_ref, r0, r1, r2, lcat_ref, m_ref):
    mix_all(slot_ref, (r0, r1, r2), lcat_ref, m_ref)


def probe_body(x_ref, s_ref, rcat_ref, probe_ref):
    high, low = halves(jnp.concatenate([unpack(x_ref[...]), unpack(s_ref[...])], axis=0))
    side = rcat_ref.shape[2]
    for p in range(rcat_ref.shape[0]):
        both = lax.dot_general(
            jnp.concatenate([high, high, low], axis=1),
            jnp.concatenate([rcat_ref[p, 0], rcat_ref[p, 1], rcat_ref[p, 0]], axis=1),
            (((1,), (1,)), ((), ())),
            preferred_element_type=F32,
        )
        probe_ref[0, p] = both[:side]
        probe_ref[1, p] = both[side:]


def spread(value):
    total = jnp.sum(value, axis=0, keepdims=True)
    return sum(total[:, j : j + LANES] for j in range(0, total.shape[1], LANES))


def meet_body(m_ref, probe_ref, s0, x0, h0, part_ref):
    o = lax.axis_index("ops")
    x, r, h = x0[o], s0[o], h0[o]
    on_x, on_s = [
        sum(probe_ref[k, p] * m_ref[p] for p in range(m_ref.shape[0])) for k in range(2)
    ]
    lanes(tile([rows(x * r), rows(r * r), rows(r * h), spread(on_x), spread(on_s)]), part_ref)


def blend_body(c_in, a_ref, b_ref, x_ref, out_ref):
    pairs = a_ref.shape[0]
    out_ref[:pairs] = c_in[2:3, 0:1] * a_ref[...] + c_in[3:4, 0:1] * b_ref[...]
    out_ref[pairs] = unpack(x_ref[...])


def cross_body(flag_ref, b_ref, n_ref, m_ref, w_ref, s0, s1, u_ref):
    stay = flag_ref[0:1, 0:1] > 0.5
    pairs, side, _ = m_ref.shape
    new = unpack(jnp.where(stay[None], s0[...], s1[...]))
    x = jnp.where(stay, b_ref[pairs], n_ref[pairs])
    left = jnp.concatenate([x.T, new.T], axis=0)
    lh, ll = halves(left)
    for p in range(pairs):
        old, new = jnp.where(stay, b_ref[p], n_ref[p]), jnp.where(stay, m_ref[p], w_ref[p])
        rh, rl = halves(jnp.concatenate([old, new], axis=1))
        both = three(lh, ll, rh, rl)
        u_ref[0, p] = both[:side, :side]
        u_ref[1, p] = both[:side, side:] + both[side:, :side]
        u_ref[2, p] = both[side:, side:]


def sum_body(terms_ref, mine, *refs):
    others, out_ref = refs[:-1], refs[-1]
    cw = terms_ref.shape[1]
    block = jnp.sum(terms_ref[...], axis=0)
    scalars = mine[...]
    for one in others:
        scalars = scalars + one[...]
    for o in range(out_ref.shape[0]):
        out_ref[o, :cw] = block
        out_ref[o, cw:] = scalars


def numbers(tiles, count):
    total = jnp.sum(jnp.sum(tiles, axis=0), axis=1, keepdims=True)
    return [total[i : i + 1] for i in range(count)]


def store(out_ref, values):
    out_ref[...] = tile([jnp.broadcast_to(v, (1, LANES)) for v in values])


def first_residual_body(g_ref, x_ref, diag_ref, r_ref, c_ref, d_ref):
    pack(d_ref, (), d_ref.shape, diag_ref[0].astype(F32))
    cw = x_ref.shape[1]
    squares, energy = numbers(g_ref[:, cw:], 2)
    factor = lax.rsqrt(squares + 1e-06)
    theta = energy * factor * factor
    r = factor * (g_ref[:, :cw] - theta * x_ref[...]) / (jnp.abs(d_ref[...] - theta) + 1.0)
    r_ref[...] = r
    store(c_ref, [factor, theta, squares * factor * factor])


def second_residual_body(
    s_ref, g_ref, x_ref, diag_ref, r_in, c_in, x_out, h_out, r_ref, c_ref, d_ref
):
    pack(d_ref, (), d_ref.shape, diag_ref[0].astype(F32))
    cw = x_ref.shape[1]
    xr, rr, rh, xhr, rhr = numbers(s_ref[:, cw:], 5)
    factor, first, xx = c_in[0:1, 0:1], c_in[1:2, 0:1], c_in[2:3, 0:1]
    on_x, on_r, theta, xx = update(
        xx, first, factor * xr, rr, factor * rh, factor * xhr, rhr
    )
    on_x = on_x * factor
    x = on_x * x_ref[...] + on_r * r_in[...]
    h = on_x * g_ref[:, :cw] + on_r * s_ref[:, :cw]
    x_out[...] = x
    h_out[...] = h
    r_ref[...] = (h - theta * x) / (jnp.abs(d_ref[...] - theta) + 1.0)
    store(c_ref, [theta, xx, on_x, on_r])


def last_body(scale, parts_ref, c_in, b_ref, s0, u_ref, wave_ref, turn_ref):
    pairs, side = u_ref.shape[1:3]
    total = jnp.sum(parts_ref[...], axis=0, keepdims=True)
    xr, rr, rh, xhr, rhr = [total[:, k : k + 1] for k in range(5)]
    on_x, on_s, _, _ = update(c_in[1:2, 0:1], c_in[0:1, 0:1], xr, rr, rh, xhr, rhr)
    on_x = on_x * scale
    on_s = on_s * scale
    wave_ref[0] = on_x * b_ref[pairs] + unpack(on_s * s0[...])
    root = 1.0 / side**0.5
    xx, xs, ss = on_x * on_x * root, on_x * on_s * root, on_s * on_s * root
    for p in range(pairs):
        turn_ref[p, 0] = xx * u_ref[0, p] + xs * u_ref[1, p] + ss * u_ref[2, p]


def paired(value):
    count = lax.axis_size("sec")
    return lax.ppermute(value, "sec", [(i, i ^ 1) for i in range(count)])


def other(value, stage):
    count, groups = lax.axis_size("sec"), lax.axis_size("ops")
    route = []
    for o in range(groups):
        for i in range(1, count - 1, 2):
            route += [(o * count + i, o * count + i + 1), (o * count + i + 1, o * count + i)]
        if groups % 2 == 0 and stage < 2:
            route += [(o * count + i, (o ^ 1) * count + i) for i in (0, count - 1)]
    return lax.ppermute(value, ("ops", "sec"), route)


def last_step(count):
    step = 1
    while step * 4 < count:
        step *= 4
    return step


def over_sectors(value):
    count = lax.axis_size("sec")
    step = 1
    while True:
        last = step == last_step(count)
        found = []
        for d in range(1, min(4, count // step)):
            route = [(i, i ^ (d * step)) for i in range(count)]
            found.append(lax.ppermute(value, "sec", route))
        if last:
            return value, found
        for one in found:
            value = value + one
        step *= 4


def exchange(value):
    return lax.all_to_all(value, "ops", 0, 0)


def local(sector_states, psi_guess, precond_diag, left_ops, right_ops, couple, new_sector):
    side = psi_guess.shape[1]
    pairs = left_ops.shape[0]
    couple = couple.reshape(pairs)
    chunks = lax.axis_size("ops")
    sectors = lax.axis_size("sec")
    cw = side // chunks * side // LANES
    block = jax.ShapeDtypeStruct((chunks, cw, LANES), F32)
    wide = jax.ShapeDtypeStruct((chunks, cw + 8, LANES), F32)
    small = jax.ShapeDtypeStruct((8, LANES), F32)
    inner = jax.ShapeDtypeStruct((pairs, side, side), F32)
    room = [pltpu.VMEM(inner.shape, F32), pltpu.SemaphoreType.DMA(())]
    pieces = jax.ShapeDtypeStruct((pairs, 2, side, side), BF16)
    loads = [pltpu.VMEM((pairs, side, side), F32)] * 2 + [pltpu.SemaphoreType.DMA((2 * pairs,))]
    work = 12 * pairs * side**3
    light = 20 * side**2

    def gathered(y, part):
        part, others = over_sectors(part)
        (full,) = call(
            sum_body, (wide,), [VMEM] * (2 + len(others)), [], light,
            exchange(y), part, *others,
        )
        return exchange(full)

    (x0,) = call(start_body, (block,), [SMEM, VMEM], [], light, sector_states, psi_guess)
    x2, x1 = other(x0, 0), paired(x0)
    lcat, rcat, flag, slots = call(
        split_body, (pieces, pieces, small, jax.ShapeDtypeStruct((pairs, 8, LANES), F32)),
        [SMEM] + [ANY] * 3,
        loads + [pltpu.SMEM((pairs,), jnp.int32), pltpu.SemaphoreType.DMA(())],
        light * pairs, new_sector, couple, left_ops, right_ops, limit=52.5,
    )
    y, mx, part = call(
        first_body, (block, inner, small), [SMEM] + [VMEM] * 6, room, work,
        sector_states, slots, x0, x1, x2, lcat, rcat, away=(1,),
    )
    g = gathered(y, part)
    r0, c = call(
        first_residual_body, (block, small), [VMEM] * 3, [pltpu.VMEM(block.shape, F32)], light,
        g, x0, precond_diag,
    )
    r2, r1 = other(r0, 1), paired(r0)
    y, mr, part = call(
        second_body, (block, inner, small), [SMEM] + [VMEM] * 8, room, work,
        sector_states, slots, r0, r1, r2, x0, g, lcat, rcat, away=(1,),
    )
    s = gathered(y, part)
    x, h, s0, c = call(
        second_residual_body, (block, block, block, small), [VMEM] * 6,
        [pltpu.VMEM(block.shape, F32)], light, s, g, x0, precond_diag, r0, c,
    )
    s2, s1 = other(s0, 2), paired(s0)
    (mx,) = call(
        blend_body, (jax.ShapeDtypeStruct((pairs + 1, side, side), F32),), [VMEM] * 4, [],
        light, c, mx, mr, x,
    )
    nx = paired(mx)
    (probe,) = call(
        probe_body, (jax.ShapeDtypeStruct((2, pairs, side, side), F32),), [VMEM] * 3, [],
        work, x, s0, rcat,
    )
    (ms,) = call(
        mix_body, (inner,), [VMEM] * 5, [], work // 2,
        slots, s0, s1, s2, lcat,
    )
    ns = paired(ms)
    many = jax.ShapeDtypeStruct((chunks * sectors, LANES), F32)
    (part,) = call(
        meet_body, (many,), [VMEM] * 5, [], light * pairs, ms, probe, s0, x, h
    )
    parts = lax.all_to_all(part, ("ops", "sec"), 0, 0)
    (u,) = call(
        cross_body, (jax.ShapeDtypeStruct((3, pairs, side, side), F32),), [VMEM] * 7,
        [], work, flag, mx, nx, ms, ns, s0, s1,
    )
    return call(
        functools.partial(last_body, float((sectors * side * side) ** 0.5)),
        (
            jax.ShapeDtypeStruct((1, side, side), F32),
            jax.ShapeDtypeStruct((pairs, 1, side, side), F32),
        ),
        [VMEM] * 5, [], light, parts, c, mx, s0, u,
    )


def solution(mesh):
    in_specs = (
        P("sec"),
        P("sec", None, None),
        P("sec", None, None),
        P("ops", "sec", None, None),
        P("ops", "sec", None, None),
        P("ops", "sec"),
        P("sec"),
    )
    out_specs = (P("sec", None, None), P("ops", "sec", None, None))
    return jax.shard_map(local, mesh=mesh, in_specs=in_specs, out_specs=out_specs, check_vma=False)
```
